32 devices in a mesh: dp: 8 (over z, y), expert: 4 (over x, core).
Axes of the slice: x: 2, y: 2, z: 4, core: 2. Of those that a mesh axis runs over, the one named last changes fastest.
Arguments:
- tokens: bfloat16 [4, 1024, 1536], P('expert', 'dp'), may hold values from -6 to 6
- cotangent: bfloat16 [4, 1024, 1536], P('expert', 'dp'), may hold values from -6 to 6
- lengths: int32 [4, 2], P('expert'), may hold values from 341 to 683, as said below
- deal: int32 [4], replicated, may hold values from 0 to 3, each once
- routes: int32 [4, 1024, 8], P('expert', 'dp'), may hold values from 0 to 39, all different within a row; in each aligned block of 128 rows (0 to 127, 128 to 255, ..., all dimensions but the last counted through in order) at most 40 rows name the same one
- gates: float32 [4, 1024, 8], P('expert', 'dp'), may hold values from 0.15 to 0.5
- q_weight: float32 [1536, 1536], P(('dp', 'expert')), may hold values from -0.625 to 0.625
- k_weight: float32 [1536, 512], P(('dp', 'expert')), may hold values from -0.625 to 0.625
- v_weight: float32 [1536, 512], P(('dp', 'expert')), may hold values from -0.15625 to 0.15625
- o_weight: float32 [1536, 1536], P(('dp', 'expert')), may hold values from -1.5 to 1.5
- gain_attn: float32 [1536], P(('dp', 'expert')), may hold values from 0.5 to 1.5
- gain_moe: float32 [1536], P(('dp', 'expert')), may hold values from 0.5 to 1.5
- in_weight: float32 [1536, 40, 1024], P('dp', 'expert'), may hold values from -0.15625 to 0.15625
- down_weight: float32 [512, 40, 1536], P('dp', 'expert'), may hold values from -1 to 1
Outputs:
- output: float32 [4, 1024, 1536], P('expert', 'dp')
- input_grad: float32 [4, 1024, 1536], P('expert', 'dp')
- q_weight_grad: float32 [1536, 1536], P(('dp', 'expert'))
- k_weight_grad: float32 [1536, 512], P(('dp', 'expert'))
- v_weight_grad: float32 [1536, 512], P(('dp', 'expert'))
- o_weight_grad: float32 [1536, 1536], P(('dp', 'expert'))
- gain_attn_grad: float32 [1536], P(('dp', 'expert'))
- gain_moe_grad: float32 [1536], P(('dp', 'expert'))
- in_weight_grad: float32 [1536, 40, 1024], P('dp', 'expert')
- down_weight_grad: float32 [512, 40, 1536], P('dp', 'expert')
The draws below stay inside these ranges and needn't reach their ends.
Inputs may be any that keep to these rules, and one draw needn't show every extreme that they name: In each group the lengths of sequences 2i and 2i + 1 sum to 1024; in some group a sequence has the largest length. `routes`: each token names 8 different experts; in the rows of one device no expert is named by more than 40 rows.
All inputs are finite; a program needn't handle non-finite values.
Results may differ from the reference program's by a relative error of at most 0.018.
The reference program's roundings to bfloat16 on the way count: a program that leaves them out, or rounds other values in their place, can miss the bound.
Values may be sent and summed in bfloat16 or wider, within the bound.
No kernel may reach another device: no remote copies, remote signals or barrier semaphores. Data moves between devices by JAX's collectives and lax.ppermute only.
A program may use at most 256 MiB of HBM per device.

```python
import math
import jax
import jax.numpy as jnp
import numpy as np
from jax import lax

D = 1536
H = 24
KVH = 8
HD = 64
E = 40
FF = 512
TOPK = 8
TOK_DEV = 128
SEQ_GROUPS = 4
GROUP_TOK = 1024
NSEQ = 2
PAIR = 1024
LOWLEN = 341
QB = 512
CAP = 40
N_DP = 8


def draw_lengths(key, part):
    pair_count = NSEQ // 2
    firsts = jax.random.randint(key, (SEQ_GROUPS, pair_count), LOWLEN, PAIR - LOWLEN + 1, dtype=jnp.int32)
    firsts = firsts.at[0, 0].set(PAIR - LOWLEN)
    seconds = PAIR - firsts
    return jnp.stack([firsts, seconds], axis=2).reshape(SEQ_GROUPS, NSEQ).astype(jnp.int32)


def levels(own_key, extent, cuts, smallest, top_value):
    factor_of, own = 1.0, jax.random.fold_in(own_key, 6)
    for dim, blocks in cuts:
        draws = jnp.exp(jax.random.uniform(jax.random.fold_in(own, dim), (blocks,), jnp.float32, smallest / len(cuts), top_value / len(cuts)))
        factor_of = factor_of * jnp.repeat(draws, extent[dim] // blocks).reshape([-1 if axis == dim else 1 for axis in range(len(extent))])
    return factor_of


def shared_out(own_key, own, number, rows, number_of, top, bound, lean):
    sequence = jax.random.permutation(own_key, number_of)
    heavy_load, usual = load_shares(number_of, rows * top, bound, lean, True), load_shares(number_of, rows * top, bound, lean, False)
    places = jnp.arange(number_of)

    def named(tallies, turn):
        used = int((tallies > 0).sum())
        fixed = max(1, used // 4)
        moved = fixed + (places - fixed + turn * (used - fixed)) % max(1, number_of - fixed)
        return jnp.zeros((number_of,), jnp.int32).at[sequence[jnp.where(places < fixed, places, moved)]].set(jnp.asarray(tallies, jnp.int32))

    tallies = jnp.where(number % 4 == 0, named(heavy_load, number // 4), named(usual, number - number // 4 - 1))
    mixed = jax.random.permutation(jax.random.fold_in(own, 3), number_of)
    giver, sink = mixed[0:number_of // 2 * 2:2], mixed[1:number_of // 2 * 2:2]
    slack = jnp.minimum(tallies[giver] - 1, bound - tallies[sink]) // 2
    slack = jnp.where((giver == sequence[0]) | (sink == sequence[0]) | (tallies[sink] == 0), 0, jnp.maximum(slack, 0))
    moved = jax.random.randint(jax.random.fold_in(own, 4), (number_of // 2,), 0, 1 << 20) % (slack + 1)
    tallies = tallies.at[giver].add(-moved).at[sink].add(moved)
    items = jnp.searchsorted(jnp.cumsum(tallies), jnp.arange(rows * top), side="right").astype(jnp.int32)
    listing = items.reshape(top, rows).T
    listing = listing[jax.random.permutation(jax.random.fold_in(own, 1), rows)]
    turn = jax.random.randint(jax.random.fold_in(own, 2), (rows, 1), 0, top)
    return jnp.take_along_axis(listing, (jnp.arange(top)[None, :] + turn) % top, axis=1)


def load_shares(number_of, total, limit, slope, full):
    weights = [(1 << 20) // math.isqrt(standing ** slope) + 1 for standing in range(1, number_of + 1)]
    largest = limit if full else min(limit, max(-(-total // number_of), total * weights[0] // sum(weights)))
    least = 1 if total - largest >= number_of - 1 else 0
    given, surplus = [largest] + [least] * (number_of - 1), total - largest - least * (number_of - 1)
    while surplus > 0:
        free = [i for i in range(1, number_of) if given[i] < largest] or [i for i in range(1, number_of) if given[i] < limit]
        whole, remaining = sum([weights[i] for i in free]), surplus
        for i in free:
            more = min(limit - given[i], max(1, remaining * weights[i] // whole), surplus)
            given[i] = given[i] + more
            surplus = surplus - more
    return np.array(given)


def normal_values(own_key, extent, width, reach, pieces=(), held_as=jnp.bfloat16):
    entries = jax.random.normal(own_key, extent, jnp.float32) * width
    if len(pieces) > 0:
        entries = levels(own_key, extent, pieces, -0.22, 0.18) * entries
    return jnp.clip(entries, min=-reach, max=reach).astype(held_as)


def setup_inputs(seed: int = 0) -> dict:
    key_list = jax.random.split(jax.random.key(seed), 15)
    tokens = normal_values(key_list[0], (SEQ_GROUPS, GROUP_TOK, D), 1.0, 6.0, ((0, 4), (1, 8)))
    cotangent = normal_values(key_list[1], (SEQ_GROUPS, GROUP_TOK, D), 1.0, 6.0, ((0, 4), (1, 8)))
    lengths = draw_lengths(jax.random.fold_in(key_list[14], 71), 0)
    deal = jax.random.permutation(key_list[3], SEQ_GROUPS).astype(jnp.int32)
    routes_keys = jax.random.split(jax.random.fold_in(key_list[4], 1), SEQ_GROUPS * GROUP_TOK // TOK_DEV)
    routes_turns = jax.random.permutation(jax.random.fold_in(key_list[4], 3), SEQ_GROUPS * GROUP_TOK // TOK_DEV)
    routes = jax.vmap(lambda own, number: shared_out(jax.random.fold_in(key_list[4], 2), own, number, TOK_DEV, E, TOPK, CAP, 1))(routes_keys, routes_turns).reshape((SEQ_GROUPS, GROUP_TOK, TOPK))
    gates = jnp.clip(0.15 + 0.35 * jax.random.uniform(key_list[5], (SEQ_GROUPS, GROUP_TOK, TOPK), jnp.float32) ** levels(key_list[5], (SEQ_GROUPS, GROUP_TOK, TOPK), ((0, 4), (1, 8)), -0.2, 0.2), 0.15, 0.5)
    q_weight = normal_values(key_list[6], (D, H * HD), (D // 16) ** -0.5, 0.625, ((0, 32),), jnp.float32)
    k_weight = normal_values(key_list[7], (D, KVH * HD), (D // 16) ** -0.5, 0.625, ((0, 32),), jnp.float32)
    v_weight = normal_values(key_list[8], (D, KVH * HD), D ** -0.5, 0.15625, ((0, 32),), jnp.float32)
    o_weight = normal_values(key_list[9], (D, H * HD), 16 ** -0.5, 1.5, ((0, 32),), jnp.float32)
    gain_attn = jnp.clip(1.0 + 0.1 * jax.random.normal(key_list[10], (D,), jnp.float32), 0.5, 1.5)
    gain_moe = jnp.clip(1.0 + 0.1 * jax.random.normal(key_list[11], (D,), jnp.float32), 0.5, 1.5)
    in_weight = normal_values(key_list[12], (D, E, 2 * FF), D ** -0.5, 0.15625, ((0, 8), (1, 4)), jnp.float32)
    down_weight = normal_values(key_list[13], (FF, E, D), (FF // 16) ** -0.5, 1.0, ((0, 8), (1, 4)), jnp.float32)
    return dict(tokens=tokens, cotangent=cotangent, lengths=lengths, deal=deal, routes=routes, gates=gates, q_weight=q_weight, k_weight=k_weight, v_weight=v_weight, o_weight=o_weight, gain_attn=gain_attn, gain_moe=gain_moe, in_weight=in_weight, down_weight=down_weight)


EPSILON = 1e-06
RESIDUAL = 0.22
SCORE_SCALE = 0.015625
THETA = 10000.0
NEGATIVE = -1e+30
PRECISION = lax.Precision.HIGHEST

@jax.custom_vjp
def low(v):
    return lax.optimization_barrier(v.astype(jnp.bfloat16)).astype(jnp.float32)

@jax.custom_vjp
def low_back(v):
    return v

def low_keep(v):
    return (low(v), None)

def low_pass(kept, grad):
    return (grad,)

def back_keep(v):
    return (v, None)

def back_low(kept, grad):
    return (low(grad),)
low.defvjp(low_keep, low_pass)
low_back.defvjp(back_keep, back_low)

def rms_scale(values, gain):
    return values * lax.rsqrt(lax.optimization_barrier(jnp.mean(values * values, axis=-1, keepdims=True)) + EPSILON) * gain

def rotate(values, cosine, sine_table):
    half_width = values.shape[-1] // 2
    turned = jnp.concatenate([-values[..., half_width:], values[..., :half_width]], axis=-1)
    return values * cosine + turned * sine_table

def rope_tables(lengths):
    places = jnp.arange(GROUP_TOK, dtype=jnp.int32)
    seq_ends = jnp.cumsum(lengths, axis=1).astype(jnp.int32)
    seq_starts = (seq_ends - lengths).astype(jnp.int32)
    member = (places[None, :, None] >= seq_starts[:, None, :]) & (places[None, :, None] < seq_ends[:, None, :])
    seq_ids = lax.optimization_barrier(jnp.sum((places[None, :, None] >= seq_ends[:, None, :]).astype(jnp.int32), axis=-1)).astype(jnp.int32)
    offsets = lax.optimization_barrier(jnp.sum(jnp.where(member, places[None, :, None] - seq_starts[:, None, :], 0), axis=-1))
    frequency = THETA ** (-jnp.arange(HD // 2, dtype=jnp.float32) * 2.0 / HD)
    angles = offsets.astype(jnp.float32)[..., None] * frequency
    angles = jnp.concatenate([angles, angles], axis=-1)[:, :, None, :]
    return (seq_ids, jnp.cos(angles), jnp.sin(angles))

def attend_group(group_in):
    query_rows, key_rows, value_rows, seq_ids = group_in
    places = jnp.arange(GROUP_TOK, dtype=jnp.int32)

    def score_block(block_in):
        query_block, begin_at = block_in
        query_places = begin_at + jnp.arange(QB, dtype=jnp.int32)
        query_seq = lax.dynamic_slice_in_dim(seq_ids, begin_at, QB, 0)
        scores = SCORE_SCALE * jnp.einsum('tkgd,skd->kgts', query_block, key_rows, precision=PRECISION)
        scores = low_back(scores)
        allowed = (query_seq[:, None] == seq_ids[None, :]) & (places[None, :] <= query_places[:, None])
        scores = jnp.where(allowed, scores, NEGATIVE)
        attn_probs = jax.nn.softmax(scores, axis=-1)
        return jnp.einsum('kgts,skd->tkgd', low(attn_probs), value_rows, precision=PRECISION)
    query_blocks = query_rows.reshape(GROUP_TOK // QB, QB, KVH, H // KVH, HD)
    begins = (jnp.arange(GROUP_TOK // QB, dtype=jnp.int32) * QB).astype(jnp.int32)
    mixed_blocks = lax.map(jax.checkpoint(score_block), (query_blocks, begins))
    return mixed_blocks.reshape(GROUP_TOK, KVH, H // KVH, HD)

def reference(tokens, cotangent, lengths, deal, routes, gates, q_weight, k_weight, v_weight, o_weight, gain_attn, gain_moe, in_weight, down_weight):
    seq_ids, cosine, sine_table = rope_tables(lengths)
    deal_index = deal.astype(jnp.int32)
    dealt_tokens = tokens[deal_index].astype(jnp.float32)
    dealt_cotangent = cotangent[deal_index].astype(jnp.float32)
    blocks = SEQ_GROUPS * N_DP
    flat_routes = routes.reshape(blocks, TOK_DEV * TOPK).astype(jnp.int32)
    matches = (flat_routes[..., None] == jnp.arange(E, dtype=jnp.int32)).astype(jnp.int32)
    running = jnp.cumsum(matches, axis=1)
    slot_rank = lax.optimization_barrier(jnp.sum(matches * running, axis=-1)) - 1
    slot_index = (flat_routes * CAP + slot_rank).astype(jnp.int32)
    flat_gates = gates.reshape(blocks, TOK_DEV * TOPK).astype(jnp.float32)

    def layer_forward(inputs, q_master, k_master, v_master, o_master, gain_one, gain_two, in_master, down_master):
        q_low = low(q_master)
        k_low = low(k_master)
        v_low = low(v_master)
        o_low = low(o_master)
        in_table = jnp.transpose(low(in_master), (1, 0, 2))
        down_table = jnp.transpose(low(down_master), (1, 0, 2))
        first_norm = low(rms_scale(inputs, low(gain_one)))
        query_rows = low_back(jnp.einsum('gtd,de->gte', first_norm, q_low, precision=PRECISION))
        query_rows = low(rotate(query_rows.reshape(SEQ_GROUPS, GROUP_TOK, H, HD), cosine, sine_table))
        query_rows = query_rows.reshape(SEQ_GROUPS, GROUP_TOK, KVH, H // KVH, HD)
        key_rows = low_back(jnp.einsum('gtd,de->gte', first_norm, k_low, precision=PRECISION))
        key_rows = low(rotate(key_rows.reshape(SEQ_GROUPS, GROUP_TOK, KVH, HD), cosine, sine_table))
        value_rows = low(low_back(jnp.einsum('gtd,de->gte', first_norm, v_low, precision=PRECISION)))
        value_rows = value_rows.reshape(SEQ_GROUPS, GROUP_TOK, KVH, HD)
        mixed_rows = lax.map(attend_group, (query_rows, key_rows, value_rows, seq_ids))
        mixed_rows = low(low_back(mixed_rows.reshape(SEQ_GROUPS, GROUP_TOK, H * HD)))
        branch = low_back(jnp.einsum('gte,de->gtd', mixed_rows, o_low, precision=PRECISION))
        middle = inputs + RESIDUAL * branch
        sent_rows = low(rms_scale(middle, low(gain_two)))

        def expert_block(block_in):
            block_rows, block_slots, block_gates = block_in
            copies = low_back(jnp.repeat(block_rows, TOPK, axis=0))
            buffer = jnp.zeros((E * CAP, D), jnp.float32).at[block_slots].set(copies).reshape(E, CAP, D)
            gate_up = low_back(jnp.einsum('ecd,edf->ecf', buffer, in_table, precision=PRECISION))
            hidden = low(jax.nn.silu(gate_up[..., :FF]) * gate_up[..., FF:])
            result = low(low_back(jnp.einsum('ecf,efd->ecd', hidden, down_table, precision=PRECISION)))
            picked = result.reshape(E * CAP, D)[block_slots] * block_gates[:, None]
            return lax.optimization_barrier(jnp.sum(picked.reshape(TOK_DEV, TOPK, D), axis=1))
        expert_sum = lax.map(jax.checkpoint(expert_block), (sent_rows.reshape(blocks, TOK_DEV, D), slot_index, flat_gates))
        return middle + RESIDUAL * expert_sum.reshape(SEQ_GROUPS, GROUP_TOK, D)
    dealt_output, pullback = jax.vjp(layer_forward, dealt_tokens, q_weight, k_weight, v_weight, o_weight, gain_attn, gain_moe, in_weight, down_weight)
    gradients = pullback(dealt_cotangent)
    output = jnp.zeros_like(dealt_output).at[deal_index].set(dealt_output)
    input_grad = jnp.zeros_like(gradients[0]).at[deal_index].set(gradients[0])
    return (output, input_grad, gradients[1], gradients[2], gradients[3], gradients[4], gradients[5], gradients[6], gradients[7], gradients[8])
```

```python
import jax
import jax.numpy as jnp
from jax import lax
from jax.sharding import PartitionSpec as P

H = 24
KVH = 8
HD = 64
E = 40
FF = 512
TOPK = 8
CAP = 40


EPSILON = 1e-06
RESIDUAL = 0.22
SCORE_SCALE = 0.015625
THETA = 10000.0
NEGATIVE = -1e30
ROWS_DIMS = (((0,), (0,)), ((), ()))
COLS_DIMS = (((1,), (1,)), ((), ()))


def rms_scale(values, gain):
    return values * lax.rsqrt(jnp.mean(values * values, axis=-1, keepdims=True) + EPSILON) * gain


def rotate(values, cosine, sine_table):
    half_width = values.shape[-1] // 2
    turned = jnp.concatenate([-values[..., half_width:], values[..., :half_width]], axis=-1)
    return values * cosine + turned * sine_table


def turn_back(grads_in, cosine, sine_table):
    half_width = grads_in.shape[-1] // 2
    scaled = grads_in * sine_table
    return grads_in * cosine + jnp.concatenate(
        [scaled[..., half_width:], -scaled[..., :half_width]], axis=-1
    )


def silu_product(gate_in, up_in):
    return jax.nn.silu(gate_in) * up_in


def locate(where_at, seq_ends):
    return jnp.sum((where_at[:, None] >= seq_ends[None, :]).astype(jnp.int32), axis=-1)


def cut_block(source, begin_at, block_rows, heads):
    piece = lax.dynamic_slice_in_dim(source, begin_at, block_rows, 0)
    return piece.reshape(block_rows, heads, source.shape[1] // heads)


def group_chooser(wanted, carried, pieces, start):
    piece_rows = pieces[0].shape[0]
    inside = (wanted >= start) & (wanted < start + piece_rows)
    offset_at = jnp.clip(wanted, 0, piece_rows - 1)
    return tuple(
        (
            jnp.where(inside, lax.dynamic_slice_in_dim(member_piece, offset_at, 1, 0), member_carry)
            for member_piece, member_carry in zip(pieces, carried)
        )
    )


def per_device_wide(
    tokens,
    cotangent,
    lengths,
    deal,
    routes,
    gates,
    q_weight,
    k_weight,
    v_weight,
    o_weight,
    gain_attn,
    gain_moe,
    in_weight,
    down_weight,
):
    tok_rows = tokens.shape[1]
    model_width = tokens.shape[2]
    group_rows = tok_rows * lax.axis_size("dp")
    block_rows = min(512, group_rows)
    heads_per = H // KVH
    owner_index = lax.axis_index("expert")
    group_ids = jnp.arange(deal.shape[0], dtype=jnp.int32)
    wanted_in = jnp.sum(jnp.where(group_ids == owner_index, deal, 0))
    wanted_out = jnp.sum(jnp.where(deal == owner_index, group_ids, 0))
    dealt_tokens, dealt_cotangent = group_chooser(
        wanted_in,
        (jnp.zeros_like(tokens), jnp.zeros_like(cotangent)),
        (
            lax.all_gather(tokens, "expert", axis=0, tiled=True),
            lax.all_gather(cotangent, "expert", axis=0, tiled=True),
        ),
        jnp.int32(0),
    )
    inputs = dealt_tokens[0].astype(jnp.float32)
    q_full, k_full, v_full, o_full, gain_one, gain_two = (
        lax.all_gather(q_weight.astype(jnp.bfloat16), ("dp", "expert"), axis=0, tiled=True),
        lax.all_gather(k_weight.astype(jnp.bfloat16), ("dp", "expert"), axis=0, tiled=True),
        lax.all_gather(v_weight.astype(jnp.bfloat16), ("dp", "expert"), axis=0, tiled=True),
        lax.all_gather(o_weight.astype(jnp.bfloat16), ("dp", "expert"), axis=0, tiled=True),
        lax.all_gather(gain_attn.astype(jnp.bfloat16), ("dp", "expert"), axis=0, tiled=True),
        lax.all_gather(gain_moe.astype(jnp.bfloat16), ("dp", "expert"), axis=0, tiled=True),
    )
    gain_one = gain_one.astype(jnp.float32)
    gain_two = gain_two.astype(jnp.float32)
    seq_lengths = lengths[0]
    seq_ends = jnp.cumsum(seq_lengths)
    seq_starts = seq_ends - seq_lengths
    first_place = lax.axis_index("dp") * tok_rows
    places = first_place + jnp.arange(tok_rows, dtype=jnp.int32)
    member = (places[:, None] >= seq_starts[None, :]) & (places[:, None] < seq_ends[None, :])
    offsets = jnp.sum(jnp.where(member, places[:, None] - seq_starts[None, :], 0), axis=-1)
    frequency = THETA ** (-jnp.arange(HD // 2, dtype=jnp.float32) * 2.0 / HD)
    angles = offsets.astype(jnp.float32)[:, None] * frequency[None, :]
    angles = jnp.concatenate([angles, angles], axis=-1)[:, None, :]
    cosine = jnp.cos(angles)
    sine_table = jnp.sin(angles)
    query_seq = locate(places, seq_ends)
    seq_floor = jnp.sum(jnp.where(member[0], seq_starts, 0))
    low_block = seq_floor // block_rows
    high_block = (first_place + tok_rows - 1) // block_rows + 1
    normed = rms_scale(inputs, gain_one).astype(jnp.bfloat16)
    query_pre = jnp.dot(normed, q_full, preferred_element_type=jnp.float32).reshape(tok_rows, H, HD)
    key_pre = jnp.dot(normed, k_full, preferred_element_type=jnp.float32).reshape(tok_rows, KVH, HD)
    value_rows = jnp.dot(normed, v_full, preferred_element_type=jnp.float32).astype(jnp.bfloat16)
    queries = (
        rotate(query_pre, cosine, sine_table)
        .astype(jnp.bfloat16)
        .reshape(tok_rows, KVH, heads_per, HD)
    )
    key_rows = rotate(key_pre, cosine, sine_table).astype(jnp.bfloat16).reshape(tok_rows, KVH * HD)
    all_keys, all_values = (
        lax.all_gather(key_rows, "dp", axis=0, tiled=True),
        lax.all_gather(value_rows, "dp", axis=0, tiled=True),
    )

    def scores_for(block_id, key_block):
        begin_at = block_id * block_rows
        key_places = begin_at + jnp.arange(block_rows, dtype=jnp.int32)
        allowed = (query_seq[:, None] == locate(key_places, seq_ends)[None, :]) & (
            key_places[None, :] <= places[:, None]
        )
        raw_scores = SCORE_SCALE * jnp.einsum(
            "tkgd,skd->kgts", queries, key_block, preferred_element_type=jnp.float32
        )
        return (raw_scores, allowed)

    def stats_step(block_id, carried):
        run_top, run_total = carried
        key_block = cut_block(all_keys, block_id * block_rows, block_rows, KVH)
        raw_scores, allowed = scores_for(block_id, key_block)
        new_top = jnp.maximum(run_top, jnp.max(jnp.where(allowed, raw_scores, NEGATIVE), axis=-1))
        weights_now = jnp.where(allowed, jnp.exp(raw_scores - new_top[..., None]), 0.0)
        run_total = run_total * jnp.exp(run_top - new_top) + jnp.sum(weights_now, axis=-1)
        return (new_top, run_total)

    top_init = jnp.full((KVH, heads_per, tok_rows), NEGATIVE, jnp.float32)
    total_init = jnp.zeros((KVH, heads_per, tok_rows), jnp.float32)
    run_top, run_total = lax.fori_loop(low_block, high_block, stats_step, (top_init, total_init))
    log_total = run_top + jnp.log(run_total)

    def attn_probs(block_id, key_block):
        raw_scores, allowed = scores_for(block_id, key_block)
        return jnp.where(allowed, jnp.exp(raw_scores - log_total[..., None]), 0.0)

    def value_step(block_id, running):
        key_block = cut_block(all_keys, block_id * block_rows, block_rows, KVH)
        value_block = cut_block(all_values, block_id * block_rows, block_rows, KVH)
        chances = attn_probs(block_id, key_block).astype(jnp.bfloat16)
        return running + jnp.einsum(
            "kgts,skd->tkgd", chances, value_block, preferred_element_type=jnp.float32
        )

    mixed_init = jnp.zeros((tok_rows, KVH, heads_per, HD), jnp.float32)
    mixed_rows = lax.fori_loop(low_block, high_block, value_step, mixed_init).reshape(
        tok_rows, H * HD
    )
    mixed_low = mixed_rows.astype(jnp.bfloat16)
    branch = lax.dot_general(mixed_low, o_full, COLS_DIMS, preferred_element_type=jnp.float32)
    middle = inputs + RESIDUAL * branch
    sent_rows = rms_scale(middle, gain_two).astype(jnp.bfloat16)
    route_ids = routes[0].reshape(tok_rows * TOPK)
    matches = (route_ids[:, None] == jnp.arange(E, dtype=jnp.int32)[None, :]).astype(jnp.int32)
    slot_rank = jnp.sum(matches * jnp.cumsum(matches, axis=0), axis=-1) - 1
    slot_index = route_ids * CAP + slot_rank
    copies = jnp.repeat(sent_rows, TOPK, axis=0)
    outgoing = (
        jnp.zeros((E * CAP, model_width), jnp.bfloat16)
        .at[slot_index]
        .set(copies)
        .reshape(E, CAP, model_width)
    )
    arrived = lax.all_to_all(outgoing, "expert", split_axis=0, concat_axis=1, tiled=True)
    w_in, w_down = (
        lax.all_gather(in_weight.astype(jnp.bfloat16), "dp", axis=0, tiled=True),
        lax.all_gather(down_weight.astype(jnp.bfloat16), "dp", axis=0, tiled=True),
    )
    gate_up = jnp.einsum("erd,def->erf", arrived, w_in, preferred_element_type=jnp.float32)
    gate_part = gate_up[..., :FF]
    up_part = gate_up[..., FF:]
    hidden = silu_product(gate_part, up_part).astype(jnp.bfloat16)
    produced = jnp.einsum(
        "erf,fed->erd", hidden, w_down, preferred_element_type=jnp.float32
    ).astype(jnp.bfloat16)
    returned = lax.all_to_all(produced, "expert", split_axis=1, concat_axis=0, tiled=True).reshape(
        E * CAP, model_width
    )
    route_gates = gates[0].reshape(tok_rows * TOPK)
    picked = returned[slot_index].astype(jnp.float32) * route_gates[:, None]
    expert_sum = jnp.sum(picked.reshape(tok_rows, TOPK, model_width), axis=1)
    output = middle + RESIDUAL * expert_sum
    upstream = dealt_cotangent[0].astype(jnp.float32)
    spread = (RESIDUAL * route_gates[:, None] * jnp.repeat(upstream, TOPK, axis=0)).astype(
        jnp.bfloat16
    )
    back_out = (
        jnp.zeros((E * CAP, model_width), jnp.bfloat16)
        .at[slot_index]
        .set(spread)
        .reshape(E, CAP, model_width)
    )
    back_in = lax.all_to_all(back_out, "expert", split_axis=0, concat_axis=1, tiled=True)
    hidden_grad = jnp.einsum("erd,fed->erf", back_in, w_down, preferred_element_type=jnp.float32)
    down_term = jnp.einsum("erf,erd->fed", hidden, back_in, preferred_element_type=jnp.float32)
    ignored, silu_pull = jax.vjp(silu_product, gate_part, up_part)
    gate_grad, up_grad = silu_pull(hidden_grad)
    gate_up_grad = jnp.concatenate([gate_grad, up_grad], axis=-1).astype(jnp.bfloat16)
    in_term = jnp.einsum("erd,erf->def", arrived, gate_up_grad, preferred_element_type=jnp.float32)
    arrived_grad = jnp.einsum(
        "erf,def->erd", gate_up_grad, w_in, preferred_element_type=jnp.float32
    ).astype(jnp.bfloat16)
    sent_back = lax.all_to_all(
        arrived_grad, "expert", split_axis=1, concat_axis=0, tiled=True
    ).reshape(E * CAP, model_width)
    sent_grad = jnp.sum(
        sent_back[slot_index].astype(jnp.float32).reshape(tok_rows, TOPK, model_width), axis=1
    )
    in_grad, down_grad = (
        lax.psum_scatter(
            in_term.astype(jnp.bfloat16), "dp", scatter_dimension=0, tiled=True
        ).astype(jnp.float32),
        lax.psum_scatter(
            down_term.astype(jnp.bfloat16), "dp", scatter_dimension=0, tiled=True
        ).astype(jnp.float32),
    )
    ignored, second_pull = jax.vjp(rms_scale, middle, gain_two)
    middle_part, gain_two_term = second_pull(sent_grad)
    middle_grad = upstream + middle_part
    branch_grad = (RESIDUAL * middle_grad).astype(jnp.bfloat16)
    o_term = lax.dot_general(branch_grad, mixed_low, ROWS_DIMS, preferred_element_type=jnp.float32)
    grad_heads = jnp.dot(branch_grad, o_full, preferred_element_type=jnp.float32).astype(
        jnp.bfloat16
    )
    grad_heads = grad_heads.reshape(tok_rows, KVH, heads_per, HD)

    def delta_step(block_id, running):
        key_block = cut_block(all_keys, block_id * block_rows, block_rows, KVH)
        value_block = cut_block(all_values, block_id * block_rows, block_rows, KVH)
        chances = attn_probs(block_id, key_block)
        prob_grad = jnp.einsum(
            "tkgd,skd->kgts", grad_heads, value_block, preferred_element_type=jnp.float32
        )
        return running + jnp.sum(chances * prob_grad, axis=-1)

    row_delta = lax.fori_loop(
        low_block, high_block, delta_step, jnp.zeros((KVH, heads_per, tok_rows), jnp.float32)
    )

    def grad_step(block_id, carried):
        query_grad, key_buffer, value_buffer = carried
        begin_at = block_id * block_rows
        key_block = cut_block(all_keys, begin_at, block_rows, KVH)
        value_block = cut_block(all_values, begin_at, block_rows, KVH)
        chances = attn_probs(block_id, key_block)
        prob_grad = jnp.einsum(
            "tkgd,skd->kgts", grad_heads, value_block, preferred_element_type=jnp.float32
        )
        score_grad = (chances * (prob_grad - row_delta[..., None])).astype(jnp.bfloat16)
        query_grad = query_grad + SCORE_SCALE * jnp.einsum(
            "kgts,skd->tkgd", score_grad, key_block, preferred_element_type=jnp.float32
        )
        key_part = SCORE_SCALE * jnp.einsum(
            "kgts,tkgd->skd", score_grad, queries, preferred_element_type=jnp.float32
        )
        value_part = jnp.einsum(
            "kgts,tkgd->skd",
            chances.astype(jnp.bfloat16),
            grad_heads,
            preferred_element_type=jnp.float32,
        )
        key_buffer = lax.dynamic_update_slice_in_dim(
            key_buffer, key_part.reshape(block_rows, KVH * HD), begin_at, 0
        )
        value_buffer = lax.dynamic_update_slice_in_dim(
            value_buffer, value_part.reshape(block_rows, KVH * HD), begin_at, 0
        )
        return (query_grad, key_buffer, value_buffer)

    grad_init = (
        jnp.zeros((tok_rows, KVH, heads_per, HD), jnp.float32),
        jnp.zeros((group_rows, KVH * HD), jnp.float32),
        jnp.zeros((group_rows, KVH * HD), jnp.float32),
    )
    query_grad, key_buffer, value_buffer = lax.fori_loop(
        low_block, high_block, grad_step, grad_init
    )
    key_grad, value_grad = (
        lax.psum_scatter(
            key_buffer.astype(jnp.bfloat16), "dp", scatter_dimension=0, tiled=True
        ).astype(jnp.float32),
        lax.psum_scatter(
            value_buffer.astype(jnp.bfloat16), "dp", scatter_dimension=0, tiled=True
        ).astype(jnp.float32),
    )
    query_low = (
        turn_back(query_grad.reshape(tok_rows, H, HD), cosine, sine_table)
        .reshape(tok_rows, H * HD)
        .astype(jnp.bfloat16)
    )
    key_low = (
        turn_back(key_grad.reshape(tok_rows, KVH, HD), cosine, sine_table)
        .reshape(tok_rows, KVH * HD)
        .astype(jnp.bfloat16)
    )
    value_low = value_grad.astype(jnp.bfloat16)
    q_term = lax.dot_general(normed, query_low, ROWS_DIMS, preferred_element_type=jnp.float32)
    k_term = lax.dot_general(normed, key_low, ROWS_DIMS, preferred_element_type=jnp.float32)
    v_term = lax.dot_general(normed, value_low, ROWS_DIMS, preferred_element_type=jnp.float32)
    normed_grad = lax.dot_general(query_low, q_full, COLS_DIMS, preferred_element_type=jnp.float32)
    normed_grad = normed_grad + lax.dot_general(
        key_low, k_full, COLS_DIMS, preferred_element_type=jnp.float32
    )
    normed_grad = normed_grad + lax.dot_general(
        value_low, v_full, COLS_DIMS, preferred_element_type=jnp.float32
    )
    ignored, first_pull = jax.vjp(rms_scale, inputs, gain_one)
    input_part, gain_one_term = first_pull(normed_grad)
    input_grad = middle_grad + input_part
    q_grad, k_grad, v_grad, o_grad, gain_attn_grad, gain_moe_grad = (
        lax.psum_scatter(q_term, ("dp", "expert"), scatter_dimension=0, tiled=True),
        lax.psum_scatter(k_term, ("dp", "expert"), scatter_dimension=0, tiled=True),
        lax.psum_scatter(v_term, ("dp", "expert"), scatter_dimension=0, tiled=True),
        lax.psum_scatter(o_term, ("dp", "expert"), scatter_dimension=0, tiled=True),
        lax.psum_scatter(gain_one_term, ("dp", "expert"), scatter_dimension=0, tiled=True),
        lax.psum_scatter(gain_two_term, ("dp", "expert"), scatter_dimension=0, tiled=True),
    )
    given_output, given_input_grad = group_chooser(
        wanted_out,
        (
            jnp.zeros((1, tok_rows, model_width), jnp.float32),
            jnp.zeros((1, tok_rows, model_width), jnp.float32),
        ),
        (
            lax.all_gather(output[None].astype(jnp.bfloat16), "expert", axis=0, tiled=True).astype(
                jnp.float32
            ),
            lax.all_gather(
                input_grad[None].astype(jnp.bfloat16), "expert", axis=0, tiled=True
            ).astype(jnp.float32),
        ),
        jnp.int32(0),
    )
    return (
        given_output,
        given_input_grad,
        q_grad,
        k_grad,
        v_grad,
        o_grad,
        gain_attn_grad,
        gain_moe_grad,
        in_grad,
        down_grad,
    )


def rounded(values):
    return lax.reduce_precision(values, 8, 7)


def rope_parts(seq_lengths, rows):
    seq_ends = jnp.cumsum(seq_lengths)
    seq_starts = seq_ends - seq_lengths
    places = jnp.arange(rows, dtype=jnp.int32)
    member = (places[:, None] >= seq_starts[None, :]) & (places[:, None] < seq_ends[None, :])
    offsets = jnp.sum(jnp.where(member, places[:, None] - seq_starts[None, :], 0), axis=-1)
    frequency = THETA ** (-jnp.arange(HD // 2, dtype=jnp.float32) * 2.0 / HD)
    angles = offsets.astype(jnp.float32)[:, None] * frequency[None, :]
    angles = jnp.concatenate([angles, angles], axis=-1)[:, None, :]
    seq_ids = locate(places, seq_ends)
    return places, seq_ids, jnp.cos(angles), jnp.sin(angles)


def per_device(
    tokens,
    cotangent,
    lengths,
    deal,
    routes,
    gates,
    q_weight,
    k_weight,
    v_weight,
    o_weight,
    gain_attn,
    gain_moe,
    in_weight,
    down_weight,
):
    n_dp = lax.axis_size("dp")
    n_ex = lax.axis_size("expert")
    tok_rows = tokens.shape[1]
    model = tokens.shape[2]
    group_rows = tok_rows * n_dp
    kv_here = KVH // n_dp
    heads_per = H // KVH
    q_cols = kv_here * heads_per * HD
    kv_cols = kv_here * HD
    own_experts = in_weight.shape[1]
    ff_here = FF // n_dp
    ff_cols = own_experts * ff_here
    w_rows = q_weight.shape[0]
    both = ("dp", "expert")
    ex_index = lax.axis_index("expert")
    group_ids = jnp.arange(deal.shape[0], dtype=jnp.int32)
    dealt_of = jnp.argmax((deal[None, :] == group_ids[:, None]).astype(jnp.int32), axis=1)
    own_dealt = jnp.sum(jnp.where(deal == ex_index, group_ids, 0))

    group_tokens = lax.all_gather(tokens[0], "dp", axis=0, tiled=True)

    def by_owner(weight):
        return weight.astype(jnp.bfloat16).reshape(w_rows, n_dp, weight.shape[1] // n_dp)

    length_parts = jnp.stack([lengths[0] // 128, lengths[0] % 128]).reshape(-1).astype(jnp.bfloat16)
    n_len = length_parts.shape[0]
    extra = jnp.concatenate(
        [
            gain_attn.astype(jnp.bfloat16)[:, None],
            gain_moe.astype(jnp.bfloat16)[:, None],
            jnp.broadcast_to(length_parts[None, :], (w_rows, n_len)),
            jnp.zeros((w_rows, 126 - n_len), jnp.bfloat16),
        ],
        axis=1,
    )
    attn_out = jnp.concatenate(
        [
            by_owner(q_weight),
            by_owner(k_weight),
            by_owner(v_weight),
            by_owner(o_weight),
            jnp.broadcast_to(extra[:, None, :], (w_rows, n_dp, 128)),
        ],
        axis=2,
    ).transpose(1, 0, 2)
    attn_in = lax.all_to_all(attn_out, "dp", split_axis=0, concat_axis=0, tiled=True)
    attn_all = lax.all_gather(attn_in, "expert", axis=0)
    attn_w = attn_all.transpose(1, 0, 2, 3).reshape(model, -1)
    qkv_cols = q_cols + 2 * kv_cols
    qkv_w = attn_w[:, :qkv_cols]
    o_w = attn_w[:, qkv_cols : qkv_cols + q_cols]
    side = attn_w[:, qkv_cols + q_cols :]
    gain_one = side[:, 0].astype(jnp.float32)
    gain_two = side[:, 1].astype(jnp.float32)
    own_parts = lax.dynamic_index_in_dim(attn_all, own_dealt, 0, keepdims=False)[
        0, 0, qkv_cols + q_cols + 2 : qkv_cols + q_cols + 2 + n_len
    ].astype(jnp.int32)
    seq_lengths = own_parts[: n_len // 2] * 128 + own_parts[n_len // 2 :]

    gate_rows = gates[0]
    gate_top = rounded(gate_rows)
    gate_mid = rounded(gate_rows - gate_top)
    gate_low = gate_rows - gate_top - gate_mid
    meta = jnp.concatenate(
        [
            routes[0].astype(jnp.float32),
            gate_top,
            gate_mid,
            gate_low,
            jnp.zeros((tok_rows, 128 - 4 * TOPK), jnp.float32),
        ],
        axis=1,
    ).astype(jnp.bfloat16)
    cot_all = lax.all_gather(
        jnp.concatenate([cotangent[0], meta], axis=1), both, axis=0, tiled=True
    )

    in_out = (
        in_weight.astype(jnp.bfloat16)
        .reshape(in_weight.shape[0], own_experts, 2, n_dp, ff_here)
        .transpose(3, 0, 2, 1, 4)
        .reshape(n_dp, in_weight.shape[0], 2 * ff_cols)
    )
    in_w = lax.all_to_all(in_out, "dp", split_axis=0, concat_axis=0, tiled=True).reshape(
        model, 2 * ff_cols
    )
    down_w = down_weight.astype(jnp.bfloat16).transpose(1, 0, 2).reshape(ff_cols, model)

    places, seq_ids, cosine, sine_table = rope_parts(seq_lengths, group_rows)
    group_inputs = group_tokens.astype(jnp.float32)
    first_scale = lax.rsqrt(jnp.mean(group_inputs * group_inputs, axis=-1, keepdims=True) + EPSILON)
    normed = (group_inputs * first_scale * gain_one).astype(jnp.bfloat16)
    qkv = jnp.dot(normed, qkv_w, preferred_element_type=jnp.float32)
    queries = rotate(
        qkv[:, :q_cols].reshape(group_rows, kv_here * heads_per, HD), cosine, sine_table
    )
    queries = queries.astype(jnp.bfloat16).reshape(group_rows, kv_here, heads_per, HD)
    keys = rotate(
        qkv[:, q_cols : q_cols + kv_cols].reshape(group_rows, kv_here, HD), cosine, sine_table
    ).astype(jnp.bfloat16)
    vals = qkv[:, q_cols + kv_cols :].astype(jnp.bfloat16).reshape(group_rows, kv_here, HD)
    allowed = (seq_ids[:, None] == seq_ids[None, :]) & (places[None, :] <= places[:, None])
    raw_scores = SCORE_SCALE * jnp.einsum(
        "tkgd,skd->kgts", queries, keys, preferred_element_type=jnp.float32
    )
    chances = jax.nn.softmax(jnp.where(allowed, raw_scores, NEGATIVE), axis=-1)
    chances_low = chances.astype(jnp.bfloat16)
    mixed_low = (
        jnp.einsum("kgts,skd->tkgd", chances_low, vals, preferred_element_type=jnp.float32)
        .astype(jnp.bfloat16)
        .reshape(group_rows, q_cols)
    )
    branch_part = lax.dot_general(mixed_low, o_w, COLS_DIMS, preferred_element_type=jnp.float32)
    branch = lax.psum_scatter(
        branch_part.astype(jnp.bfloat16), "dp", scatter_dimension=0, tiled=True
    ).astype(jnp.float32)
    inputs = tokens[0].astype(jnp.float32)
    middle = inputs + RESIDUAL * branch
    second_scale = lax.rsqrt(jnp.mean(middle * middle, axis=-1, keepdims=True) + EPSILON)
    sent_rows = (middle * second_scale * gain_two).astype(jnp.bfloat16)
    sent_all = lax.all_gather(sent_rows, both, axis=0, tiled=True)

    meta_all = cot_all[:, model:].reshape(n_dp, n_ex, tok_rows, 128)
    meta_all = jnp.take(meta_all, dealt_of, axis=1).reshape(-1, 128).astype(jnp.float32)
    route_all = meta_all[:, :TOPK]
    gate_all = (
        meta_all[:, TOPK : 2 * TOPK]
        + meta_all[:, 2 * TOPK : 3 * TOPK]
        + meta_all[:, 3 * TOPK : 4 * TOPK]
    )
    expert_ids = (ex_index * own_experts + jnp.arange(own_experts, dtype=jnp.int32)).astype(
        jnp.float32
    )
    dense_gates = jnp.sum(
        jnp.where(route_all[:, :, None] == expert_ids[None, None, :], gate_all[:, :, None], 0.0),
        axis=1,
    )
    gate_cols = jnp.repeat(dense_gates, ff_here, axis=1)
    cot_rows = cot_all[:, :model]

    gate_up = jnp.dot(sent_all, in_w, preferred_element_type=jnp.float32)
    gate_part = gate_up[:, :ff_cols]
    up_part = gate_up[:, ff_cols:]
    sigma = jax.nn.sigmoid(gate_part)
    silu = gate_part * sigma
    hidden = (silu * up_part).astype(jnp.bfloat16).astype(jnp.float32)
    weighted = (gate_cols * hidden).astype(jnp.bfloat16)
    pulled = lax.dot_general(cot_rows, down_w, COLS_DIMS, preferred_element_type=jnp.float32)
    hidden_grad = RESIDUAL * gate_cols * pulled
    gate_grad = hidden_grad * up_part * (sigma * (1.0 + gate_part * (1.0 - sigma)))
    up_grad = hidden_grad * silu
    gate_up_grad = jnp.concatenate([gate_grad, up_grad], axis=1).astype(jnp.bfloat16)
    sent_grad_part = lax.dot_general(
        gate_up_grad, in_w, COLS_DIMS, preferred_element_type=jnp.float32
    ).astype(jnp.bfloat16)
    sent_grad = lax.psum_scatter(sent_grad_part, both, scatter_dimension=0, tiled=True).astype(
        jnp.float32
    )
    out_part = jnp.dot(weighted, down_w, preferred_element_type=jnp.float32).astype(jnp.bfloat16)
    expert_sum = lax.psum_scatter(out_part, both, scatter_dimension=0, tiled=True).astype(
        jnp.float32
    )
    output = middle + RESIDUAL * expert_sum
    in_term = lax.dot_general(sent_all, gate_up_grad, ROWS_DIMS, preferred_element_type=jnp.float32)
    in_back = lax.all_to_all(
        in_term.astype(jnp.bfloat16).reshape(n_dp, in_weight.shape[0], 2 * ff_cols),
        "dp",
        split_axis=0,
        concat_axis=0,
        tiled=True,
    )
    in_grad = (
        in_back.reshape(n_dp, in_weight.shape[0], 2, own_experts, ff_here)
        .transpose(1, 3, 2, 0, 4)
        .reshape(in_weight.shape)
        .astype(jnp.float32)
    )
    down_term = RESIDUAL * lax.dot_general(
        weighted, cot_rows, ROWS_DIMS, preferred_element_type=jnp.float32
    )
    down_grad = down_term.reshape(own_experts, ff_here, model).transpose(1, 0, 2)

    upstream = cotangent[0].astype(jnp.float32)
    scaled_grad = sent_grad * gain_two
    middle_grad = (
        upstream
        + second_scale * scaled_grad
        - middle
        * second_scale**3
        * jnp.mean(scaled_grad * middle, axis=-1, keepdims=True)
    )
    gain_two_part = jnp.sum(sent_grad * middle * second_scale, axis=0)
    branch_grad = (RESIDUAL * middle_grad).astype(jnp.bfloat16)
    branch_grad_all = lax.all_gather(branch_grad, "dp", axis=0, tiled=True)

    o_term = lax.dot_general(
        branch_grad_all, mixed_low, ROWS_DIMS, preferred_element_type=jnp.float32
    )
    grad_heads = (
        jnp.dot(branch_grad_all, o_w, preferred_element_type=jnp.float32)
        .astype(jnp.bfloat16)
        .reshape(group_rows, kv_here, heads_per, HD)
    )
    prob_grad = jnp.einsum(
        "tkgd,skd->kgts", grad_heads, vals, preferred_element_type=jnp.float32
    )
    row_delta = jnp.sum(chances * prob_grad, axis=-1, keepdims=True)
    score_grad = (chances * (prob_grad - row_delta)).astype(jnp.bfloat16)
    query_grad = SCORE_SCALE * jnp.einsum(
        "kgts,skd->tkgd", score_grad, keys, preferred_element_type=jnp.float32
    )
    key_grad = SCORE_SCALE * jnp.einsum(
        "kgts,tkgd->skd", score_grad, queries, preferred_element_type=jnp.float32
    )
    value_grad = jnp.einsum(
        "kgts,tkgd->skd", chances_low, grad_heads, preferred_element_type=jnp.float32
    )
    query_low = turn_back(
        query_grad.reshape(group_rows, kv_here * heads_per, HD), cosine, sine_table
    ).reshape(group_rows, q_cols)
    key_low = turn_back(key_grad, cosine, sine_table).reshape(group_rows, kv_cols)
    qkv_grad = jnp.concatenate(
        [query_low, key_low, value_grad.reshape(group_rows, kv_cols)], axis=1
    ).astype(jnp.bfloat16)
    normed_grad_part = lax.dot_general(
        qkv_grad, qkv_w, COLS_DIMS, preferred_element_type=jnp.float32
    )
    gain_one_part = jnp.sum(normed_grad_part * group_inputs * first_scale, axis=0)
    normed_grad = lax.psum_scatter(
        normed_grad_part.astype(jnp.bfloat16), "dp", scatter_dimension=0, tiled=True
    ).astype(jnp.float32)
    qkv_term = lax.dot_general(normed, qkv_grad, ROWS_DIMS, preferred_element_type=jnp.float32)
    grads = jnp.concatenate(
        [
            qkv_term,
            o_term,
            gain_one_part[:, None],
            gain_two_part[:, None],
            jnp.zeros((model, 126), jnp.float32),
        ],
        axis=1,
    ).astype(jnp.bfloat16)
    grads = lax.psum_scatter(
        grads.reshape(n_dp, n_ex, w_rows, -1).transpose(1, 0, 2, 3),
        "expert",
        scatter_dimension=0,
        tiled=True,
    )[0]
    grads = lax.all_to_all(grads, "dp", split_axis=0, concat_axis=0, tiled=True).astype(jnp.float32)

    def own_rows(begin, width):
        return grads[:, :, begin : begin + width].transpose(1, 0, 2).reshape(w_rows, n_dp * width)

    q_grad = own_rows(0, q_cols)
    k_grad = own_rows(q_cols, kv_cols)
    v_grad = own_rows(q_cols + kv_cols, kv_cols)
    o_grad = own_rows(qkv_cols, q_cols)
    gain_attn_grad = jnp.sum(grads[:, :, qkv_cols + q_cols], axis=0)
    gain_moe_grad = jnp.sum(grads[:, :, qkv_cols + q_cols + 1], axis=0)

    own_scale = lax.rsqrt(jnp.mean(inputs * inputs, axis=-1, keepdims=True) + EPSILON)
    scaled_one = normed_grad * gain_one
    input_grad = (
        middle_grad
        + own_scale * scaled_one
        - inputs * own_scale**3 * jnp.mean(scaled_one * inputs, axis=-1, keepdims=True)
    )
    return (
        output[None],
        input_grad[None],
        q_grad,
        k_grad,
        v_grad,
        o_grad,
        gain_attn_grad,
        gain_moe_grad,
        in_grad,
        down_grad,
    )


def solution(mesh):
    placed = (
        P("expert", "dp", None),
        P("expert", "dp", None),
        P("expert", None),
        P(),
        P("expert", "dp", None),
        P("expert", "dp", None),
        P(("dp", "expert"), None),
        P(("dp", "expert"), None),
        P(("dp", "expert"), None),
        P(("dp", "expert"), None),
        P(("dp", "expert")),
        P(("dp", "expert")),
        P("dp", "expert", None),
        P("dp", "expert", None),
    )
    n_dp = mesh.shape["dp"]
    split_heads = KVH % n_dp == 0 and (FF // n_dp) % 64 == 0
    return jax.shard_map(
        per_device if split_heads else per_device_wide,
        mesh=mesh,
        in_specs=placed,
        out_specs=(
            P("expert", "dp", None),
            P("expert", "dp", None),
            P(("dp", "expert"), None),
            P(("dp", "expert"), None),
            P(("dp", "expert"), None),
            P(("dp", "expert"), None),
            P(("dp", "expert")),
            P(("dp", "expert")),
            P("dp", "expert", None),
            P("dp", "expert", None),
        ),
        check_vma=False,
    )
```

```python
import functools

import jax
import jax.numpy as jnp
from jax import lax
from jax.experimental import pallas as pl
from jax.experimental.pallas import tpu as pltpu
from jax.sharding import PartitionSpec as P

H = 24
KVH = 8
HD = 64
E = 40
FF = 512
TOPK = 8
CAP = 40


EPSILON = 1e-06
RESIDUAL = 0.22
SCORE_SCALE = 0.015625
THETA = 10000.0
NEGATIVE = -1e30
ROWS_DIMS = (((0,), (0,)), ((), ()))
COLS_DIMS = (((1,), (1,)), ((), ()))


def rms_scale(values, gain):
    return values * lax.rsqrt(jnp.mean(values * values, axis=-1, keepdims=True) + EPSILON) * gain


def rotate(values, cosine, sine_table):
    half_width = values.shape[-1] // 2
    turned = jnp.concatenate([-values[..., half_width:], values[..., :half_width]], axis=-1)
    return values * cosine + turned * sine_table


def turn_back(grads_in, cosine, sine_table):
    half_width = grads_in.shape[-1] // 2
    scaled = grads_in * sine_table
    return grads_in * cosine + jnp.concatenate(
        [scaled[..., half_width:], -scaled[..., :half_width]], axis=-1
    )


def silu_product(gate_in, up_in):
    return jax.nn.silu(gate_in) * up_in


def locate(where_at, seq_ends):
    return jnp.sum((where_at[:, None] >= seq_ends[None, :]).astype(jnp.int32), axis=-1)


def cut_block(source, begin_at, block_rows, heads):
    piece = lax.dynamic_slice_in_dim(source, begin_at, block_rows, 0)
    return piece.reshape(block_rows, heads, source.shape[1] // heads)


def group_chooser(wanted, carried, pieces, start):
    piece_rows = pieces[0].shape[0]
    inside = (wanted >= start) & (wanted < start + piece_rows)
    offset_at = jnp.clip(wanted, 0, piece_rows - 1)
    return tuple(
        (
            jnp.where(inside, lax.dynamic_slice_in_dim(member_piece, offset_at, 1, 0), member_carry)
            for member_piece, member_carry in zip(pieces, carried)
        )
    )


def per_device_wide(
    tokens,
    cotangent,
    lengths,
    deal,
    routes,
    gates,
    q_weight,
    k_weight,
    v_weight,
    o_weight,
    gain_attn,
    gain_moe,
    in_weight,
    down_weight,
):
    tok_rows = tokens.shape[1]
    model_width = tokens.shape[2]
    group_rows = tok_rows * lax.axis_size("dp")
    block_rows = min(512, group_rows)
    heads_per = H // KVH
    owner_index = lax.axis_index("expert")
    group_ids = jnp.arange(deal.shape[0], dtype=jnp.int32)
    wanted_in = jnp.sum(jnp.where(group_ids == owner_index, deal, 0))
    wanted_out = jnp.sum(jnp.where(deal == owner_index, group_ids, 0))
    dealt_tokens, dealt_cotangent = group_chooser(
        wanted_in,
        (jnp.zeros_like(tokens), jnp.zeros_like(cotangent)),
        (
            lax.all_gather(tokens, "expert", axis=0, tiled=True),
            lax.all_gather(cotangent, "expert", axis=0, tiled=True),
        ),
        jnp.int32(0),
    )
    inputs = dealt_tokens[0].astype(jnp.float32)
    q_full, k_full, v_full, o_full, gain_one, gain_two = (
        lax.all_gather(q_weight.astype(jnp.bfloat16), ("dp", "expert"), axis=0, tiled=True),
        lax.all_gather(k_weight.astype(jnp.bfloat16), ("dp", "expert"), axis=0, tiled=True),
        lax.all_gather(v_weight.astype(jnp.bfloat16), ("dp", "expert"), axis=0, tiled=True),
        lax.all_gather(o_weight.astype(jnp.bfloat16), ("dp", "expert"), axis=0, tiled=True),
        lax.all_gather(gain_attn.astype(jnp.bfloat16), ("dp", "expert"), axis=0, tiled=True),
        lax.all_gather(gain_moe.astype(jnp.bfloat16), ("dp", "expert"), axis=0, tiled=True),
    )
    gain_one = gain_one.astype(jnp.float32)
    gain_two = gain_two.astype(jnp.float32)
    seq_lengths = lengths[0]
    seq_ends = jnp.cumsum(seq_lengths)
    seq_starts = seq_ends - seq_lengths
    first_place = lax.axis_index("dp") * tok_rows
    places = first_place + jnp.arange(tok_rows, dtype=jnp.int32)
    member = (places[:, None] >= seq_starts[None, :]) & (places[:, None] < seq_ends[None, :])
    offsets = jnp.sum(jnp.where(member, places[:, None] - seq_starts[None, :], 0), axis=-1)
    frequency = THETA ** (-jnp.arange(HD // 2, dtype=jnp.float32) * 2.0 / HD)
    angles = offsets.astype(jnp.float32)[:, None] * frequency[None, :]
    angles = jnp.concatenate([angles, angles], axis=-1)[:, None, :]
    cosine = jnp.cos(angles)
    sine_table = jnp.sin(angles)
    query_seq = locate(places, seq_ends)
    seq_floor = jnp.sum(jnp.where(member[0], seq_starts, 0))
    low_block = seq_floor // block_rows
    high_block = (first_place + tok_rows - 1) // block_rows + 1
    normed = rms_scale(inputs, gain_one).astype(jnp.bfloat16)
    query_pre = jnp.dot(normed, q_full, preferred_element_type=jnp.float32).reshape(tok_rows, H, HD)
    key_pre = jnp.dot(normed, k_full, preferred_element_type=jnp.float32).reshape(tok_rows, KVH, HD)
    value_rows = jnp.dot(normed, v_full, preferred_element_type=jnp.float32).astype(jnp.bfloat16)
    queries = (
        rotate(query_pre, cosine, sine_table)
        .astype(jnp.bfloat16)
        .reshape(tok_rows, KVH, heads_per, HD)
    )
    key_rows = rotate(key_pre, cosine, sine_table).astype(jnp.bfloat16).reshape(tok_rows, KVH * HD)
    all_keys, all_values = (
        lax.all_gather(key_rows, "dp", axis=0, tiled=True),
        lax.all_gather(value_rows, "dp", axis=0, tiled=True),
    )

    def scores_for(block_id, key_block):
        begin_at = block_id * block_rows
        key_places = begin_at + jnp.arange(block_rows, dtype=jnp.int32)
        allowed = (query_seq[:, None] == locate(key_places, seq_ends)[None, :]) & (
            key_places[None, :] <= places[:, None]
        )
        raw_scores = SCORE_SCALE * jnp.einsum(
            "tkgd,skd->kgts", queries, key_block, preferred_element_type=jnp.float32
        )
        return (raw_scores, allowed)

    def stats_step(block_id, carried):
        run_top, run_total = carried
        key_block = cut_block(all_keys, block_id * block_rows, block_rows, KVH)
        raw_scores, allowed = scores_for(block_id, key_block)
        new_top = jnp.maximum(run_top, jnp.max(jnp.where(allowed, raw_scores, NEGATIVE), axis=-1))
        weights_now = jnp.where(allowed, jnp.exp(raw_scores - new_top[..., None]), 0.0)
        run_total = run_total * jnp.exp(run_top - new_top) + jnp.sum(weights_now, axis=-1)
        return (new_top, run_total)

    top_init = jnp.full((KVH, heads_per, tok_rows), NEGATIVE, jnp.float32)
    total_init = jnp.zeros((KVH, heads_per, tok_rows), jnp.float32)
    run_top, run_total = lax.fori_loop(low_block, high_block, stats_step, (top_init, total_init))
    log_total = run_top + jnp.log(run_total)

    def attn_probs(block_id, key_block):
        raw_scores, allowed = scores_for(block_id, key_block)
        return jnp.where(allowed, jnp.exp(raw_scores - log_total[..., None]), 0.0)

    def value_step(block_id, running):
        key_block = cut_block(all_keys, block_id * block_rows, block_rows, KVH)
        value_block = cut_block(all_values, block_id * block_rows, block_rows, KVH)
        chances = attn_probs(block_id, key_block).astype(jnp.bfloat16)
        return running + jnp.einsum(
            "kgts,skd->tkgd", chances, value_block, preferred_element_type=jnp.float32
        )

    mixed_init = jnp.zeros((tok_rows, KVH, heads_per, HD), jnp.float32)
    mixed_rows = lax.fori_loop(low_block, high_block, value_step, mixed_init).reshape(
        tok_rows, H * HD
    )
    mixed_low = mixed_rows.astype(jnp.bfloat16)
    branch = lax.dot_general(mixed_low, o_full, COLS_DIMS, preferred_element_type=jnp.float32)
    middle = inputs + RESIDUAL * branch
    sent_rows = rms_scale(middle, gain_two).astype(jnp.bfloat16)
    route_ids = routes[0].reshape(tok_rows * TOPK)
    matches = (route_ids[:, None] == jnp.arange(E, dtype=jnp.int32)[None, :]).astype(jnp.int32)
    slot_rank = jnp.sum(matches * jnp.cumsum(matches, axis=0), axis=-1) - 1
    slot_index = route_ids * CAP + slot_rank
    copies = jnp.repeat(sent_rows, TOPK, axis=0)
    outgoing = (
        jnp.zeros((E * CAP, model_width), jnp.bfloat16)
        .at[slot_index]
        .set(copies)
        .reshape(E, CAP, model_width)
    )
    arrived = lax.all_to_all(outgoing, "expert", split_axis=0, concat_axis=1, tiled=True)
    w_in, w_down = (
        lax.all_gather(in_weight.astype(jnp.bfloat16), "dp", axis=0, tiled=True),
        lax.all_gather(down_weight.astype(jnp.bfloat16), "dp", axis=0, tiled=True),
    )
    gate_up = jnp.einsum("erd,def->erf", arrived, w_in, preferred_element_type=jnp.float32)
    gate_part = gate_up[..., :FF]
    up_part = gate_up[..., FF:]
    hidden = silu_product(gate_part, up_part).astype(jnp.bfloat16)
    produced = jnp.einsum(
        "erf,fed->erd", hidden, w_down, preferred_element_type=jnp.float32
    ).astype(jnp.bfloat16)
    returned = lax.all_to_all(produced, "expert", split_axis=1, concat_axis=0, tiled=True).reshape(
        E * CAP, model_width
    )
    route_gates = gates[0].reshape(tok_rows * TOPK)
    picked = returned[slot_index].astype(jnp.float32) * route_gates[:, None]
    expert_sum = jnp.sum(picked.reshape(tok_rows, TOPK, model_width), axis=1)
    output = middle + RESIDUAL * expert_sum
    upstream = dealt_cotangent[0].astype(jnp.float32)
    spread = (RESIDUAL * route_gates[:, None] * jnp.repeat(upstream, TOPK, axis=0)).astype(
        jnp.bfloat16
    )
    back_out = (
        jnp.zeros((E * CAP, model_width), jnp.bfloat16)
        .at[slot_index]
        .set(spread)
        .reshape(E, CAP, model_width)
    )
    back_in = lax.all_to_all(back_out, "expert", split_axis=0, concat_axis=1, tiled=True)
    hidden_grad = jnp.einsum("erd,fed->erf", back_in, w_down, preferred_element_type=jnp.float32)
    down_term = jnp.einsum("erf,erd->fed", hidden, back_in, preferred_element_type=jnp.float32)
    ignored, silu_pull = jax.vjp(silu_product, gate_part, up_part)
    gate_grad, up_grad = silu_pull(hidden_grad)
    gate_up_grad = jnp.concatenate([gate_grad, up_grad], axis=-1).astype(jnp.bfloat16)
    in_term = jnp.einsum("erd,erf->def", arrived, gate_up_grad, preferred_element_type=jnp.float32)
    arrived_grad = jnp.einsum(
        "erf,def->erd", gate_up_grad, w_in, preferred_element_type=jnp.float32
    ).astype(jnp.bfloat16)
    sent_back = lax.all_to_all(
        arrived_grad, "expert", split_axis=1, concat_axis=0, tiled=True
    ).reshape(E * CAP, model_width)
    sent_grad = jnp.sum(
        sent_back[slot_index].astype(jnp.float32).reshape(tok_rows, TOPK, model_width), axis=1
    )
    in_grad, down_grad = (
        lax.psum_scatter(
            in_term.astype(jnp.bfloat16), "dp", scatter_dimension=0, tiled=True
        ).astype(jnp.float32),
        lax.psum_scatter(
            down_term.astype(jnp.bfloat16), "dp", scatter_dimension=0, tiled=True
        ).astype(jnp.float32),
    )
    ignored, second_pull = jax.vjp(rms_scale, middle, gain_two)
    middle_part, gain_two_term = second_pull(sent_grad)
    middle_grad = upstream + middle_part
    branch_grad = (RESIDUAL * middle_grad).astype(jnp.bfloat16)
    o_term = lax.dot_general(branch_grad, mixed_low, ROWS_DIMS, preferred_element_type=jnp.float32)
    grad_heads = jnp.dot(branch_grad, o_full, preferred_element_type=jnp.float32).astype(
        jnp.bfloat16
    )
    grad_heads = grad_heads.reshape(tok_rows, KVH, heads_per, HD)

    def delta_step(block_id, running):
        key_block = cut_block(all_keys, block_id * block_rows, block_rows, KVH)
        value_block = cut_block(all_values, block_id * block_rows, block_rows, KVH)
        chances = attn_probs(block_id, key_block)
        prob_grad = jnp.einsum(
            "tkgd,skd->kgts", grad_heads, value_block, preferred_element_type=jnp.float32
        )
        return running + jnp.sum(chances * prob_grad, axis=-1)

    row_delta = lax.fori_loop(
        low_block, high_block, delta_step, jnp.zeros((KVH, heads_per, tok_rows), jnp.float32)
    )

    def grad_step(block_id, carried):
        query_grad, key_buffer, value_buffer = carried
        begin_at = block_id * block_rows
        key_block = cut_block(all_keys, begin_at, block_rows, KVH)
        value_block = cut_block(all_values, begin_at, block_rows, KVH)
        chances = attn_probs(block_id, key_block)
        prob_grad = jnp.einsum(
            "tkgd,skd->kgts", grad_heads, value_block, preferred_element_type=jnp.float32
        )
        score_grad = (chances * (prob_grad - row_delta[..., None])).astype(jnp.bfloat16)
        query_grad = query_grad + SCORE_SCALE * jnp.einsum(
            "kgts,skd->tkgd", score_grad, key_block, preferred_element_type=jnp.float32
        )
        key_part = SCORE_SCALE * jnp.einsum(
            "kgts,tkgd->skd", score_grad, queries, preferred_element_type=jnp.float32
        )
        value_part = jnp.einsum(
            "kgts,tkgd->skd",
            chances.astype(jnp.bfloat16),
            grad_heads,
            preferred_element_type=jnp.float32,
        )
        key_buffer = lax.dynamic_update_slice_in_dim(
            key_buffer, key_part.reshape(block_rows, KVH * HD), begin_at, 0
        )
        value_buffer = lax.dynamic_update_slice_in_dim(
            value_buffer, value_part.reshape(block_rows, KVH * HD), begin_at, 0
        )
        return (query_grad, key_buffer, value_buffer)

    grad_init = (
        jnp.zeros((tok_rows, KVH, heads_per, HD), jnp.float32),
        jnp.zeros((group_rows, KVH * HD), jnp.float32),
        jnp.zeros((group_rows, KVH * HD), jnp.float32),
    )
    query_grad, key_buffer, value_buffer = lax.fori_loop(
        low_block, high_block, grad_step, grad_init
    )
    key_grad, value_grad = (
        lax.psum_scatter(
            key_buffer.astype(jnp.bfloat16), "dp", scatter_dimension=0, tiled=True
        ).astype(jnp.float32),
        lax.psum_scatter(
            value_buffer.astype(jnp.bfloat16), "dp", scatter_dimension=0, tiled=True
        ).astype(jnp.float32),
    )
    query_low = (
        turn_back(query_grad.reshape(tok_rows, H, HD), cosine, sine_table)
        .reshape(tok_rows, H * HD)
        .astype(jnp.bfloat16)
    )
    key_low = (
        turn_back(key_grad.reshape(tok_rows, KVH, HD), cosine, sine_table)
        .reshape(tok_rows, KVH * HD)
        .astype(jnp.bfloat16)
    )
    value_low = value_grad.astype(jnp.bfloat16)
    q_term = lax.dot_general(normed, query_low, ROWS_DIMS, preferred_element_type=jnp.float32)
    k_term = lax.dot_general(normed, key_low, ROWS_DIMS, preferred_element_type=jnp.float32)
    v_term = lax.dot_general(normed, value_low, ROWS_DIMS, preferred_element_type=jnp.float32)
    normed_grad = lax.dot_general(query_low, q_full, COLS_DIMS, preferred_element_type=jnp.float32)
    normed_grad = normed_grad + lax.dot_general(
        key_low, k_full, COLS_DIMS, preferred_element_type=jnp.float32
    )
    normed_grad = normed_grad + lax.dot_general(
        value_low, v_full, COLS_DIMS, preferred_element_type=jnp.float32
    )
    ignored, first_pull = jax.vjp(rms_scale, inputs, gain_one)
    input_part, gain_one_term = first_pull(normed_grad)
    input_grad = middle_grad + input_part
    q_grad, k_grad, v_grad, o_grad, gain_attn_grad, gain_moe_grad = (
        lax.psum_scatter(q_term, ("dp", "expert"), scatter_dimension=0, tiled=True),
        lax.psum_scatter(k_term, ("dp", "expert"), scatter_dimension=0, tiled=True),
        lax.psum_scatter(v_term, ("dp", "expert"), scatter_dimension=0, tiled=True),
        lax.psum_scatter(o_term, ("dp", "expert"), scatter_dimension=0, tiled=True),
        lax.psum_scatter(gain_one_term, ("dp", "expert"), scatter_dimension=0, tiled=True),
        lax.psum_scatter(gain_two_term, ("dp", "expert"), scatter_dimension=0, tiled=True),
    )
    given_output, given_input_grad = group_chooser(
        wanted_out,
        (
            jnp.zeros((1, tok_rows, model_width), jnp.float32),
            jnp.zeros((1, tok_rows, model_width), jnp.float32),
        ),
        (
            lax.all_gather(output[None].astype(jnp.bfloat16), "expert", axis=0, tiled=True).astype(
                jnp.float32
            ),
            lax.all_gather(
                input_grad[None].astype(jnp.bfloat16), "expert", axis=0, tiled=True
            ).astype(jnp.float32),
        ),
        jnp.int32(0),
    )
    return (
        given_output,
        given_input_grad,
        q_grad,
        k_grad,
        v_grad,
        o_grad,
        gain_attn_grad,
        gain_moe_grad,
        in_grad,
        down_grad,
    )


SWAP_Y = [(i, i ^ 1) for i in range(8)]
SWAP_CORE = [(j, j ^ 1) for j in range(4)]
SWAP_X = [(j, j ^ 2) for j in range(4)]


def along_z(moves):
    return [(2 * s + y, 2 * d + y) for s, d in moves for y in range(2)]


Z_NEAR = along_z([(0, 1), (1, 0), (2, 3), (3, 2)])
Z_MIDDLE = along_z([(1, 2), (2, 1)])
Z_OUT = along_z([(1, 0), (2, 3)])
Z_IN = along_z([(0, 1), (3, 2)])
SLOT_Z = ((0, 1, 2, 3), (1, 0, 3, 2), (2, 2, 1, 1), (3, 3, 0, 0))


def over_dp(piece, moves):
    return lax.ppermute(piece, "dp", moves)


def over_expert(piece, moves):
    return lax.ppermute(piece, "expert", moves)


def added(first, *others):
    total = first.astype(jnp.float32)
    for other in others:
        total = total + other.astype(jnp.float32)
    return total.astype(jnp.bfloat16)


def z_gather(piece):
    near = over_dp(piece, Z_NEAR)
    middle = over_dp(piece, Z_MIDDLE)
    far = over_dp(near, Z_MIDDLE)
    third = middle + over_dp(middle, Z_OUT)
    fourth = far + over_dp(far, Z_OUT)
    return [piece, near, third, fourth]


def z_scatter(own, near, third, fourth):
    fourth = added(fourth, over_dp(fourth, Z_IN))
    third = added(third, over_dp(third, Z_IN))
    near = added(near, over_dp(fourth, Z_MIDDLE))
    return (
        own.astype(jnp.float32)
        + over_dp(near, Z_NEAR).astype(jnp.float32)
        + over_dp(third, Z_MIDDLE).astype(jnp.float32)
    )


def dp_gather(piece):
    parts = []
    for slot in z_gather(piece):
        parts += [slot, over_dp(slot, SWAP_Y)]
    return jnp.concatenate(parts, axis=0)


def dp_scatter(total):
    rows = total.shape[0] // 8
    slots = []
    for s in range(4):
        here = total[2 * s * rows : (2 * s + 1) * rows]
        there = total[(2 * s + 1) * rows : (2 * s + 2) * rows]
        slots.append(added(here, over_dp(there, SWAP_Y)))
    return z_scatter(*slots)


def all_gather_rows(piece):
    half = piece.shape[0] // 2
    parts = []
    for slot in z_gather(piece):
        top = jnp.concatenate([slot[:half], over_dp(slot[:half], SWAP_Y)], axis=0)
        low = jnp.concatenate([slot[half:], over_expert(slot[half:], SWAP_X)], axis=0)
        parts += [top, over_expert(top, SWAP_X), low, over_dp(low, SWAP_Y)]
    here = jnp.concatenate(parts, axis=0)
    return jnp.concatenate([here, over_expert(here, SWAP_CORE)], axis=0)


def scatter_rows(total):
    rows = total.shape[0] // 32
    half = rows // 2
    here, there = total[: 16 * rows], total[16 * rows :]
    slots = []
    for s in range(4):
        block = slice(4 * s * rows, 4 * (s + 1) * rows)
        both_cores = added(here[block], over_expert(there[block], SWAP_CORE))
        top = added(both_cores[:rows], over_expert(both_cores[rows : 2 * rows], SWAP_X))
        low = added(both_cores[2 * rows : 3 * rows], over_dp(both_cores[3 * rows :], SWAP_Y))
        top = added(top[:half], over_dp(top[half:], SWAP_Y))
        low = added(low[:half], over_expert(low[half:], SWAP_X))
        slots.append(jnp.concatenate([top, low], axis=0))
    return z_scatter(*slots)


def gathered_order(dp_index, ex_index):
    z_own, y_own = dp_index // 2, dp_index % 2
    r = jnp.arange(64, dtype=jnp.int32)
    core, slot, half, outer, inner = r // 32, r // 8 % 4, r // 4 % 2, r // 2 % 2, r % 2
    flip_y = jnp.where(half == 0, inner, outer)
    flip_x = jnp.where(half == 0, outer, inner)
    slot_z = jnp.take(jnp.asarray(SLOT_Z, jnp.int32)[:, z_own], slot)
    return 2 * slot_z + (y_own ^ flip_y), ex_index ^ (2 * flip_x + core), half


def take_kernel(index_ref, *refs, at_once):
    count = len(refs) // (at_once + 1)
    for p in range(count):
        target = refs[count * at_once + p]
        rows = target.shape[0] // at_once
        for k in range(at_once):
            target[k * rows : (k + 1) * rows, :] = refs[p * at_once + k][...]


def take_blocks(index, array, parts, block):
    at_once = 8
    steps = index.shape[1] // at_once

    def source(row, column, k):
        return lambda i, idx: (idx[row, at_once * i + k], column)

    return pl.pallas_call(
        functools.partial(take_kernel, at_once=at_once),
        out_shape=[
            jax.ShapeDtypeStruct((index.shape[1] * block, width), array.dtype)
            for row, column, width in parts
        ],
        grid_spec=pltpu.PrefetchScalarGridSpec(
            num_scalar_prefetch=1,
            grid=(steps,),
            in_specs=[
                pl.BlockSpec((block, width), source(row, column, k))
                for row, column, width in parts
                for k in range(at_once)
            ],
            out_specs=[
                pl.BlockSpec((at_once * block, width), lambda i, idx: (i, 0))
                for row, column, width in parts
            ],
        ),
        name="take_blocks",
    )(index, *([array] * (at_once * len(parts))))


def attend_masks(row_ids, col_ids, begin, rows):
    seq_rows = row_ids[pl.ds(begin, rows), 0:1]
    place_rows = row_ids[pl.ds(begin, rows), 1:2]
    return (seq_rows == col_ids[0:1, :]) & (col_ids[1:2, :] <= place_rows)


def attend_kernel(q_ref, k_ref, v_ref, row_ids, col_ids, o_ref, top_ref, total_ref, *, heads, rows):
    for kv in range(k_ref.shape[1] // HD):
        keys = k_ref[:, kv * HD : (kv + 1) * HD]
        vals = v_ref[:, kv * HD : (kv + 1) * HD]

        def step(i, carry):
            begin = pl.multiple_of(i * rows, rows)
            allowed = attend_masks(row_ids, col_ids, begin, rows)
            outs, tops, totals = [], [], []
            for h in range(heads):
                at = (kv * heads + h) * HD
                scores = SCORE_SCALE * lax.dot_general(
                    q_ref[pl.ds(begin, rows), at : at + HD],
                    keys,
                    COLS_DIMS,
                    preferred_element_type=jnp.float32,
                )
                scores = jnp.where(allowed, scores, NEGATIVE)
                top = jnp.max(scores, axis=-1, keepdims=True)
                weights = jnp.exp(scores - top)
                total = jnp.sum(weights, axis=-1, keepdims=True)
                chances = (weights / total).astype(jnp.bfloat16)
                outs.append(jnp.dot(chances, vals, preferred_element_type=jnp.float32))
                tops.append(top)
                totals.append(total)
            begin_at = kv * heads
            o_ref[pl.ds(begin, rows), begin_at * HD : (begin_at + heads) * HD] = jnp.concatenate(
                outs, axis=1
            ).astype(jnp.bfloat16)
            top_ref[pl.ds(begin, rows), begin_at : begin_at + heads] = jnp.concatenate(tops, axis=1)
            total_ref[pl.ds(begin, rows), begin_at : begin_at + heads] = jnp.concatenate(
                totals, axis=1
            )
            return carry

        lax.fori_loop(0, q_ref.shape[0] // rows, step, 0)


def attend(queries, keys, vals, row_ids, col_ids):
    rows = queries.shape[0]
    heads = queries.shape[1] // HD
    return pl.pallas_call(
        functools.partial(attend_kernel, heads=H // KVH, rows=min(256, rows)),
        out_shape=[
            jax.ShapeDtypeStruct(queries.shape, jnp.bfloat16),
            jax.ShapeDtypeStruct((rows, heads), jnp.float32),
            jax.ShapeDtypeStruct((rows, heads), jnp.float32),
        ],
        name="attend",
    )(queries, keys, vals, row_ids, col_ids)


def attend_back_kernel(
    q_ref, k_ref, v_ref, g_ref, top_ref, total_ref, row_ids, col_ids, dq_ref, dk_ref, dv_ref, *, heads, rows
):
    dk_ref[...] = jnp.zeros_like(dk_ref)
    dv_ref[...] = jnp.zeros_like(dv_ref)
    for kv in range(k_ref.shape[1] // HD):
        cols = slice(kv * HD, (kv + 1) * HD)
        keys = k_ref[:, cols]
        vals = v_ref[:, cols]

        def step(i, carry):
            begin = pl.multiple_of(i * rows, rows)
            allowed = attend_masks(row_ids, col_ids, begin, rows)
            pulled = []
            key_grad = jnp.zeros((k_ref.shape[0], HD), jnp.float32)
            value_grad = jnp.zeros((k_ref.shape[0], HD), jnp.float32)
            for h in range(heads):
                head = kv * heads + h
                query = q_ref[pl.ds(begin, rows), head * HD : (head + 1) * HD]
                grad = g_ref[pl.ds(begin, rows), head * HD : (head + 1) * HD]
                scores = SCORE_SCALE * lax.dot_general(
                    query, keys, COLS_DIMS, preferred_element_type=jnp.float32
                )
                scores = jnp.where(allowed, scores, NEGATIVE)
                weights = jnp.exp(scores - top_ref[pl.ds(begin, rows), head : head + 1])
                chances = weights / total_ref[pl.ds(begin, rows), head : head + 1]
                prob_grad = lax.dot_general(
                    grad, vals, COLS_DIMS, preferred_element_type=jnp.float32
                )
                delta = jnp.sum(chances * prob_grad, axis=-1, keepdims=True)
                score_grad = (chances * (prob_grad - delta)).astype(jnp.bfloat16)
                pulled.append(
                    SCORE_SCALE * jnp.dot(score_grad, keys, preferred_element_type=jnp.float32)
                )
                key_grad += lax.dot_general(
                    score_grad, query, ROWS_DIMS, preferred_element_type=jnp.float32
                )
                value_grad += lax.dot_general(
                    chances.astype(jnp.bfloat16), grad, ROWS_DIMS, preferred_element_type=jnp.float32
                )
            dq_ref[pl.ds(begin, rows), kv * heads * HD : (kv + 1) * heads * HD] = jnp.concatenate(
                pulled, axis=1
            )
            dk_ref[:, cols] += SCORE_SCALE * key_grad
            dv_ref[:, cols] += value_grad
            return carry

        lax.fori_loop(0, q_ref.shape[0] // rows, step, 0)


def attend_back(queries, keys, vals, grads_in, top, total, row_ids, col_ids):
    rows = queries.shape[0]
    return pl.pallas_call(
        functools.partial(attend_back_kernel, heads=H // KVH, rows=min(256, rows)),
        out_shape=[
            jax.ShapeDtypeStruct(queries.shape, jnp.float32),
            jax.ShapeDtypeStruct(keys.shape, jnp.float32),
            jax.ShapeDtypeStruct(keys.shape, jnp.float32),
        ],
        name="attend_back",
    )(queries, keys, vals, grads_in, top, total, row_ids, col_ids)


def after(value, *earlier):
    return lax.optimization_barrier((value, *earlier))[0]


def rounded(values):
    return lax.reduce_precision(values, 8, 7)


def rope_parts(seq_lengths, places):
    seq_ends = jnp.cumsum(seq_lengths)
    seq_starts = seq_ends - seq_lengths
    member = (places[:, None] >= seq_starts[None, :]) & (places[:, None] < seq_ends[None, :])
    offsets = jnp.sum(jnp.where(member, places[:, None] - seq_starts[None, :], 0), axis=-1)
    frequency = THETA ** (-jnp.arange(HD // 2, dtype=jnp.float32) * 2.0 / HD)
    angles = offsets.astype(jnp.float32)[:, None] * frequency[None, :]
    angles = jnp.concatenate([angles, angles], axis=-1)[:, None, :]
    seq_ids = locate(places, seq_ends)
    return seq_ids, jnp.cos(angles), jnp.sin(angles)


def per_device(
    tokens,
    cotangent,
    lengths,
    deal,
    routes,
    gates,
    q_weight,
    k_weight,
    v_weight,
    o_weight,
    gain_attn,
    gain_moe,
    in_weight,
    down_weight,
):
    n_dp = lax.axis_size("dp")
    n_ex = lax.axis_size("expert")
    tok_rows = tokens.shape[1]
    model = tokens.shape[2]
    group_rows = tok_rows * n_dp
    kv_here = KVH // n_dp
    heads_per = H // KVH
    q_cols = kv_here * heads_per * HD
    kv_cols = kv_here * HD
    own_experts = in_weight.shape[1]
    ff_here = FF // n_dp
    ff_cols = own_experts * ff_here
    w_rows = q_weight.shape[0]
    ex_index = lax.axis_index("expert")
    group_ids = jnp.arange(deal.shape[0], dtype=jnp.int32)
    dealt_of = jnp.argmax((deal[None, :] == group_ids[:, None]).astype(jnp.int32), axis=1)
    own_dealt = jnp.sum(jnp.where(deal == ex_index, group_ids, 0))

    group_tokens = dp_gather(tokens[0])
    z_own, y_own = lax.axis_index("dp") // 2, lax.axis_index("dp") % 2
    slot_dp = 2 * jnp.asarray(SLOT_Z, jnp.int32)[:, z_own]
    block_dp = jnp.stack([slot_dp + y_own, slot_dp + 1 - y_own], axis=1).reshape(-1)
    places = (block_dp[:, None] * tok_rows + jnp.arange(tok_rows, dtype=jnp.int32)).reshape(-1)

    def by_owner(weight):
        return weight.astype(jnp.bfloat16).reshape(w_rows, n_dp, weight.shape[1] // n_dp)

    length_parts = jnp.stack([lengths[0] // 128, lengths[0] % 128]).reshape(-1).astype(jnp.bfloat16)
    n_len = length_parts.shape[0]
    extra = jnp.concatenate(
        [
            gain_attn.astype(jnp.bfloat16)[:, None],
            gain_moe.astype(jnp.bfloat16)[:, None],
            jnp.broadcast_to(length_parts[None, :], (w_rows, n_len)),
            jnp.zeros((w_rows, 126 - n_len), jnp.bfloat16),
        ],
        axis=1,
    )
    attn_out = jnp.concatenate(
        [
            by_owner(q_weight),
            by_owner(k_weight),
            by_owner(v_weight),
            by_owner(o_weight),
            jnp.broadcast_to(extra[:, None, :], (w_rows, n_dp, 128)),
        ],
        axis=2,
    ).transpose(1, 0, 2)
    attn_in = lax.all_to_all(attn_out, "dp", split_axis=0, concat_axis=0, tiled=True)
    attn_all = lax.all_gather(attn_in, "expert", axis=0)
    attn_w = attn_all.transpose(1, 0, 2, 3).reshape(model, -1)
    qkv_cols = q_cols + 2 * kv_cols
    qkv_w = attn_w[:, :qkv_cols]
    o_w = attn_w[:, qkv_cols : qkv_cols + q_cols]
    side = attn_w[:, qkv_cols + q_cols :]
    gain_one = side[:, 0].astype(jnp.float32)
    gain_two = side[:, 1].astype(jnp.float32)
    own_parts = lax.dynamic_index_in_dim(attn_all, own_dealt, 0, keepdims=False)[
        0, 0, qkv_cols + q_cols + 2 : qkv_cols + q_cols + 2 + n_len
    ].astype(jnp.int32)
    seq_lengths = own_parts[: n_len // 2] * 128 + own_parts[n_len // 2 :]

    gate_rows = gates[0]
    gate_top = rounded(gate_rows)
    gate_mid = rounded(gate_rows - gate_top)
    gate_low = gate_rows - gate_top - gate_mid
    meta = jnp.concatenate(
        [
            routes[0].astype(jnp.float32),
            gate_top,
            gate_mid,
            gate_low,
            jnp.zeros((tok_rows, 128 - 4 * TOPK), jnp.float32),
        ],
        axis=1,
    ).astype(jnp.bfloat16)
    both = ("dp", "expert")
    cot_out = after(jnp.concatenate([cotangent[0], meta], axis=1), group_tokens)
    cot_all = lax.all_gather(cot_out, both, axis=0, tiled=True)
    from_dp, from_ex, from_half = gathered_order(lax.axis_index("dp"), ex_index)
    rows_from = (from_dp * n_ex + from_ex) * 2 + from_half
    meta_from = (from_dp * n_ex + jnp.take(dealt_of, from_ex)) * 2 + from_half
    cot_rows, meta_all = take_blocks(
        jnp.stack([rows_from, meta_from]),
        cot_all,
        [(0, 0, model), (1, model // 128, 128)],
        tok_rows // 2,
    )
    rows_to = jnp.zeros_like(rows_from).at[rows_from].set(jnp.arange(64, dtype=jnp.int32))

    in_out = (
        in_weight.astype(jnp.bfloat16)
        .reshape(in_weight.shape[0], own_experts, 2, n_dp, ff_here)
        .transpose(3, 0, 2, 1, 4)
        .reshape(n_dp, in_weight.shape[0], 2 * ff_cols)
    )
    in_w = lax.all_to_all(after(in_out, group_tokens), "dp", split_axis=0, concat_axis=0, tiled=True).reshape(
        model, 2 * ff_cols
    )
    down_w = down_weight.astype(jnp.bfloat16).transpose(1, 0, 2).reshape(ff_cols, model)

    seq_ids, cosine, sine_table = rope_parts(seq_lengths, places)
    group_inputs = group_tokens.astype(jnp.float32)
    first_scale = lax.rsqrt(jnp.mean(group_inputs * group_inputs, axis=-1, keepdims=True) + EPSILON)
    normed = (group_inputs * first_scale * gain_one).astype(jnp.bfloat16)
    qkv = jnp.dot(normed, qkv_w, preferred_element_type=jnp.float32)
    queries = (
        rotate(qkv[:, :q_cols].reshape(group_rows, kv_here * heads_per, HD), cosine, sine_table)
        .astype(jnp.bfloat16)
        .reshape(group_rows, q_cols)
    )
    keys = (
        rotate(
            qkv[:, q_cols : q_cols + kv_cols].reshape(group_rows, kv_here, HD), cosine, sine_table
        )
        .astype(jnp.bfloat16)
        .reshape(group_rows, kv_cols)
    )
    vals = qkv[:, q_cols + kv_cols :].astype(jnp.bfloat16)
    row_ids = jnp.stack([seq_ids, places], axis=1)
    col_ids = jnp.stack([seq_ids, places], axis=0)
    mixed_low, run_top, run_total = attend(queries, keys, vals, row_ids, col_ids)
    branch_part = lax.dot_general(mixed_low, o_w, COLS_DIMS, preferred_element_type=jnp.float32)
    branch = dp_scatter(branch_part.astype(jnp.bfloat16))
    inputs = tokens[0].astype(jnp.float32)
    middle = inputs + RESIDUAL * branch
    second_scale = lax.rsqrt(jnp.mean(middle * middle, axis=-1, keepdims=True) + EPSILON)
    sent_rows = (middle * second_scale * gain_two).astype(jnp.bfloat16)
    sent_all = all_gather_rows(after(sent_rows, in_w))

    meta_all = meta_all.astype(jnp.float32)
    route_all = meta_all[:, :TOPK]
    gate_all = (
        meta_all[:, TOPK : 2 * TOPK]
        + meta_all[:, 2 * TOPK : 3 * TOPK]
        + meta_all[:, 3 * TOPK : 4 * TOPK]
    )
    expert_ids = (ex_index * own_experts + jnp.arange(own_experts, dtype=jnp.int32)).astype(
        jnp.float32
    )
    dense_gates = jnp.sum(
        jnp.where(route_all[:, :, None] == expert_ids[None, None, :], gate_all[:, :, None], 0.0),
        axis=1,
    )
    gate_cols = jnp.repeat(dense_gates, ff_here, axis=1)

    gate_up = jnp.dot(sent_all, in_w, preferred_element_type=jnp.float32)
    gate_part = gate_up[:, :ff_cols]
    up_part = gate_up[:, ff_cols:]
    sigma = jax.nn.sigmoid(gate_part)
    silu = gate_part * sigma
    hidden = (silu * up_part).astype(jnp.bfloat16).astype(jnp.float32)
    weighted = (gate_cols * hidden).astype(jnp.bfloat16)
    pulled = lax.dot_general(cot_rows, down_w, COLS_DIMS, preferred_element_type=jnp.float32)
    hidden_grad = RESIDUAL * gate_cols * pulled
    gate_grad = hidden_grad * up_part * (sigma * (1.0 + gate_part * (1.0 - sigma)))
    up_grad = hidden_grad * silu
    gate_up_grad = jnp.concatenate([gate_grad, up_grad], axis=1).astype(jnp.bfloat16)
    sent_grad_part = lax.dot_general(
        gate_up_grad, in_w, COLS_DIMS, preferred_element_type=jnp.float32
    ).astype(jnp.bfloat16)
    sent_grad = scatter_rows(sent_grad_part)
    (weighted_out,) = take_blocks(
        rows_to[None], weighted, [(0, 0, ff_cols)], tok_rows // 2
    )
    out_part = jnp.dot(weighted_out, down_w, preferred_element_type=jnp.float32).astype(jnp.bfloat16)
    in_term = lax.dot_general(sent_all, gate_up_grad, ROWS_DIMS, preferred_element_type=jnp.float32)
    in_back = lax.all_to_all(
        in_term.astype(jnp.bfloat16).reshape(n_dp, in_weight.shape[0], 2 * ff_cols),
        "dp",
        split_axis=0,
        concat_axis=0,
        tiled=True,
    )
    in_grad = (
        in_back.reshape(n_dp, in_weight.shape[0], 2, own_experts, ff_here)
        .transpose(1, 3, 2, 0, 4)
        .reshape(in_weight.shape)
        .astype(jnp.float32)
    )
    down_term = RESIDUAL * lax.dot_general(
        weighted, cot_rows, ROWS_DIMS, preferred_element_type=jnp.float32
    )
    down_grad = down_term.reshape(own_experts, ff_here, model).transpose(1, 0, 2)

    upstream = cotangent[0].astype(jnp.float32)
    scaled_grad = sent_grad * gain_two
    middle_grad = (
        upstream
        + second_scale * scaled_grad
        - middle
        * second_scale**3
        * jnp.mean(scaled_grad * middle, axis=-1, keepdims=True)
    )
    gain_two_part = jnp.sum(sent_grad * middle * second_scale, axis=0)
    branch_grad = (RESIDUAL * middle_grad).astype(jnp.bfloat16)
    branch_grad_all = dp_gather(branch_grad)
    expert_sum = lax.psum_scatter(out_part, both, scatter_dimension=0, tiled=True).astype(
        jnp.float32
    )
    output = middle + RESIDUAL * expert_sum

    o_term = lax.dot_general(
        branch_grad_all, mixed_low, ROWS_DIMS, preferred_element_type=jnp.float32
    )
    grad_heads = jnp.dot(branch_grad_all, o_w, preferred_element_type=jnp.float32).astype(
        jnp.bfloat16
    )
    query_grad, key_grad, value_grad = attend_back(
        queries, keys, vals, grad_heads, run_top, run_total, row_ids, col_ids
    )
    query_low = turn_back(
        query_grad.reshape(group_rows, kv_here * heads_per, HD), cosine, sine_table
    ).reshape(group_rows, q_cols)
    key_low = turn_back(
        key_grad.reshape(group_rows, kv_here, HD), cosine, sine_table
    ).reshape(group_rows, kv_cols)
    qkv_grad = jnp.concatenate(
        [query_low, key_low, value_grad], axis=1
    ).astype(jnp.bfloat16)
    normed_grad_part = lax.dot_general(
        qkv_grad, qkv_w, COLS_DIMS, preferred_element_type=jnp.float32
    )
    gain_one_part = jnp.sum(normed_grad_part * group_inputs * first_scale, axis=0)
    normed_grad = dp_scatter(normed_grad_part.astype(jnp.bfloat16))
    qkv_term = lax.dot_general(normed, qkv_grad, ROWS_DIMS, preferred_element_type=jnp.float32)
    grads = jnp.concatenate(
        [
            qkv_term,
            o_term,
            gain_one_part[:, None],
            gain_two_part[:, None],
            jnp.zeros((model, 126), jnp.float32),
        ],
        axis=1,
    ).astype(jnp.bfloat16)
    grads = grads.reshape(n_dp, n_ex, w_rows, -1)
    own_g, core_g, x_g, xc_g = [
        lax.dynamic_index_in_dim(grads, ex_index ^ k, 1, keepdims=False) for k in range(n_ex)
    ]
    from_core = over_expert(jnp.stack([core_g, xc_g]), SWAP_CORE)
    grads = added(
        own_g, from_core[0], over_expert(added(x_g, from_core[1]), SWAP_X)
    )
    grads = lax.all_to_all(grads, "dp", split_axis=0, concat_axis=0, tiled=True).astype(jnp.float32)

    def own_rows(begin, width):
        return grads[:, :, begin : begin + width].transpose(1, 0, 2).reshape(w_rows, n_dp * width)

    q_grad = own_rows(0, q_cols)
    k_grad = own_rows(q_cols, kv_cols)
    v_grad = own_rows(q_cols + kv_cols, kv_cols)
    o_grad = own_rows(qkv_cols, q_cols)
    gain_attn_grad = jnp.sum(grads[:, :, qkv_cols + q_cols], axis=0)
    gain_moe_grad = jnp.sum(grads[:, :, qkv_cols + q_cols + 1], axis=0)

    own_scale = lax.rsqrt(jnp.mean(inputs * inputs, axis=-1, keepdims=True) + EPSILON)
    scaled_one = normed_grad * gain_one
    input_grad = (
        middle_grad
        + own_scale * scaled_one
        - inputs * own_scale**3 * jnp.mean(scaled_one * inputs, axis=-1, keepdims=True)
    )
    return (
        output[None],
        input_grad[None],
        q_grad,
        k_grad,
        v_grad,
        o_grad,
        gain_attn_grad,
        gain_moe_grad,
        in_grad,
        down_grad,
    )


def solution(mesh):
    placed = (
        P("expert", "dp", None),
        P("expert", "dp", None),
        P("expert", None),
        P(),
        P("expert", "dp", None),
        P("expert", "dp", None),
        P(("dp", "expert"), None),
        P(("dp", "expert"), None),
        P(("dp", "expert"), None),
        P(("dp", "expert"), None),
        P(("dp", "expert")),
        P(("dp", "expert")),
        P("dp", "expert", None),
        P("dp", "expert", None),
    )
    n_dp = mesh.shape["dp"]
    split_heads = n_dp == 8 and mesh.shape["expert"] == 4
    return jax.shard_map(
        per_device if split_heads else per_device_wide,
        mesh=mesh,
        in_specs=placed,
        out_specs=(
            P("expert", "dp", None),
            P("expert", "dp", None),
            P(("dp", "expert"), None),
            P(("dp", "expert"), None),
            P(("dp", "expert"), None),
            P(("dp", "expert"), None),
            P(("dp", "expert")),
            P(("dp", "expert")),
            P("dp", "expert", None),
            P("dp", "expert", None),
        ),
        check_vma=False,
    )
```

```python
import functools

import jax
import jax.numpy as jnp
from jax import lax
from jax.experimental import pallas as pl
from jax.experimental.pallas import tpu as pltpu
from jax.sharding import PartitionSpec as P


H = 24
KVH = 8
HD = 64
E = 40
FF = 512
TOPK = 8
CAP = 40


EPSILON = 1e-06
RESIDUAL = 0.22
SCORE_SCALE = 0.015625
THETA = 10000.0
NEGATIVE = -1e30
ROWS_DIMS = (((0,), (0,)), ((), ()))
COLS_DIMS = (((1,), (1,)), ((), ()))


def rms_scale(values, gain):
    return values * lax.rsqrt(jnp.mean(values * values, axis=-1, keepdims=True) + EPSILON) * gain


def rotate(values, cosine, sine_table):
    half_width = values.shape[-1] // 2
    turned = jnp.concatenate([-values[..., half_width:], values[..., :half_width]], axis=-1)
    return values * cosine + turned * sine_table


def turn_back(grads_in, cosine, sine_table):
    half_width = grads_in.shape[-1] // 2
    scaled = grads_in * sine_table
    return grads_in * cosine + jnp.concatenate(
        [scaled[..., half_width:], -scaled[..., :half_width]], axis=-1
    )


def silu_product(gate_in, up_in):
    return jax.nn.silu(gate_in) * up_in


def locate(where_at, seq_ends):
    return jnp.sum((where_at[:, None] >= seq_ends[None, :]).astype(jnp.int32), axis=-1)


def cut_block(source, begin_at, block_rows, heads):
    piece = lax.dynamic_slice_in_dim(source, begin_at, block_rows, 0)
    return piece.reshape(block_rows, heads, source.shape[1] // heads)


def group_chooser(wanted, carried, pieces, start):
    piece_rows = pieces[0].shape[0]
    inside = (wanted >= start) & (wanted < start + piece_rows)
    offset_at = jnp.clip(wanted, 0, piece_rows - 1)
    return tuple(
        (
            jnp.where(inside, lax.dynamic_slice_in_dim(member_piece, offset_at, 1, 0), member_carry)
            for member_piece, member_carry in zip(pieces, carried)
        )
    )


def per_device_wide(
    tokens,
    cotangent,
    lengths,
    deal,
    routes,
    gates,
    q_weight,
    k_weight,
    v_weight,
    o_weight,
    gain_attn,
    gain_moe,
    in_weight,
    down_weight,
):
    tok_rows = tokens.shape[1]
    model_width = tokens.shape[2]
    group_rows = tok_rows * lax.axis_size("dp")
    block_rows = min(512, group_rows)
    heads_per = H // KVH
    owner_index = lax.axis_index("expert")
    group_ids = jnp.arange(deal.shape[0], dtype=jnp.int32)
    wanted_in = jnp.sum(jnp.where(group_ids == owner_index, deal, 0))
    wanted_out = jnp.sum(jnp.where(deal == owner_index, group_ids, 0))
    dealt_tokens, dealt_cotangent = group_chooser(
        wanted_in,
        (jnp.zeros_like(tokens), jnp.zeros_like(cotangent)),
        (
            lax.all_gather(tokens, "expert", axis=0, tiled=True),
            lax.all_gather(cotangent, "expert", axis=0, tiled=True),
        ),
        jnp.int32(0),
    )
    inputs = dealt_tokens[0].astype(jnp.float32)
    q_full, k_full, v_full, o_full, gain_one, gain_two = (
        lax.all_gather(q_weight.astype(jnp.bfloat16), ("dp", "expert"), axis=0, tiled=True),
        lax.all_gather(k_weight.astype(jnp.bfloat16), ("dp", "expert"), axis=0, tiled=True),
        lax.all_gather(v_weight.astype(jnp.bfloat16), ("dp", "expert"), axis=0, tiled=True),
        lax.all_gather(o_weight.astype(jnp.bfloat16), ("dp", "expert"), axis=0, tiled=True),
        lax.all_gather(gain_attn.astype(jnp.bfloat16), ("dp", "expert"), axis=0, tiled=True),
        lax.all_gather(gain_moe.astype(jnp.bfloat16), ("dp", "expert"), axis=0, tiled=True),
    )
    gain_one = gain_one.astype(jnp.float32)
    gain_two = gain_two.astype(jnp.float32)
    seq_lengths = lengths[0]
    seq_ends = jnp.cumsum(seq_lengths)
    seq_starts = seq_ends - seq_lengths
    first_place = lax.axis_index("dp") * tok_rows
    places = first_place + jnp.arange(tok_rows, dtype=jnp.int32)
    member = (places[:, None] >= seq_starts[None, :]) & (places[:, None] < seq_ends[None, :])
    offsets = jnp.sum(jnp.where(member, places[:, None] - seq_starts[None, :], 0), axis=-1)
    frequency = THETA ** (-jnp.arange(HD // 2, dtype=jnp.float32) * 2.0 / HD)
    angles = offsets.astype(jnp.float32)[:, None] * frequency[None, :]
    angles = jnp.concatenate([angles, angles], axis=-1)[:, None, :]
    cosine = jnp.cos(angles)
    sine_table = jnp.sin(angles)
    query_seq = locate(places, seq_ends)
    seq_floor = jnp.sum(jnp.where(member[0], seq_starts, 0))
    low_block = seq_floor // block_rows
    high_block = (first_place + tok_rows - 1) // block_rows + 1
    normed = rms_scale(inputs, gain_one).astype(jnp.bfloat16)
    query_pre = jnp.dot(normed, q_full, preferred_element_type=jnp.float32).reshape(tok_rows, H, HD)
    key_pre = jnp.dot(normed, k_full, preferred_element_type=jnp.float32).reshape(tok_rows, KVH, HD)
    value_rows = jnp.dot(normed, v_full, preferred_element_type=jnp.float32).astype(jnp.bfloat16)
    queries = (
        rotate(query_pre, cosine, sine_table)
        .astype(jnp.bfloat16)
        .reshape(tok_rows, KVH, heads_per, HD)
    )
    key_rows = rotate(key_pre, cosine, sine_table).astype(jnp.bfloat16).reshape(tok_rows, KVH * HD)
    all_keys, all_values = (
        lax.all_gather(key_rows, "dp", axis=0, tiled=True),
        lax.all_gather(value_rows, "dp", axis=0, tiled=True),
    )

    def scores_for(block_id, key_block):
        begin_at = block_id * block_rows
        key_places = begin_at + jnp.arange(block_rows, dtype=jnp.int32)
        allowed = (query_seq[:, None] == locate(key_places, seq_ends)[None, :]) & (
            key_places[None, :] <= places[:, None]
        )
        raw_scores = SCORE_SCALE * jnp.einsum(
            "tkgd,skd->kgts", queries, key_block, preferred_element_type=jnp.float32
        )
        return (raw_scores, allowed)

    def stats_step(block_id, carried):
        run_top, run_total = carried
        key_block = cut_block(all_keys, block_id * block_rows, block_rows, KVH)
        raw_scores, allowed = scores_for(block_id, key_block)
        new_top = jnp.maximum(run_top, jnp.max(jnp.where(allowed, raw_scores, NEGATIVE), axis=-1))
        weights_now = jnp.where(allowed, jnp.exp(raw_scores - new_top[..., None]), 0.0)
        run_total = run_total * jnp.exp(run_top - new_top) + jnp.sum(weights_now, axis=-1)
        return (new_top, run_total)

    top_init = jnp.full((KVH, heads_per, tok_rows), NEGATIVE, jnp.float32)
    total_init = jnp.zeros((KVH, heads_per, tok_rows), jnp.float32)
    run_top, run_total = lax.fori_loop(low_block, high_block, stats_step, (top_init, total_init))
    log_total = run_top + jnp.log(run_total)

    def attn_probs(block_id, key_block):
        raw_scores, allowed = scores_for(block_id, key_block)
        return jnp.where(allowed, jnp.exp(raw_scores - log_total[..., None]), 0.0)

    def value_step(block_id, running):
        key_block = cut_block(all_keys, block_id * block_rows, block_rows, KVH)
        value_block = cut_block(all_values, block_id * block_rows, block_rows, KVH)
        chances = attn_probs(block_id, key_block).astype(jnp.bfloat16)
        return running + jnp.einsum(
            "kgts,skd->tkgd", chances, value_block, preferred_element_type=jnp.float32
        )

    mixed_init = jnp.zeros((tok_rows, KVH, heads_per, HD), jnp.float32)
    mixed_rows = lax.fori_loop(low_block, high_block, value_step, mixed_init).reshape(
        tok_rows, H * HD
    )
    mixed_low = mixed_rows.astype(jnp.bfloat16)
    branch = lax.dot_general(mixed_low, o_full, COLS_DIMS, preferred_element_type=jnp.float32)
    middle = inputs + RESIDUAL * branch
    sent_rows = rms_scale(middle, gain_two).astype(jnp.bfloat16)
    route_ids = routes[0].reshape(tok_rows * TOPK)
    matches = (route_ids[:, None] == jnp.arange(E, dtype=jnp.int32)[None, :]).astype(jnp.int32)
    slot_rank = jnp.sum(matches * jnp.cumsum(matches, axis=0), axis=-1) - 1
    slot_index = route_ids * CAP + slot_rank
    copies = jnp.repeat(sent_rows, TOPK, axis=0)
    outgoing = (
        jnp.zeros((E * CAP, model_width), jnp.bfloat16)
        .at[slot_index]
        .set(copies)
        .reshape(E, CAP, model_width)
    )
    arrived = lax.all_to_all(outgoing, "expert", split_axis=0, concat_axis=1, tiled=True)
    w_in, w_down = (
        lax.all_gather(in_weight.astype(jnp.bfloat16), "dp", axis=0, tiled=True),
        lax.all_gather(down_weight.astype(jnp.bfloat16), "dp", axis=0, tiled=True),
    )
    gate_up = jnp.einsum("erd,def->erf", arrived, w_in, preferred_element_type=jnp.float32)
    gate_part = gate_up[..., :FF]
    up_part = gate_up[..., FF:]
    hidden = silu_product(gate_part, up_part).astype(jnp.bfloat16)
    produced = jnp.einsum(
        "erf,fed->erd", hidden, w_down, preferred_element_type=jnp.float32
    ).astype(jnp.bfloat16)
    returned = lax.all_to_all(produced, "expert", split_axis=1, concat_axis=0, tiled=True).reshape(
        E * CAP, model_width
    )
    route_gates = gates[0].reshape(tok_rows * TOPK)
    picked = returned[slot_index].astype(jnp.float32) * route_gates[:, None]
    expert_sum = jnp.sum(picked.reshape(tok_rows, TOPK, model_width), axis=1)
    output = middle + RESIDUAL * expert_sum
    upstream = dealt_cotangent[0].astype(jnp.float32)
    spread = (RESIDUAL * route_gates[:, None] * jnp.repeat(upstream, TOPK, axis=0)).astype(
        jnp.bfloat16
    )
    back_out = (
        jnp.zeros((E * CAP, model_width), jnp.bfloat16)
        .at[slot_index]
        .set(spread)
        .reshape(E, CAP, model_width)
    )
    back_in = lax.all_to_all(back_out, "expert", split_axis=0, concat_axis=1, tiled=True)
    hidden_grad = jnp.einsum("erd,fed->erf", back_in, w_down, preferred_element_type=jnp.float32)
    down_term = jnp.einsum("erf,erd->fed", hidden, back_in, preferred_element_type=jnp.float32)
    ignored, silu_pull = jax.vjp(silu_product, gate_part, up_part)
    gate_grad, up_grad = silu_pull(hidden_grad)
    gate_up_grad = jnp.concatenate([gate_grad, up_grad], axis=-1).astype(jnp.bfloat16)
    in_term = jnp.einsum("erd,erf->def", arrived, gate_up_grad, preferred_element_type=jnp.float32)
    arrived_grad = jnp.einsum(
        "erf,def->erd", gate_up_grad, w_in, preferred_element_type=jnp.float32
    ).astype(jnp.bfloat16)
    sent_back = lax.all_to_all(
        arrived_grad, "expert", split_axis=1, concat_axis=0, tiled=True
    ).reshape(E * CAP, model_width)
    sent_grad = jnp.sum(
        sent_back[slot_index].astype(jnp.float32).reshape(tok_rows, TOPK, model_width), axis=1
    )
    in_grad, down_grad = (
        lax.psum_scatter(
            in_term.astype(jnp.bfloat16), "dp", scatter_dimension=0, tiled=True
        ).astype(jnp.float32),
        lax.psum_scatter(
            down_term.astype(jnp.bfloat16), "dp", scatter_dimension=0, tiled=True
        ).astype(jnp.float32),
    )
    ignored, second_pull = jax.vjp(rms_scale, middle, gain_two)
    middle_part, gain_two_term = second_pull(sent_grad)
    middle_grad = upstream + middle_part
    branch_grad = (RESIDUAL * middle_grad).astype(jnp.bfloat16)
    o_term = lax.dot_general(branch_grad, mixed_low, ROWS_DIMS, preferred_element_type=jnp.float32)
    grad_heads = jnp.dot(branch_grad, o_full, preferred_element_type=jnp.float32).astype(
        jnp.bfloat16
    )
    grad_heads = grad_heads.reshape(tok_rows, KVH, heads_per, HD)

    def delta_step(block_id, running):
        key_block = cut_block(all_keys, block_id * block_rows, block_rows, KVH)
        value_block = cut_block(all_values, block_id * block_rows, block_rows, KVH)
        chances = attn_probs(block_id, key_block)
        prob_grad = jnp.einsum(
            "tkgd,skd->kgts", grad_heads, value_block, preferred_element_type=jnp.float32
        )
        return running + jnp.sum(chances * prob_grad, axis=-1)

    row_delta = lax.fori_loop(
        low_block, high_block, delta_step, jnp.zeros((KVH, heads_per, tok_rows), jnp.float32)
    )

    def grad_step(block_id, carried):
        query_grad, key_buffer, value_buffer = carried
        begin_at = block_id * block_rows
        key_block = cut_block(all_keys, begin_at, block_rows, KVH)
        value_block = cut_block(all_values, begin_at, block_rows, KVH)
        chances = attn_probs(block_id, key_block)
        prob_grad = jnp.einsum(
            "tkgd,skd->kgts", grad_heads, value_block, preferred_element_type=jnp.float32
        )
        score_grad = (chances * (prob_grad - row_delta[..., None])).astype(jnp.bfloat16)
        query_grad = query_grad + SCORE_SCALE * jnp.einsum(
            "kgts,skd->tkgd", score_grad, key_block, preferred_element_type=jnp.float32
        )
        key_part = SCORE_SCALE * jnp.einsum(
            "kgts,tkgd->skd", score_grad, queries, preferred_element_type=jnp.float32
        )
        value_part = jnp.einsum(
            "kgts,tkgd->skd",
            chances.astype(jnp.bfloat16),
            grad_heads,
            preferred_element_type=jnp.float32,
        )
        key_buffer = lax.dynamic_update_slice_in_dim(
            key_buffer, key_part.reshape(block_rows, KVH * HD), begin_at, 0
        )
        value_buffer = lax.dynamic_update_slice_in_dim(
            value_buffer, value_part.reshape(block_rows, KVH * HD), begin_at, 0
        )
        return (query_grad, key_buffer, value_buffer)

    grad_init = (
        jnp.zeros((tok_rows, KVH, heads_per, HD), jnp.float32),
        jnp.zeros((group_rows, KVH * HD), jnp.float32),
        jnp.zeros((group_rows, KVH * HD), jnp.float32),
    )
    query_grad, key_buffer, value_buffer = lax.fori_loop(
        low_block, high_block, grad_step, grad_init
    )
    key_grad, value_grad = (
        lax.psum_scatter(
            key_buffer.astype(jnp.bfloat16), "dp", scatter_dimension=0, tiled=True
        ).astype(jnp.float32),
        lax.psum_scatter(
            value_buffer.astype(jnp.bfloat16), "dp", scatter_dimension=0, tiled=True
        ).astype(jnp.float32),
    )
    query_low = (
        turn_back(query_grad.reshape(tok_rows, H, HD), cosine, sine_table)
        .reshape(tok_rows, H * HD)
        .astype(jnp.bfloat16)
    )
    key_low = (
        turn_back(key_grad.reshape(tok_rows, KVH, HD), cosine, sine_table)
        .reshape(tok_rows, KVH * HD)
        .astype(jnp.bfloat16)
    )
    value_low = value_grad.astype(jnp.bfloat16)
    q_term = lax.dot_general(normed, query_low, ROWS_DIMS, preferred_element_type=jnp.float32)
    k_term = lax.dot_general(normed, key_low, ROWS_DIMS, preferred_element_type=jnp.float32)
    v_term = lax.dot_general(normed, value_low, ROWS_DIMS, preferred_element_type=jnp.float32)
    normed_grad = lax.dot_general(query_low, q_full, COLS_DIMS, preferred_element_type=jnp.float32)
    normed_grad = normed_grad + lax.dot_general(
        key_low, k_full, COLS_DIMS, preferred_element_type=jnp.float32
    )
    normed_grad = normed_grad + lax.dot_general(
        value_low, v_full, COLS_DIMS, preferred_element_type=jnp.float32
    )
    ignored, first_pull = jax.vjp(rms_scale, inputs, gain_one)
    input_part, gain_one_term = first_pull(normed_grad)
    input_grad = middle_grad + input_part
    q_grad, k_grad, v_grad, o_grad, gain_attn_grad, gain_moe_grad = (
        lax.psum_scatter(q_term, ("dp", "expert"), scatter_dimension=0, tiled=True),
        lax.psum_scatter(k_term, ("dp", "expert"), scatter_dimension=0, tiled=True),
        lax.psum_scatter(v_term, ("dp", "expert"), scatter_dimension=0, tiled=True),
        lax.psum_scatter(o_term, ("dp", "expert"), scatter_dimension=0, tiled=True),
        lax.psum_scatter(gain_one_term, ("dp", "expert"), scatter_dimension=0, tiled=True),
        lax.psum_scatter(gain_two_term, ("dp", "expert"), scatter_dimension=0, tiled=True),
    )
    given_output, given_input_grad = group_chooser(
        wanted_out,
        (
            jnp.zeros((1, tok_rows, model_width), jnp.float32),
            jnp.zeros((1, tok_rows, model_width), jnp.float32),
        ),
        (
            lax.all_gather(output[None].astype(jnp.bfloat16), "expert", axis=0, tiled=True).astype(
                jnp.float32
            ),
            lax.all_gather(
                input_grad[None].astype(jnp.bfloat16), "expert", axis=0, tiled=True
            ).astype(jnp.float32),
        ),
        jnp.int32(0),
    )
    return (
        given_output,
        given_input_grad,
        q_grad,
        k_grad,
        v_grad,
        o_grad,
        gain_attn_grad,
        gain_moe_grad,
        in_grad,
        down_grad,
    )


SWAP_Y = [(i, i ^ 1) for i in range(8)]
SWAP_CORE = [(j, j ^ 1) for j in range(4)]
SWAP_X = [(j, j ^ 2) for j in range(4)]


def along_z(moves):
    return [(2 * s + y, 2 * d + y) for s, d in moves for y in range(2)]


Z_NEAR = along_z([(0, 1), (1, 0), (2, 3), (3, 2)])
Z_MIDDLE = along_z([(1, 2), (2, 1)])
Z_OUT = along_z([(1, 0), (2, 3)])
Z_IN = along_z([(0, 1), (3, 2)])
SLOT_Z = ((0, 1, 2, 3), (1, 0, 3, 2), (2, 2, 1, 1), (3, 3, 0, 0))


def over_dp(piece, moves):
    return lax.ppermute(piece, "dp", moves)


def over_expert(piece, moves):
    return lax.ppermute(piece, "expert", moves)


def added(first, *others):
    total = first.astype(jnp.float32)
    for other in others:
        total = total + other.astype(jnp.float32)
    return total.astype(jnp.bfloat16)


def halves(array):
    half = array.shape[0] // 2
    return array[:half], array[half:]


def joined(*arrays):
    return jnp.concatenate(arrays, axis=0)


def one_round(outs, ins, cover=None):
    if cover is None:
        return lax.optimization_barrier(outs), None
    return lax.optimization_barrier((outs, cover(lambda x: after(x, *ins))))


def swap_y(value):
    return over_dp(value, SWAP_Y)


def swap_x(value):
    return over_expert(value, SWAP_X)


def swap_core(value):
    return over_expert(value, SWAP_CORE)


def dp_gather(piece, covers=(None, None, None, None)):
    (near, middle, y0), work1 = one_round(
        (over_dp(piece, Z_NEAR), over_dp(piece, Z_MIDDLE), swap_y(piece)), (piece,), covers[0]
    )
    (far, out1, y1), work2 = one_round(
        (over_dp(near, Z_MIDDLE), over_dp(middle, Z_OUT), swap_y(near)), (near, middle), covers[1]
    )
    third = middle + out1
    (out2, y2), work3 = one_round((over_dp(far, Z_OUT), swap_y(third)), (far, third), covers[2])
    fourth = far + out2
    y3, work4 = one_round(swap_y(fourth), (fourth,), covers[3])
    return joined(piece, y0, near, y1, third, y2, fourth, y3), (work1, work2, work3, work4)


class DpScatter:
    def __init__(self, total):
        blocks = jnp.split(total, 8, axis=0)
        self.own, self.sent = blocks[0::2], blocks[1::2]
        self.round = 0

    def step(self, tie=lambda v: v):
        self.round += 1
        if self.round == 1:
            self.z = swap_y(tie(self.sent[3]))
        elif self.round == 2:
            self.fourth = added(self.own[3], self.z)
            self.z = over_dp(tie(self.fourth), Z_IN), swap_y(self.sent[2])
        elif self.round == 3:
            fourth = added(self.fourth, self.z[0])
            self.third = added(self.own[2], self.z[1])
            self.z = (
                over_dp(tie(fourth), Z_MIDDLE),
                over_dp(self.third, Z_IN),
                swap_y(self.sent[1]),
            )
        else:
            third = added(self.third, self.z[1])
            near = added(self.own[1], self.z[2], self.z[0])
            self.z = (
                over_dp(tie(near), Z_NEAR),
                over_dp(third, Z_MIDDLE),
                swap_y(self.sent[0]),
            )
        return self.z

    def keep(self, values):
        self.z = values

    def total(self):
        total = self.own[0].astype(jnp.float32)
        for value in self.z:
            total = total + value.astype(jnp.float32)
        return total


def gather_beside_sum(piece, project, mix):
    (near, middle), projected = one_round(
        (over_dp(piece, Z_NEAR), over_dp(piece, Z_MIDDLE)), (piece,), project
    )
    (far, out1, y0), (mixed, part) = one_round(
        (over_dp(near, Z_MIDDLE), over_dp(middle, Z_OUT), swap_y(piece)),
        (near, middle),
        lambda tie: mix(tie, projected),
    )
    third = middle + out1
    pair0 = joined(piece, y0)
    total = DpScatter(part)
    (out2, y1, x0, sums), _ = one_round(
        (over_dp(far, Z_OUT), swap_y(near), swap_x(pair0), total.step()), (far, pair0)
    )
    total.keep(sums)
    fourth = far + out2
    pair1 = joined(near, y1)
    (y2, x1, sums), _ = one_round((swap_y(third), swap_x(pair1), total.step()), (third, pair1))
    total.keep(sums)
    pair2 = joined(third, y2)
    (y3, x2, sums), _ = one_round((swap_y(fourth), swap_x(pair2), total.step()), (fourth, pair2))
    total.keep(sums)
    pair3 = joined(fourth, y3)
    (x3, sums), _ = one_round((swap_x(pair3), total.step()), (pair3,))
    total.keep(sums)
    here = joined(pair0, x0, pair1, x1, pair2, x2, pair3, x3)
    return joined(here, swap_core(here)), total.total(), (projected, mixed)


def gather_slots(piece, covers):
    y, x, core = swap_y, swap_x, swap_core
    t0, l0 = halves(piece)
    outs = over_dp(piece, Z_NEAR), over_dp(piece, Z_MIDDLE), y(t0), x(l0)
    (near, middle, yt0, xl0), _ = one_round(outs, (piece,))
    t1, l1 = halves(near)
    top0, low0 = joined(t0, yt0), joined(l0, xl0)
    outs = over_dp(near, Z_MIDDLE), over_dp(middle, Z_OUT), x(top0), y(low0), y(t1), x(l1)
    (far, out1, xt0, yl0, yt1, xl1), work2 = one_round(outs, (top0, low0), covers[0])
    third = middle + out1
    t2, l2 = halves(third)
    top1, low1, here0 = joined(t1, yt1), joined(l1, xl1), joined(top0, xt0, low0, yl0)
    outs = over_dp(far, Z_OUT), x(top1), y(low1), y(t2), x(l2), core(here0)
    (out2, xt1, yl1, yt2, xl2, core0), work3 = one_round(outs, (top1, low1), covers[1])
    fourth = far + out2
    t3, l3 = halves(fourth)
    slot0 = joined(here0, core0)
    top2, low2, here1 = joined(t2, yt2), joined(l2, xl2), joined(top1, xt1, low1, yl1)
    outs = x(top2), y(low2), y(t3), x(l3), core(here1)
    (xt2, yl2, yt3, xl3, core1), work4 = one_round(
        outs, (top2, low2), lambda tie: covers[2](tie, slot0)
    )
    slot1 = joined(here1, core1)
    top3, low3, here2 = joined(t3, yt3), joined(l3, xl3), joined(top2, xt2, low2, yl2)
    outs = x(top3), y(low3), core(here2)
    (xt3, yl3, core2), work5 = one_round(outs, (top3, low3), lambda tie: covers[2](tie, slot1))
    slot2 = joined(here2, core2)
    here3 = joined(top3, xt3, low3, yl3)
    core3, work6 = one_round(core(here3), (here3,), lambda tie: covers[2](tie, slot2))
    slot3 = joined(here3, core3)
    return [slot0, slot1, slot2, slot3], [work4, work5, work6], (work2, work3)


def scatter_slots(totals, covers):
    y, x, core = swap_y, swap_x, swap_core

    def big(here):
        top, low = halves(here)
        (ta, tb), (la, lb) = halves(top), halves(low)
        return (ta, la), (x(tb), y(lb))

    def small(top, low):
        (ta, tb), (la, lb) = halves(top), halves(low)
        return (ta, la), (y(tb), x(lb))

    works = []

    def run(outs, ins, cover):
        outs, work = one_round(outs, ins, cover and (lambda tie: cover(tie, works)))
        works.append(work)
        return outs

    (m0, o0), (m1, o1), (m2, o2), (m3, o3) = [halves(t) for t in totals]
    c3 = run(core(o3), (o3,), covers[0])
    h3 = added(m3, c3)
    k3, b3 = big(h3)
    (b3, c2) = run((b3, core(o2)), (h3,), covers[1])
    p3 = [added(k, v) for k, v in zip(k3, b3)]
    h2 = added(m2, c2)
    k2, b2 = big(h2)
    s3, a3 = small(*p3)
    (a3, b2, c1, c0) = run((a3, b2, core(o1), core(o0)), (h2, *p3), covers[2])
    fourth = joined(*[added(k, v) for k, v in zip(s3, a3)])
    p2 = [added(k, v) for k, v in zip(k2, b2)]
    h1, h0 = added(m1, c1), added(m0, c0)
    k1, b1 = big(h1)
    s2, a2 = small(*p2)
    (z3, a2, b1) = run(
        (over_dp(fourth, Z_IN), a2, b1), (fourth, h1, *p2), covers[3]
    )
    fourth = added(fourth, z3)
    third = joined(*[added(k, v) for k, v in zip(s2, a2)])
    p1 = [added(k, v) for k, v in zip(k1, b1)]
    k0, b0 = big(h0)
    s1, a1 = small(*p1)
    (z3, z2, a1, b0) = run(
        (over_dp(fourth, Z_MIDDLE), over_dp(third, Z_IN), a1, b0), (fourth, third, *p1), covers[4]
    )
    third = added(third, z2)
    near = added(joined(*[added(k, v) for k, v in zip(s1, a1)]), z3)
    p0 = [added(k, v) for k, v in zip(k0, b0)]
    s0, a0 = small(*p0)
    (z1, z2, a0) = run(
        (over_dp(near, Z_NEAR), over_dp(third, Z_MIDDLE), a0), (near, third, *p0), covers[5]
    )
    own = joined(*[added(k, v) for k, v in zip(s0, a0)])
    total = own.astype(jnp.float32) + z1.astype(jnp.float32) + z2.astype(jnp.float32)
    return total, works


def far_order(ex_index, dealt_of):
    r = jnp.arange(64, dtype=jnp.int32)
    slot, core, half, outer, inner = r // 16, r // 8 % 2, r // 4 % 2, r // 2 % 2, r % 2
    flip_y = jnp.where(half == 0, inner, outer)
    flip_x = jnp.where(half == 0, outer, inner)

    def place(flip):
        return ((flip % 2 * 4 + slot) * 4 + flip // 2 * 2 + flip_y) * 2 + half

    flip = 2 * flip_x + core
    return place(flip), place(jnp.take(dealt_of, ex_index ^ flip) ^ ex_index)


def take_kernel(index_ref, *refs, at_once):
    count = len(refs) // (at_once + 1)
    for p in range(count):
        target = refs[count * at_once + p]
        rows = target.shape[0] // at_once
        for k in range(at_once):
            target[k * rows : (k + 1) * rows, :] = refs[p * at_once + k][...]


def take_blocks(index, array, parts, block):
    at_once = 8
    steps = index.shape[1] // at_once

    def source(row, column, k):
        return lambda i, idx: (idx[row, at_once * i + k], column)

    return pl.pallas_call(
        functools.partial(take_kernel, at_once=at_once),
        out_shape=[
            jax.ShapeDtypeStruct((index.shape[1] * block, width), array.dtype)
            for row, column, width in parts
        ],
        grid_spec=pltpu.PrefetchScalarGridSpec(
            num_scalar_prefetch=1,
            grid=(steps,),
            in_specs=[
                pl.BlockSpec((block, width), source(row, column, k))
                for row, column, width in parts
                for k in range(at_once)
            ],
            out_specs=[
                pl.BlockSpec((at_once * block, width), lambda i, idx: (i, 0))
                for row, column, width in parts
            ],
        ),
        name="take_blocks",
    )(index, *([array] * (at_once * len(parts))))


def attend_masks(row_ids, col_ids, begin, rows):
    seq_rows = row_ids[pl.ds(begin, rows), 0:1]
    place_rows = row_ids[pl.ds(begin, rows), 1:2]
    return (seq_rows == col_ids[0:1, :]) & (col_ids[1:2, :] <= place_rows)


def attend_kernel(q_ref, k_ref, v_ref, row_ids, col_ids, o_ref, top_ref, total_ref, *, heads, rows):
    for kv in range(k_ref.shape[1] // HD):
        keys = k_ref[:, kv * HD : (kv + 1) * HD]
        vals = v_ref[:, kv * HD : (kv + 1) * HD]

        def step(i, carry):
            begin = pl.multiple_of(i * rows, rows)
            allowed = attend_masks(row_ids, col_ids, begin, rows)
            outs, tops, totals = [], [], []
            for h in range(heads):
                at = (kv * heads + h) * HD
                scores = SCORE_SCALE * lax.dot_general(
                    q_ref[pl.ds(begin, rows), at : at + HD],
                    keys,
                    COLS_DIMS,
                    preferred_element_type=jnp.float32,
                )
                scores = jnp.where(allowed, scores, NEGATIVE)
                top = jnp.max(scores, axis=-1, keepdims=True)
                weights = jnp.exp(scores - top)
                total = jnp.sum(weights, axis=-1, keepdims=True)
                chances = (weights / total).astype(jnp.bfloat16)
                outs.append(jnp.dot(chances, vals, preferred_element_type=jnp.float32))
                tops.append(top)
                totals.append(total)
            begin_at = kv * heads
            o_ref[pl.ds(begin, rows), begin_at * HD : (begin_at + heads) * HD] = jnp.concatenate(
                outs, axis=1
            ).astype(jnp.bfloat16)
            top_ref[pl.ds(begin, rows), begin_at : begin_at + heads] = jnp.concatenate(tops, axis=1)
            total_ref[pl.ds(begin, rows), begin_at : begin_at + heads] = jnp.concatenate(
                totals, axis=1
            )
            return carry

        lax.fori_loop(0, q_ref.shape[0] // rows, step, 0)


def attend(queries, keys, vals, row_ids, col_ids):
    rows = queries.shape[0]
    heads = queries.shape[1] // HD
    return pl.pallas_call(
        functools.partial(attend_kernel, heads=H // KVH, rows=min(256, rows)),
        out_shape=[
            jax.ShapeDtypeStruct(queries.shape, jnp.bfloat16),
            jax.ShapeDtypeStruct((rows, heads), jnp.float32),
            jax.ShapeDtypeStruct((rows, heads), jnp.float32),
        ],
        name="attend",
    )(queries, keys, vals, row_ids, col_ids)


def attend_back_kernel(
    q_ref, k_ref, v_ref, g_ref, top_ref, total_ref, row_ids, col_ids, dq_ref, dk_ref, dv_ref, *, heads, rows
):
    dk_ref[...] = jnp.zeros_like(dk_ref)
    dv_ref[...] = jnp.zeros_like(dv_ref)
    for kv in range(k_ref.shape[1] // HD):
        cols = slice(kv * HD, (kv + 1) * HD)
        keys = k_ref[:, cols]
        vals = v_ref[:, cols]

        def step(i, carry):
            begin = pl.multiple_of(i * rows, rows)
            allowed = attend_masks(row_ids, col_ids, begin, rows)
            pulled = []
            key_grad = jnp.zeros((k_ref.shape[0], HD), jnp.float32)
            value_grad = jnp.zeros((k_ref.shape[0], HD), jnp.float32)
            for h in range(heads):
                head = kv * heads + h
                query = q_ref[pl.ds(begin, rows), head * HD : (head + 1) * HD]
                grad = g_ref[pl.ds(begin, rows), head * HD : (head + 1) * HD]
                scores = SCORE_SCALE * lax.dot_general(
                    query, keys, COLS_DIMS, preferred_element_type=jnp.float32
                )
                scores = jnp.where(allowed, scores, NEGATIVE)
                weights = jnp.exp(scores - top_ref[pl.ds(begin, rows), head : head + 1])
                chances = weights / total_ref[pl.ds(begin, rows), head : head + 1]
                prob_grad = lax.dot_general(
                    grad, vals, COLS_DIMS, preferred_element_type=jnp.float32
                )
                delta = jnp.sum(chances * prob_grad, axis=-1, keepdims=True)
                score_grad = (chances * (prob_grad - delta)).astype(jnp.bfloat16)
                pulled.append(
                    SCORE_SCALE * jnp.dot(score_grad, keys, preferred_element_type=jnp.float32)
                )
                key_grad += lax.dot_general(
                    score_grad, query, ROWS_DIMS, preferred_element_type=jnp.float32
                )
                value_grad += lax.dot_general(
                    chances.astype(jnp.bfloat16), grad, ROWS_DIMS, preferred_element_type=jnp.float32
                )
            dq_ref[pl.ds(begin, rows), kv * heads * HD : (kv + 1) * heads * HD] = jnp.concatenate(
                pulled, axis=1
            )
            dk_ref[:, cols] += SCORE_SCALE * key_grad
            dv_ref[:, cols] += value_grad
            return carry

        lax.fori_loop(0, q_ref.shape[0] // rows, step, 0)


def attend_back(queries, keys, vals, grads_in, top, total, row_ids, col_ids):
    rows = queries.shape[0]
    return pl.pallas_call(
        functools.partial(attend_back_kernel, heads=H // KVH, rows=min(256, rows)),
        out_shape=[
            jax.ShapeDtypeStruct(queries.shape, jnp.float32),
            jax.ShapeDtypeStruct(keys.shape, jnp.float32),
            jax.ShapeDtypeStruct(keys.shape, jnp.float32),
        ],
        name="attend_back",
    )(queries, keys, vals, grads_in, top, total, row_ids, col_ids)


def after(value, *earlier):
    return lax.optimization_barrier((value, *earlier))[0]


def rounded(values):
    return lax.reduce_precision(values, 8, 7)


def rope_parts(seq_lengths, places):
    seq_ends = jnp.cumsum(seq_lengths)
    seq_starts = seq_ends - seq_lengths
    member = (places[:, None] >= seq_starts[None, :]) & (places[:, None] < seq_ends[None, :])
    offsets = jnp.sum(jnp.where(member, places[:, None] - seq_starts[None, :], 0), axis=-1)
    frequency = THETA ** (-jnp.arange(HD // 2, dtype=jnp.float32) * 2.0 / HD)
    angles = offsets.astype(jnp.float32)[:, None] * frequency[None, :]
    angles = jnp.concatenate([angles, angles], axis=-1)[:, None, :]
    seq_ids = locate(places, seq_ends)
    return seq_ids, jnp.cos(angles), jnp.sin(angles)


def per_device(
    tokens,
    cotangent,
    lengths,
    deal,
    routes,
    gates,
    q_weight,
    k_weight,
    v_weight,
    o_weight,
    gain_attn,
    gain_moe,
    in_weight,
    down_weight,
):
    n_dp = lax.axis_size("dp")
    n_ex = lax.axis_size("expert")
    tok_rows = tokens.shape[1]
    model = tokens.shape[2]
    group_rows = tok_rows * n_dp
    kv_here = KVH // n_dp
    heads_per = H // KVH
    q_cols = kv_here * heads_per * HD
    kv_cols = kv_here * HD
    own_experts = in_weight.shape[1]
    ff_here = FF // n_dp
    ff_cols = own_experts * ff_here
    w_rows = q_weight.shape[0]
    ex_index = lax.axis_index("expert")
    group_ids = jnp.arange(deal.shape[0], dtype=jnp.int32)
    dealt_of = jnp.argmax((deal[None, :] == group_ids[:, None]).astype(jnp.int32), axis=1)
    own_dealt = jnp.sum(jnp.where(deal == ex_index, group_ids, 0))

    def by_owner(weight):
        return weight.astype(jnp.bfloat16).reshape(w_rows, n_dp, weight.shape[1] // n_dp)

    length_parts = jnp.stack([lengths[0] // 128, lengths[0] % 128]).reshape(-1).astype(jnp.bfloat16)
    n_len = length_parts.shape[0]
    extra = jnp.concatenate(
        [
            gain_attn.astype(jnp.bfloat16)[:, None],
            gain_moe.astype(jnp.bfloat16)[:, None],
            jnp.broadcast_to(length_parts[None, :], (w_rows, n_len)),
            jnp.zeros((w_rows, 126 - n_len), jnp.bfloat16),
        ],
        axis=1,
    )

    def pack_in(tie):
        return (
            tie(in_weight)
            .astype(jnp.bfloat16)
            .reshape(in_weight.shape[0], own_experts, 2, n_dp, ff_here)
            .transpose(3, 0, 2, 1, 4)
            .reshape(n_dp, in_weight.shape[0], 2 * ff_cols)
        )

    attn_out = jnp.concatenate(
        [
            by_owner(q_weight),
            by_owner(k_weight),
            by_owner(v_weight),
            by_owner(o_weight),
            jnp.broadcast_to(extra[:, None, :], (w_rows, n_dp, 128)),
        ],
        axis=2,
    ).transpose(1, 0, 2)
    attn_in = lax.all_to_all(attn_out, "dp", split_axis=0, concat_axis=0, tiled=True)

    group_tokens, (_, in_out, _, _) = dp_gather(tokens[0], (None, pack_in, None, None))
    attn_two = jnp.stack([attn_in, swap_core(attn_in)])
    attn_four = joined(attn_two, swap_x(attn_two))
    in_w = lax.all_to_all(
        after(in_out, group_tokens, attn_in), "dp", split_axis=0, concat_axis=0, tiled=True
    ).reshape(model, 2 * ff_cols)
    z_own, y_own = lax.axis_index("dp") // 2, lax.axis_index("dp") % 2
    slot_dp = 2 * jnp.asarray(SLOT_Z, jnp.int32)[:, z_own]
    block_dp = jnp.stack([slot_dp + y_own, slot_dp + 1 - y_own], axis=1).reshape(-1)
    places = (block_dp[:, None] * tok_rows + jnp.arange(tok_rows, dtype=jnp.int32)).reshape(-1)


    def of_expert(index):
        return lax.dynamic_index_in_dim(attn_four, index ^ ex_index, 0, keepdims=False)

    attn_all = jnp.stack([of_expert(e) for e in range(n_ex)])
    attn_w = attn_all.transpose(1, 0, 2, 3).reshape(model, -1)
    qkv_cols = q_cols + 2 * kv_cols
    qkv_w = attn_w[:, :qkv_cols]
    o_w = attn_w[:, qkv_cols : qkv_cols + q_cols]
    side = attn_w[:, qkv_cols + q_cols :]
    gain_one = side[:, 0].astype(jnp.float32)
    gain_two = side[:, 1].astype(jnp.float32)
    own_parts = of_expert(own_dealt)[
        0, 0, qkv_cols + q_cols + 2 : qkv_cols + q_cols + 2 + n_len
    ].astype(jnp.int32)
    seq_lengths = own_parts[: n_len // 2] * 128 + own_parts[n_len // 2 :]

    down_w = down_weight.astype(jnp.bfloat16).transpose(1, 0, 2).reshape(ff_cols, model)

    every = jnp.arange(E, dtype=jnp.int32)[None, :]
    dense = sum(
        jnp.where(routes[0][:, k : k + 1] == every, gates[0][:, k : k + 1], 0.0)
        for k in range(TOPK)
    )
    dense_top = rounded(dense)
    dense_mid = rounded(dense - dense_top)
    meta = jnp.concatenate(
        [
            dense_top,
            dense_mid,
            dense - dense_top - dense_mid,
            jnp.zeros((tok_rows, 128 - 3 * E), jnp.float32),
        ],
        axis=1,
    ).astype(jnp.bfloat16)

    seq_ids, cosine, sine_table = rope_parts(seq_lengths, places)
    group_inputs = group_tokens.astype(jnp.float32)
    first_scale = lax.rsqrt(jnp.mean(group_inputs * group_inputs, axis=-1, keepdims=True) + EPSILON)
    row_ids = jnp.stack([seq_ids, places], axis=1)
    col_ids = jnp.stack([seq_ids, places], axis=0)

    def project(tie):
        normed = (tie(group_inputs) * first_scale * gain_one).astype(jnp.bfloat16)
        qkv = jnp.dot(normed, qkv_w, preferred_element_type=jnp.float32)
        queries = (
            rotate(qkv[:, :q_cols].reshape(group_rows, kv_here * heads_per, HD), cosine, sine_table)
            .astype(jnp.bfloat16)
            .reshape(group_rows, q_cols)
        )
        keys = (
            rotate(
                qkv[:, q_cols : q_cols + kv_cols].reshape(group_rows, kv_here, HD),
                cosine,
                sine_table,
            )
            .astype(jnp.bfloat16)
            .reshape(group_rows, kv_cols)
        )
        vals = qkv[:, q_cols + kv_cols :].astype(jnp.bfloat16)
        return normed, queries, keys, vals

    def mix(tie, projected):
        _, queries, keys, vals = projected
        mixed = attend(tie(queries), keys, vals, row_ids, col_ids)
        part = lax.dot_general(mixed[0], o_w, COLS_DIMS, preferred_element_type=jnp.float32)
        return mixed, part.astype(jnp.bfloat16)

    cot_out = after(jnp.concatenate([cotangent[0], meta], axis=1), group_tokens)
    cot_all, branch, (projected, mixed) = gather_beside_sum(cot_out, project, mix)
    normed, queries, keys, vals = projected
    mixed_low, run_top, run_total = mixed
    rows_from, meta_from = far_order(ex_index, dealt_of)
    cot_rows, meta_all = take_blocks(
        jnp.stack([rows_from, meta_from]),
        cot_all,
        [(0, 0, model), (1, model // 128, 128)],
        tok_rows // 2,
    )
    inputs = tokens[0].astype(jnp.float32)
    middle = inputs + RESIDUAL * branch
    second_scale = lax.rsqrt(jnp.mean(middle * middle, axis=-1, keepdims=True) + EPSILON)
    sent_rows = (middle * second_scale * gain_two).astype(jnp.bfloat16)
    sent_rows = after(sent_rows, in_w, cot_rows)
    slot_rows = 8 * tok_rows

    def spread_gates(tie):
        column = jnp.arange(128, dtype=jnp.int32)[:, None]
        owner = ex_index * own_experts + jnp.arange(ff_cols, dtype=jnp.int32)[None, :] // ff_here
        spread = ((column % E == owner) & (column < 3 * E)).astype(jnp.bfloat16)
        return jnp.dot(tie(meta_all), spread, preferred_element_type=jnp.float32)

    def pull(tie):
        return lax.dot_general(
            tie(cot_rows), down_w, COLS_DIMS, preferred_element_type=jnp.float32
        )

    def up(tie, sent):
        return jnp.dot(tie(sent), in_w, preferred_element_type=jnp.float32)

    def down(gate_up, gates_here, pulled_here):
        gate_part = gate_up[:, :ff_cols]
        up_part = gate_up[:, ff_cols:]
        sigma = jax.nn.sigmoid(gate_part)
        silu = gate_part * sigma
        hidden = (silu * up_part).astype(jnp.bfloat16).astype(jnp.float32)
        weighted_here = (gates_here * hidden).astype(jnp.bfloat16)
        hidden_grad = RESIDUAL * gates_here * pulled_here
        gate_grad = hidden_grad * up_part * (sigma * (1.0 + gate_part * (1.0 - sigma)))
        up_grad = hidden_grad * silu
        grads_here = jnp.concatenate([gate_grad, up_grad], axis=1).astype(jnp.bfloat16)
        return weighted_here, grads_here

    def back(grads_here):
        return lax.dot_general(
            grads_here, in_w, COLS_DIMS, preferred_element_type=jnp.float32
        ).astype(jnp.bfloat16)

    sent_slots, ups, (gate_cols, pulled) = gather_slots(sent_rows, (spread_gates, pull, up))
    ups = ups + [up(lambda v: v, sent_slots[3])]
    weighted_slots, grad_slots = zip(
        *[
            down(
                ups[n],
                gate_cols[n * slot_rows : (n + 1) * slot_rows],
                pulled[n * slot_rows : (n + 1) * slot_rows],
            )
            for n in range(4)
        ]
    )
    sent_grad_slots = [back(g) for g in grad_slots]

    def out_rows(tie, works):
        return [
            jnp.dot(tie(part), down_w, preferred_element_type=jnp.float32).astype(jnp.bfloat16)
            for part in weighted_slots
        ]

    def in_terms(numbers, so_far):
        def work(tie, works):
            total = so_far()
            for n in numbers:
                term = lax.dot_general(
                    tie(sent_slots[n]), grad_slots[n], ROWS_DIMS, preferred_element_type=jnp.float32
                )
                total = term if total is None else total + term
            return total

        return work

    def down_terms(tie):
        return RESIDUAL * lax.dot_general(
            tie(joined(*weighted_slots)), cot_rows, ROWS_DIMS, preferred_element_type=jnp.float32
        )

    sent_grad, (_, out_slots, in_low, in_mid, in_high, _) = scatter_slots(
        sent_grad_slots,
        (
            None,
            out_rows,
            in_terms((0, 1), lambda: None),
            in_terms((2,), lambda: None),
            in_terms((3,), lambda: None),
            None,
        ),
    )
    in_term = (in_low + in_mid + in_high).astype(jnp.bfloat16)

    upstream = cotangent[0].astype(jnp.float32)
    scaled_grad = sent_grad * gain_two
    middle_grad = (
        upstream
        + second_scale * scaled_grad
        - middle
        * second_scale**3
        * jnp.mean(scaled_grad * middle, axis=-1, keepdims=True)
    )
    gain_two_part = jnp.sum(sent_grad * middle * second_scale, axis=0)
    branch_grad = (RESIDUAL * middle_grad).astype(jnp.bfloat16)

    def gather_one(tie, works):
        piece = tie(branch_grad)
        return over_dp(piece, Z_NEAR), over_dp(piece, Z_MIDDLE), swap_y(piece)

    def gather_two(tie, works):
        near, middle, _ = works[0]
        moved = over_dp(tie(near), Z_MIDDLE), over_dp(middle, Z_OUT), swap_y(near)
        return moved, down_terms(tie)

    def gather_three(tie, works):
        third = works[0][1] + works[1][0][1]
        return over_dp(tie(works[1][0][0]), Z_OUT), swap_y(third), third

    def gather_four(tie, works):
        fourth = works[1][0][0] + works[2][0]
        return swap_y(tie(fourth)), fourth

    def pull_attention(tie, works):
        (near, _, y0), ((_, _, y1), _), (_, y2, third), (y3, fourth) = works[:4]
        grad_all = joined(tie(branch_grad), y0, near, y1, third, y2, fourth, y3)
        o_term = lax.dot_general(grad_all, mixed_low, ROWS_DIMS, preferred_element_type=jnp.float32)
        grad_heads = jnp.dot(grad_all, o_w, preferred_element_type=jnp.float32).astype(
            jnp.bfloat16
        )
        return o_term, attend_back(
            queries, keys, vals, grad_heads, run_top, run_total, row_ids, col_ids
        )

    def pull_projections(tie, works):
        o_term, (query_grad, key_grad, value_grad) = works[4]
        query_low = turn_back(
            tie(query_grad).reshape(group_rows, kv_here * heads_per, HD), cosine, sine_table
        ).reshape(group_rows, q_cols)
        key_low = turn_back(
            key_grad.reshape(group_rows, kv_here, HD), cosine, sine_table
        ).reshape(group_rows, kv_cols)
        qkv_grad = jnp.concatenate([query_low, key_low, value_grad], axis=1).astype(jnp.bfloat16)
        normed_grad_part = lax.dot_general(
            qkv_grad, qkv_w, COLS_DIMS, preferred_element_type=jnp.float32
        )
        gain_one_part = jnp.sum(normed_grad_part * group_inputs * first_scale, axis=0)
        qkv_term = lax.dot_general(normed, qkv_grad, ROWS_DIMS, preferred_element_type=jnp.float32)
        grads = jnp.concatenate(
            [
                qkv_term,
                o_term,
                gain_one_part[:, None],
                gain_two_part[:, None],
                jnp.zeros((model, 126), jnp.float32),
            ],
            axis=1,
        ).astype(jnp.bfloat16)
        return normed_grad_part.astype(jnp.bfloat16), grads

    expert_sum, works = scatter_slots(
        [after(out_slots[n], sent_grad) for n in range(4)],
        (gather_one, gather_two, gather_three, gather_four, pull_attention, pull_projections),
    )
    in_back = lax.all_to_all(
        after(in_term, works[3]).reshape(n_dp, in_weight.shape[0], 2 * ff_cols),
        "dp",
        split_axis=0,
        concat_axis=0,
        tiled=True,
    )
    output = middle + RESIDUAL * expert_sum
    down_grad = works[1][1].reshape(own_experts, ff_here, model).transpose(1, 0, 2)
    normed_grad_part, grads = works[5]
    total = DpScatter(normed_grad_part)
    grads = grads.reshape(n_dp, n_ex, w_rows, -1)
    own_g, core_g, x_g, xc_g = [
        lax.dynamic_index_in_dim(grads, ex_index ^ k, 1, keepdims=False) for k in range(n_ex)
    ]
    core_pair = jnp.stack([core_g, xc_g])
    (sums, from_core), _ = one_round((total.step(), swap_core(core_pair)), (core_pair,))
    total.keep(sums)
    x_g = added(x_g, from_core[1])
    (sums, from_x), _ = one_round((total.step(), swap_x(x_g)), (x_g,))
    total.keep(sums)
    grads = lax.all_to_all(
        after(added(own_g, from_core[0], from_x), in_back), "dp", split_axis=0, concat_axis=0, tiled=True
    )
    (sums, grads), _ = one_round((total.step(), grads), ())
    total.keep(sums)
    grads = grads.astype(jnp.float32)
    total.keep(one_round(total.step(), ())[0])
    normed_grad = total.total()
    in_grad = (
        in_back
        .reshape(n_dp, in_weight.shape[0], 2, own_experts, ff_here)
        .transpose(1, 3, 2, 0, 4)
        .reshape(in_weight.shape)
        .astype(jnp.float32)
    )

    def own_rows(begin, width):
        return grads[:, :, begin : begin + width].transpose(1, 0, 2).reshape(w_rows, n_dp * width)

    q_grad = own_rows(0, q_cols)
    k_grad = own_rows(q_cols, kv_cols)
    v_grad = own_rows(q_cols + kv_cols, kv_cols)
    o_grad = own_rows(qkv_cols, q_cols)
    gain_attn_grad = jnp.sum(grads[:, :, qkv_cols + q_cols], axis=0)
    gain_moe_grad = jnp.sum(grads[:, :, qkv_cols + q_cols + 1], axis=0)

    own_scale = lax.rsqrt(jnp.mean(inputs * inputs, axis=-1, keepdims=True) + EPSILON)
    scaled_one = normed_grad * gain_one
    input_grad = (
        middle_grad
        + own_scale * scaled_one
        - inputs * own_scale**3 * jnp.mean(scaled_one * inputs, axis=-1, keepdims=True)
    )
    return (
        output[None],
        input_grad[None],
        q_grad,
        k_grad,
        v_grad,
        o_grad,
        gain_attn_grad,
        gain_moe_grad,
        in_grad,
        down_grad,
    )


def per_layer(*args):
    return per_device(*args)


def solution(mesh):
    placed = (
        P("expert", "dp", None),
        P("expert", "dp", None),
        P("expert", None),
        P(),
        P("expert", "dp", None),
        P("expert", "dp", None),
        P(("dp", "expert"), None),
        P(("dp", "expert"), None),
        P(("dp", "expert"), None),
        P(("dp", "expert"), None),
        P(("dp", "expert")),
        P(("dp", "expert")),
        P("dp", "expert", None),
        P("dp", "expert", None),
    )
    n_dp = mesh.shape["dp"]
    split_heads = n_dp == 8 and mesh.shape["expert"] == 4
    return jax.shard_map(
        per_layer if split_heads else per_device_wide,
        mesh=mesh,
        in_specs=placed,
        out_specs=(
            P("expert", "dp", None),
            P("expert", "dp", None),
            P(("dp", "expert"), None),
            P(("dp", "expert"), None),
            P(("dp", "expert"), None),
            P(("dp", "expert"), None),
            P(("dp", "expert")),
            P(("dp", "expert")),
            P("dp", "expert", None),
            P("dp", "expert", None),
        ),
        check_vma=False,
    )
```

```python
import functools

import jax
import jax.numpy as jnp
from jax import lax
from jax.experimental import pallas as pl
from jax.experimental.pallas import tpu as pltpu
from jax.sharding import PartitionSpec as P


H = 24
KVH = 8
HD = 64
E = 40
FF = 512
TOPK = 8
CAP = 40


EPSILON = 1e-06
RESIDUAL = 0.22
SCORE_SCALE = 0.015625
THETA = 10000.0
NEGATIVE = -1e30
ROWS_DIMS = (((0,), (0,)), ((), ()))
COLS_DIMS = (((1,), (1,)), ((), ()))


def rms_scale(values, gain):
    return values * lax.rsqrt(jnp.mean(values * values, axis=-1, keepdims=True) + EPSILON) * gain


def rotate(values, cosine, sine_table):
    half_width = values.shape[-1] // 2
    turned = jnp.concatenate([-values[..., half_width:], values[..., :half_width]], axis=-1)
    return values * cosine + turned * sine_table


def turn_back(grads_in, cosine, sine_table):
    half_width = grads_in.shape[-1] // 2
    scaled = grads_in * sine_table
    return grads_in * cosine + jnp.concatenate(
        [scaled[..., half_width:], -scaled[..., :half_width]], axis=-1
    )


def silu_product(gate_in, up_in):
    return jax.nn.silu(gate_in) * up_in


def locate(where_at, seq_ends):
    return jnp.sum((where_at[:, None] >= seq_ends[None, :]).astype(jnp.int32), axis=-1)


def cut_block(source, begin_at, block_rows, heads):
    piece = lax.dynamic_slice_in_dim(source, begin_at, block_rows, 0)
    return piece.reshape(block_rows, heads, source.shape[1] // heads)


def group_chooser(wanted, carried, pieces, start):
    piece_rows = pieces[0].shape[0]
    inside = (wanted >= start) & (wanted < start + piece_rows)
    offset_at = jnp.clip(wanted, 0, piece_rows - 1)
    return tuple(
        (
            jnp.where(inside, lax.dynamic_slice_in_dim(member_piece, offset_at, 1, 0), member_carry)
            for member_piece, member_carry in zip(pieces, carried)
        )
    )


def per_device_wide(
    tokens,
    cotangent,
    lengths,
    deal,
    routes,
    gates,
    q_weight,
    k_weight,
    v_weight,
    o_weight,
    gain_attn,
    gain_moe,
    in_weight,
    down_weight,
):
    tok_rows = tokens.shape[1]
    model_width = tokens.shape[2]
    group_rows = tok_rows * lax.axis_size("dp")
    block_rows = min(512, group_rows)
    heads_per = H // KVH
    owner_index = lax.axis_index("expert")
    group_ids = jnp.arange(deal.shape[0], dtype=jnp.int32)
    wanted_in = jnp.sum(jnp.where(group_ids == owner_index, deal, 0))
    wanted_out = jnp.sum(jnp.where(deal == owner_index, group_ids, 0))
    dealt_tokens, dealt_cotangent = group_chooser(
        wanted_in,
        (jnp.zeros_like(tokens), jnp.zeros_like(cotangent)),
        (
            lax.all_gather(tokens, "expert", axis=0, tiled=True),
            lax.all_gather(cotangent, "expert", axis=0, tiled=True),
        ),
        jnp.int32(0),
    )
    inputs = dealt_tokens[0].astype(jnp.float32)
    q_full, k_full, v_full, o_full, gain_one, gain_two = (
        lax.all_gather(q_weight.astype(jnp.bfloat16), ("dp", "expert"), axis=0, tiled=True),
        lax.all_gather(k_weight.astype(jnp.bfloat16), ("dp", "expert"), axis=0, tiled=True),
        lax.all_gather(v_weight.astype(jnp.bfloat16), ("dp", "expert"), axis=0, tiled=True),
        lax.all_gather(o_weight.astype(jnp.bfloat16), ("dp", "expert"), axis=0, tiled=True),
        lax.all_gather(gain_attn.astype(jnp.bfloat16), ("dp", "expert"), axis=0, tiled=True),
        lax.all_gather(gain_moe.astype(jnp.bfloat16), ("dp", "expert"), axis=0, tiled=True),
    )
    gain_one = gain_one.astype(jnp.float32)
    gain_two = gain_two.astype(jnp.float32)
    seq_lengths = lengths[0]
    seq_ends = jnp.cumsum(seq_lengths)
    seq_starts = seq_ends - seq_lengths
    first_place = lax.axis_index("dp") * tok_rows
    places = first_place + jnp.arange(tok_rows, dtype=jnp.int32)
    member = (places[:, None] >= seq_starts[None, :]) & (places[:, None] < seq_ends[None, :])
    offsets = jnp.sum(jnp.where(member, places[:, None] - seq_starts[None, :], 0), axis=-1)
    frequency = THETA ** (-jnp.arange(HD // 2, dtype=jnp.float32) * 2.0 / HD)
    angles = offsets.astype(jnp.float32)[:, None] * frequency[None, :]
    angles = jnp.concatenate([angles, angles], axis=-1)[:, None, :]
    cosine = jnp.cos(angles)
    sine_table = jnp.sin(angles)
    query_seq = locate(places, seq_ends)
    seq_floor = jnp.sum(jnp.where(member[0], seq_starts, 0))
    low_block = seq_floor // block_rows
    high_block = (first_place + tok_rows - 1) // block_rows + 1
    normed = rms_scale(inputs, gain_one).astype(jnp.bfloat16)
    query_pre = jnp.dot(normed, q_full, preferred_element_type=jnp.float32).reshape(tok_rows, H, HD)
    key_pre = jnp.dot(normed, k_full, preferred_element_type=jnp.float32).reshape(tok_rows, KVH, HD)
    value_rows = jnp.dot(normed, v_full, preferred_element_type=jnp.float32).astype(jnp.bfloat16)
    queries = (
        rotate(query_pre, cosine, sine_table)
        .astype(jnp.bfloat16)
        .reshape(tok_rows, KVH, heads_per, HD)
    )
    key_rows = rotate(key_pre, cosine, sine_table).astype(jnp.bfloat16).reshape(tok_rows, KVH * HD)
    all_keys, all_values = (
        lax.all_gather(key_rows, "dp", axis=0, tiled=True),
        lax.all_gather(value_rows, "dp", axis=0, tiled=True),
    )

    def scores_for(block_id, key_block):
        begin_at = block_id * block_rows
        key_places = begin_at + jnp.arange(block_rows, dtype=jnp.int32)
        allowed = (query_seq[:, None] == locate(key_places, seq_ends)[None, :]) & (
            key_places[None, :] <= places[:, None]
        )
        raw_scores = SCORE_SCALE * jnp.einsum(
            "tkgd,skd->kgts", queries, key_block, preferred_element_type=jnp.float32
        )
        return (raw_scores, allowed)

    def stats_step(block_id, carried):
        run_top, run_total = carried
        key_block = cut_block(all_keys, block_id * block_rows, block_rows, KVH)
        raw_scores, allowed = scores_for(block_id, key_block)
        new_top = jnp.maximum(run_top, jnp.max(jnp.where(allowed, raw_scores, NEGATIVE), axis=-1))
        weights_now = jnp.where(allowed, jnp.exp(raw_scores - new_top[..., None]), 0.0)
        run_total = run_total * jnp.exp(run_top - new_top) + jnp.sum(weights_now, axis=-1)
        return (new_top, run_total)

    top_init = jnp.full((KVH, heads_per, tok_rows), NEGATIVE, jnp.float32)
    total_init = jnp.zeros((KVH, heads_per, tok_rows), jnp.float32)
    run_top, run_total = lax.fori_loop(low_block, high_block, stats_step, (top_init, total_init))
    log_total = run_top + jnp.log(run_total)

    def attn_probs(block_id, key_block):
        raw_scores, allowed = scores_for(block_id, key_block)
        return jnp.where(allowed, jnp.exp(raw_scores - log_total[..., None]), 0.0)

    def value_step(block_id, running):
        key_block = cut_block(all_keys, block_id * block_rows, block_rows, KVH)
        value_block = cut_block(all_values, block_id * block_rows, block_rows, KVH)
        chances = attn_probs(block_id, key_block).astype(jnp.bfloat16)
        return running + jnp.einsum(
            "kgts,skd->tkgd", chances, value_block, preferred_element_type=jnp.float32
        )

    mixed_init = jnp.zeros((tok_rows, KVH, heads_per, HD), jnp.float32)
    mixed_rows = lax.fori_loop(low_block, high_block, value_step, mixed_init).reshape(
        tok_rows, H * HD
    )
    mixed_low = mixed_rows.astype(jnp.bfloat16)
    branch = lax.dot_general(mixed_low, o_full, COLS_DIMS, preferred_element_type=jnp.float32)
    middle = inputs + RESIDUAL * branch
    sent_rows = rms_scale(middle, gain_two).astype(jnp.bfloat16)
    route_ids = routes[0].reshape(tok_rows * TOPK)
    matches = (route_ids[:, None] == jnp.arange(E, dtype=jnp.int32)[None, :]).astype(jnp.int32)
    slot_rank = jnp.sum(matches * jnp.cumsum(matches, axis=0), axis=-1) - 1
    slot_index = route_ids * CAP + slot_rank
    copies = jnp.repeat(sent_rows, TOPK, axis=0)
    outgoing = (
        jnp.zeros((E * CAP, model_width), jnp.bfloat16)
        .at[slot_index]
        .set(copies)
        .reshape(E, CAP, model_width)
    )
    arrived = lax.all_to_all(outgoing, "expert", split_axis=0, concat_axis=1, tiled=True)
    w_in, w_down = (
        lax.all_gather(in_weight.astype(jnp.bfloat16), "dp", axis=0, tiled=True),
        lax.all_gather(down_weight.astype(jnp.bfloat16), "dp", axis=0, tiled=True),
    )
    gate_up = jnp.einsum("erd,def->erf", arrived, w_in, preferred_element_type=jnp.float32)
    gate_part = gate_up[..., :FF]
    up_part = gate_up[..., FF:]
    hidden = silu_product(gate_part, up_part).astype(jnp.bfloat16)
    produced = jnp.einsum(
        "erf,fed->erd", hidden, w_down, preferred_element_type=jnp.float32
    ).astype(jnp.bfloat16)
    returned = lax.all_to_all(produced, "expert", split_axis=1, concat_axis=0, tiled=True).reshape(
        E * CAP, model_width
    )
    route_gates = gates[0].reshape(tok_rows * TOPK)
    picked = returned[slot_index].astype(jnp.float32) * route_gates[:, None]
    expert_sum = jnp.sum(picked.reshape(tok_rows, TOPK, model_width), axis=1)
    output = middle + RESIDUAL * expert_sum
    upstream = dealt_cotangent[0].astype(jnp.float32)
    spread = (RESIDUAL * route_gates[:, None] * jnp.repeat(upstream, TOPK, axis=0)).astype(
        jnp.bfloat16
    )
    back_out = (
        jnp.zeros((E * CAP, model_width), jnp.bfloat16)
        .at[slot_index]
        .set(spread)
        .reshape(E, CAP, model_width)
    )
    back_in = lax.all_to_all(back_out, "expert", split_axis=0, concat_axis=1, tiled=True)
    hidden_grad = jnp.einsum("erd,fed->erf", back_in, w_down, preferred_element_type=jnp.float32)
    down_term = jnp.einsum("erf,erd->fed", hidden, back_in, preferred_element_type=jnp.float32)
    ignored, silu_pull = jax.vjp(silu_product, gate_part, up_part)
    gate_grad, up_grad = silu_pull(hidden_grad)
    gate_up_grad = jnp.concatenate([gate_grad, up_grad], axis=-1).astype(jnp.bfloat16)
    in_term = jnp.einsum("erd,erf->def", arrived, gate_up_grad, preferred_element_type=jnp.float32)
    arrived_grad = jnp.einsum(
        "erf,def->erd", gate_up_grad, w_in, preferred_element_type=jnp.float32
    ).astype(jnp.bfloat16)
    sent_back = lax.all_to_all(
        arrived_grad, "expert", split_axis=1, concat_axis=0, tiled=True
    ).reshape(E * CAP, model_width)
    sent_grad = jnp.sum(
        sent_back[slot_index].astype(jnp.float32).reshape(tok_rows, TOPK, model_width), axis=1
    )
    in_grad, down_grad = (
        lax.psum_scatter(
            in_term.astype(jnp.bfloat16), "dp", scatter_dimension=0, tiled=True
        ).astype(jnp.float32),
        lax.psum_scatter(
            down_term.astype(jnp.bfloat16), "dp", scatter_dimension=0, tiled=True
        ).astype(jnp.float32),
    )
    ignored, second_pull = jax.vjp(rms_scale, middle, gain_two)
    middle_part, gain_two_term = second_pull(sent_grad)
    middle_grad = upstream + middle_part
    branch_grad = (RESIDUAL * middle_grad).astype(jnp.bfloat16)
    o_term = lax.dot_general(branch_grad, mixed_low, ROWS_DIMS, preferred_element_type=jnp.float32)
    grad_heads = jnp.dot(branch_grad, o_full, preferred_element_type=jnp.float32).astype(
        jnp.bfloat16
    )
    grad_heads = grad_heads.reshape(tok_rows, KVH, heads_per, HD)

    def delta_step(block_id, running):
        key_block = cut_block(all_keys, block_id * block_rows, block_rows, KVH)
        value_block = cut_block(all_values, block_id * block_rows, block_rows, KVH)
        chances = attn_probs(block_id, key_block)
        prob_grad = jnp.einsum(
            "tkgd,skd->kgts", grad_heads, value_block, preferred_element_type=jnp.float32
        )
        return running + jnp.sum(chances * prob_grad, axis=-1)

    row_delta = lax.fori_loop(
        low_block, high_block, delta_step, jnp.zeros((KVH, heads_per, tok_rows), jnp.float32)
    )

    def grad_step(block_id, carried):
        query_grad, key_buffer, value_buffer = carried
        begin_at = block_id * block_rows
        key_block = cut_block(all_keys, begin_at, block_rows, KVH)
        value_block = cut_block(all_values, begin_at, block_rows, KVH)
        chances = attn_probs(block_id, key_block)
        prob_grad = jnp.einsum(
            "tkgd,skd->kgts", grad_heads, value_block, preferred_element_type=jnp.float32
        )
        score_grad = (chances * (prob_grad - row_delta[..., None])).astype(jnp.bfloat16)
        query_grad = query_grad + SCORE_SCALE * jnp.einsum(
            "kgts,skd->tkgd", score_grad, key_block, preferred_element_type=jnp.float32
        )
        key_part = SCORE_SCALE * jnp.einsum(
            "kgts,tkgd->skd", score_grad, queries, preferred_element_type=jnp.float32
        )
        value_part = jnp.einsum(
            "kgts,tkgd->skd",
            chances.astype(jnp.bfloat16),
            grad_heads,
            preferred_element_type=jnp.float32,
        )
        key_buffer = lax.dynamic_update_slice_in_dim(
            key_buffer, key_part.reshape(block_rows, KVH * HD), begin_at, 0
        )
        value_buffer = lax.dynamic_update_slice_in_dim(
            value_buffer, value_part.reshape(block_rows, KVH * HD), begin_at, 0
        )
        return (query_grad, key_buffer, value_buffer)

    grad_init = (
        jnp.zeros((tok_rows, KVH, heads_per, HD), jnp.float32),
        jnp.zeros((group_rows, KVH * HD), jnp.float32),
        jnp.zeros((group_rows, KVH * HD), jnp.float32),
    )
    query_grad, key_buffer, value_buffer = lax.fori_loop(
        low_block, high_block, grad_step, grad_init
    )
    key_grad, value_grad = (
        lax.psum_scatter(
            key_buffer.astype(jnp.bfloat16), "dp", scatter_dimension=0, tiled=True
        ).astype(jnp.float32),
        lax.psum_scatter(
            value_buffer.astype(jnp.bfloat16), "dp", scatter_dimension=0, tiled=True
        ).astype(jnp.float32),
    )
    query_low = (
        turn_back(query_grad.reshape(tok_rows, H, HD), cosine, sine_table)
        .reshape(tok_rows, H * HD)
        .astype(jnp.bfloat16)
    )
    key_low = (
        turn_back(key_grad.reshape(tok_rows, KVH, HD), cosine, sine_table)
        .reshape(tok_rows, KVH * HD)
        .astype(jnp.bfloat16)
    )
    value_low = value_grad.astype(jnp.bfloat16)
    q_term = lax.dot_general(normed, query_low, ROWS_DIMS, preferred_element_type=jnp.float32)
    k_term = lax.dot_general(normed, key_low, ROWS_DIMS, preferred_element_type=jnp.float32)
    v_term = lax.dot_general(normed, value_low, ROWS_DIMS, preferred_element_type=jnp.float32)
    normed_grad = lax.dot_general(query_low, q_full, COLS_DIMS, preferred_element_type=jnp.float32)
    normed_grad = normed_grad + lax.dot_general(
        key_low, k_full, COLS_DIMS, preferred_element_type=jnp.float32
    )
    normed_grad = normed_grad + lax.dot_general(
        value_low, v_full, COLS_DIMS, preferred_element_type=jnp.float32
    )
    ignored, first_pull = jax.vjp(rms_scale, inputs, gain_one)
    input_part, gain_one_term = first_pull(normed_grad)
    input_grad = middle_grad + input_part
    q_grad, k_grad, v_grad, o_grad, gain_attn_grad, gain_moe_grad = (
        lax.psum_scatter(q_term, ("dp", "expert"), scatter_dimension=0, tiled=True),
        lax.psum_scatter(k_term, ("dp", "expert"), scatter_dimension=0, tiled=True),
        lax.psum_scatter(v_term, ("dp", "expert"), scatter_dimension=0, tiled=True),
        lax.psum_scatter(o_term, ("dp", "expert"), scatter_dimension=0, tiled=True),
        lax.psum_scatter(gain_one_term, ("dp", "expert"), scatter_dimension=0, tiled=True),
        lax.psum_scatter(gain_two_term, ("dp", "expert"), scatter_dimension=0, tiled=True),
    )
    given_output, given_input_grad = group_chooser(
        wanted_out,
        (
            jnp.zeros((1, tok_rows, model_width), jnp.float32),
            jnp.zeros((1, tok_rows, model_width), jnp.float32),
        ),
        (
            lax.all_gather(output[None].astype(jnp.bfloat16), "expert", axis=0, tiled=True).astype(
                jnp.float32
            ),
            lax.all_gather(
                input_grad[None].astype(jnp.bfloat16), "expert", axis=0, tiled=True
            ).astype(jnp.float32),
        ),
        jnp.int32(0),
    )
    return (
        given_output,
        given_input_grad,
        q_grad,
        k_grad,
        v_grad,
        o_grad,
        gain_attn_grad,
        gain_moe_grad,
        in_grad,
        down_grad,
    )


SWAP_Y = [(i, i ^ 1) for i in range(8)]
SWAP_CORE = [(j, j ^ 1) for j in range(4)]
SWAP_X = [(j, j ^ 2) for j in range(4)]


def along_z(moves):
    return [(2 * s + y, 2 * d + y) for s, d in moves for y in range(2)]


Z_NEAR = along_z([(0, 1), (1, 0), (2, 3), (3, 2)])
Z_MIDDLE = along_z([(1, 2), (2, 1)])
Z_OUT = along_z([(1, 0), (2, 3)])
Z_IN = along_z([(0, 1), (3, 2)])
SLOT_Z = ((0, 1, 2, 3), (1, 0, 3, 2), (2, 2, 1, 1), (3, 3, 0, 0))


def over_dp(piece, moves):
    return lax.ppermute(piece, "dp", moves)


def over_expert(piece, moves):
    return lax.ppermute(piece, "expert", moves)


def added(first, *others):
    total = first.astype(jnp.float32)
    for other in others:
        total = total + other.astype(jnp.float32)
    return total.astype(jnp.bfloat16)


def halves(array):
    half = array.shape[0] // 2
    return array[:half], array[half:]


def joined(*arrays):
    return jnp.concatenate(arrays, axis=0)


def one_round(outs, ins, cover=None):
    if cover is None:
        return lax.optimization_barrier(outs), None
    return lax.optimization_barrier((outs, cover(lambda x: after(x, *ins))))


def swap_y(value):
    return over_dp(value, SWAP_Y)


def swap_x(value):
    return over_expert(value, SWAP_X)


def swap_core(value):
    return over_expert(value, SWAP_CORE)


def dp_gather(piece, covers=(None, None, None, None)):
    works = []

    def run(outs, ins, cover):
        outs, work = one_round(outs, ins, cover and (lambda tie: cover(tie, works)))
        works.append(work)
        return outs

    near, middle, y0 = run(
        (over_dp(piece, Z_NEAR), over_dp(piece, Z_MIDDLE), swap_y(piece)), (piece,), covers[0]
    )
    far, out1, y1 = run(
        (over_dp(near, Z_MIDDLE), over_dp(middle, Z_OUT), swap_y(near)), (near, middle), covers[1]
    )
    third = middle + out1
    out2, y2 = run((over_dp(far, Z_OUT), swap_y(third)), (far, third), covers[2])
    fourth = far + out2
    y3 = run(swap_y(fourth), (fourth,), covers[3])
    return joined(piece, y0, near, y1, third, y2, fourth, y3), works


class DpScatter:
    def __init__(self, total):
        blocks = jnp.split(total, 8, axis=0)
        self.own, self.sent = blocks[0::2], blocks[1::2]
        self.round = 0

    def step(self, tie=lambda v: v):
        self.round += 1
        if self.round == 1:
            self.z = swap_y(tie(self.sent[3]))
        elif self.round == 2:
            self.fourth = added(self.own[3], self.z)
            self.z = over_dp(tie(self.fourth), Z_IN), swap_y(self.sent[2])
        elif self.round == 3:
            fourth = added(self.fourth, self.z[0])
            self.third = added(self.own[2], self.z[1])
            self.z = (
                over_dp(tie(fourth), Z_MIDDLE),
                over_dp(self.third, Z_IN),
                swap_y(self.sent[1]),
            )
        else:
            third = added(self.third, self.z[1])
            near = added(self.own[1], self.z[2], self.z[0])
            self.z = (
                over_dp(tie(near), Z_NEAR),
                over_dp(third, Z_MIDDLE),
                swap_y(self.sent[0]),
            )
        return self.z

    def keep(self, values):
        self.z = values

    def total(self):
        total = self.own[0].astype(jnp.float32)
        for value in self.z:
            total = total + value.astype(jnp.float32)
        return total


def gather_beside_sum(piece, attention):
    (near, middle, y0), attended = one_round(
        (over_dp(piece, Z_NEAR), over_dp(piece, Z_MIDDLE), swap_y(piece)), (piece,), attention
    )
    part = attended[-1]
    pair0 = joined(piece, y0)
    total = DpScatter(part)
    (far, out1, y1, x0, sums), _ = one_round(
        (
            over_dp(near, Z_MIDDLE),
            over_dp(middle, Z_OUT),
            swap_y(near),
            swap_x(pair0),
            total.step(),
        ),
        (near, middle, pair0),
    )
    total.keep(sums)
    third = middle + out1
    pair1 = joined(near, y1)
    (out2, y2, x1, sums), _ = one_round(
        (over_dp(far, Z_OUT), swap_y(third), swap_x(pair1), total.step()), (far, third, pair1)
    )
    total.keep(sums)
    fourth = far + out2
    pair2 = joined(third, y2)
    (y3, x2, sums), _ = one_round((swap_y(fourth), swap_x(pair2), total.step()), (fourth, pair2))
    total.keep(sums)
    pair3 = joined(fourth, y3)
    (x3, sums), _ = one_round((swap_x(pair3), total.step()), (pair3,))
    total.keep(sums)
    here = joined(pair0, x0, pair1, x1, pair2, x2, pair3, x3)
    return joined(here, swap_core(here)), total.total(), attended


def gather_pairs(piece, covers):
    works = []

    def run(outs, ins, cover=None):
        outs, work = one_round(outs, ins, cover and (lambda tie: cover(tie, works)))
        works.append(work)
        return outs

    near, middle = run((over_dp(piece, Z_NEAR), over_dp(piece, Z_MIDDLE)), (piece,))

    def split(first, second):
        (ft, fl), (st, sl) = halves(first), halves(second)
        return joined(ft, st), joined(fl, sl)

    top, low = split(piece, near)
    far, out1, y_top, x_low = run(
        (over_dp(near, Z_MIDDLE), over_dp(middle, Z_OUT), swap_y(top), swap_x(low)),
        (top, low),
        covers[0],
    )
    third = middle + out1
    top, low = joined(top, y_top), joined(low, x_low)
    out2, x_top, y_low = run(
        (over_dp(far, Z_OUT), swap_x(top), swap_y(low)), (top, low), covers[1]
    )
    here = joined(top, x_top, low, y_low)
    top, low = split(third, far + out2)
    y_top, x_low, there = run(
        (swap_y(top), swap_x(low), swap_core(here)), (top, low, here), covers[2]
    )
    first = joined(here, there)
    top, low = joined(top, y_top), joined(low, x_low)
    x_top, y_low = run(
        (swap_x(top), swap_y(low)), (top, low), lambda tie, works: covers[3](tie, works, first)
    )
    here = joined(top, x_top, low, y_low)
    there = run(swap_core(here), (here,), covers[4])
    return (first, joined(here, there)), works


class PairScatter:
    def __init__(self, totals):
        (self.m0, self.o0), (self.m1, self.o1) = [halves(t) for t in totals]
        self.round = 0

    def across(self, parts, first, second, tie):
        (ta, tb), (la, lb) = [halves(p) for p in parts]
        return (ta, la), (first(tie(tb)), second(tie(lb)))

    def both(self, kept, moved):
        return [added(k, m) for k, m in zip(kept, moved)]

    def step(self, tie=lambda v: v):
        self.round += 1
        if self.round == 1:
            self.moved = swap_core(tie(self.o1))
        elif self.round == 2:
            parts = halves(added(self.m1, self.moved))
            self.kept1, moved1 = self.across(parts, swap_x, swap_y, tie)
            self.moved = moved1, swap_core(tie(self.o0))
        elif self.round == 3:
            parts1 = self.both(self.kept1, self.moved[0])
            parts0 = halves(added(self.m0, self.moved[1]))
            self.kept1, moved1 = self.across(parts1, swap_y, swap_x, tie)
            self.kept0, moved0 = self.across(parts0, swap_x, swap_y, tie)
            self.moved = moved1, moved0
        elif self.round == 4:
            (third_top, fourth_top), (third_low, fourth_low) = [
                halves(p) for p in self.both(self.kept1, self.moved[0])
            ]
            self.third, self.fourth = joined(third_top, third_low), joined(fourth_top, fourth_low)
            parts0 = self.both(self.kept0, self.moved[1])
            self.kept0, moved0 = self.across(parts0, swap_y, swap_x, tie)
            self.moved = moved0, over_dp(tie(self.fourth), Z_IN)
        elif self.round == 5:
            (own_top, near_top), (own_low, near_low) = [
                halves(p) for p in self.both(self.kept0, self.moved[0])
            ]
            self.own, self.near = joined(own_top, own_low), joined(near_top, near_low)
            fourth = added(self.fourth, self.moved[1])
            self.moved = over_dp(tie(fourth), Z_MIDDLE), over_dp(tie(self.third), Z_IN)
        else:
            near, third = added(self.near, self.moved[0]), added(self.third, self.moved[1])
            self.moved = over_dp(tie(near), Z_NEAR), over_dp(tie(third), Z_MIDDLE)
        return self.moved

    def keep(self, values):
        self.moved = values

    def total(self):
        total = self.own.astype(jnp.float32)
        for value in self.moved:
            total = total + value.astype(jnp.float32)
        return total


def scatter_pairs(totals, covers):
    works = []
    scatter = PairScatter(totals)
    for cover in covers:
        outs = scatter.step()
        outs, work = one_round(outs, (), cover and (lambda tie: cover(tie, works)))
        scatter.keep(outs)
        works.append(work)
    return scatter.total(), works


def far_order(ex_index, dealt_of):
    r = jnp.arange(64, dtype=jnp.int32)
    pair, core, half, outer, inner = r // 32, r // 16 % 2, r // 8 % 2, r // 4 % 2, r // 2 % 2
    slot = 2 * pair + r % 2
    flip_y = jnp.where(half == 0, inner, outer)
    flip_x = jnp.where(half == 0, outer, inner)

    def place(flip):
        return ((flip % 2 * 4 + slot) * 4 + flip // 2 * 2 + flip_y) * 2 + half

    flip = 2 * flip_x + core
    return place(flip), place(jnp.take(dealt_of, ex_index ^ flip) ^ ex_index)


def take_kernel(index_ref, *refs, at_once):
    count = len(refs) // (at_once + 1)
    for p in range(count):
        target = refs[count * at_once + p]
        rows = target.shape[0] // at_once
        for k in range(at_once):
            target[k * rows : (k + 1) * rows, :] = refs[p * at_once + k][...]


def take_blocks(index, array, parts, block):
    at_once = 8
    steps = index.shape[1] // at_once

    def source(row, column, k):
        return lambda i, idx: (idx[row, at_once * i + k], column)

    return pl.pallas_call(
        functools.partial(take_kernel, at_once=at_once),
        out_shape=[
            jax.ShapeDtypeStruct((index.shape[1] * block, width), array.dtype)
            for row, column, width in parts
        ],
        grid_spec=pltpu.PrefetchScalarGridSpec(
            num_scalar_prefetch=1,
            grid=(steps,),
            in_specs=[
                pl.BlockSpec((block, width), source(row, column, k))
                for row, column, width in parts
                for k in range(at_once)
            ],
            out_specs=[
                pl.BlockSpec((at_once * block, width), lambda i, idx: (i, 0))
                for row, column, width in parts
            ],
        ),
        name="take_blocks",
    )(index, *([array] * (at_once * len(parts))))


def attend_masks(row_ids, col_ids, begin, rows):
    seq_rows = row_ids[pl.ds(begin, rows), 0:1]
    place_rows = row_ids[pl.ds(begin, rows), 1:2]
    return (seq_rows == col_ids[0:1, :]) & (col_ids[1:2, :] <= place_rows)


def front_kernel(
    x_ref, gain_ref, w_ref, ow_ref, cos_ref, sin_ref, row_ids, col_ids,
    normed_ref, q_ref, k_ref, v_ref, o_ref, top_ref, total_ref, part_ref, *, heads, rows
):
    q_cols = heads * HD
    steps = x_ref.shape[0] // rows

    def project(i, carry):
        here = pl.ds(pl.multiple_of(i * rows, rows), rows)
        inputs = x_ref[here, :].astype(jnp.float32)
        scale = lax.rsqrt(jnp.mean(inputs * inputs, axis=-1, keepdims=True) + EPSILON)
        normed = (inputs * scale * gain_ref[...]).astype(jnp.bfloat16)
        normed_ref[here, :] = normed
        qkv = jnp.dot(normed, w_ref[...], preferred_element_type=jnp.float32)
        cosine, sine = cos_ref[here, :], sin_ref[here, :]
        turned = []
        for h in range(heads + 1):
            turned.append(rotate(qkv[:, h * HD : (h + 1) * HD], cosine, sine))
        q_ref[here, :] = jnp.concatenate(turned[:heads], axis=1).astype(jnp.bfloat16)
        k_ref[here, :] = turned[heads].astype(jnp.bfloat16)
        v_ref[here, :] = qkv[:, q_cols + HD :].astype(jnp.bfloat16)
        return carry

    lax.fori_loop(0, steps, project, 0)
    keys, vals = k_ref[...], v_ref[...]

    def step(i, carry):
        begin = pl.multiple_of(i * rows, rows)
        here = pl.ds(begin, rows)
        allowed = attend_masks(row_ids, col_ids, begin, rows)
        outs, tops, totals = [], [], []
        for h in range(heads):
            scores = SCORE_SCALE * lax.dot_general(
                q_ref[here, h * HD : (h + 1) * HD],
                keys,
                COLS_DIMS,
                preferred_element_type=jnp.float32,
            )
            scores = jnp.where(allowed, scores, NEGATIVE)
            top = jnp.max(scores, axis=-1, keepdims=True)
            weights = jnp.exp(scores - top)
            total = jnp.sum(weights, axis=-1, keepdims=True)
            chances = (weights / total).astype(jnp.bfloat16)
            outs.append(jnp.dot(chances, vals, preferred_element_type=jnp.float32))
            tops.append(top)
            totals.append(total)
        mixed = jnp.concatenate(outs, axis=1).astype(jnp.bfloat16)
        o_ref[here, :] = mixed
        top_ref[here, :] = jnp.concatenate(tops, axis=1)
        total_ref[here, :] = jnp.concatenate(totals, axis=1)
        part_ref[here, :] = lax.dot_general(
            mixed, ow_ref[...], COLS_DIMS, preferred_element_type=jnp.float32
        ).astype(jnp.bfloat16)
        return carry

    lax.fori_loop(0, steps, step, 0)


def front(inputs, gain, qkv_w, o_w, cosine, sine, row_ids, col_ids):
    rows, model = inputs.shape
    heads = H // KVH
    low = jnp.bfloat16
    return pl.pallas_call(
        functools.partial(front_kernel, heads=heads, rows=min(256, rows)),
        out_shape=[
            jax.ShapeDtypeStruct((rows, model), low),
            jax.ShapeDtypeStruct((rows, heads * HD), low),
            jax.ShapeDtypeStruct((rows, HD), low),
            jax.ShapeDtypeStruct((rows, HD), low),
            jax.ShapeDtypeStruct((rows, heads * HD), low),
            jax.ShapeDtypeStruct((rows, heads), jnp.float32),
            jax.ShapeDtypeStruct((rows, heads), jnp.float32),
            jax.ShapeDtypeStruct((rows, model), low),
        ],
        name="front",
    )(inputs, gain, qkv_w, o_w, cosine, sine, row_ids, col_ids)


def rear_kernel(
    g_ref, ow_ref, q_ref, k_ref, v_ref, top_ref, total_ref, row_ids, col_ids, cos_ref, sin_ref,
    w_ref, x_ref, qkvg_ref, part_ref, gain_ref, dk_ref, dv_ref, *, heads, rows
):
    q_cols = heads * HD
    steps = x_ref.shape[0] // rows
    dk_ref[...] = jnp.zeros_like(dk_ref)
    dv_ref[...] = jnp.zeros_like(dv_ref)
    gain_ref[...] = jnp.zeros_like(gain_ref)
    keys, vals = k_ref[...], v_ref[...]

    def step(i, carry):
        begin = pl.multiple_of(i * rows, rows)
        here = pl.ds(begin, rows)
        allowed = attend_masks(row_ids, col_ids, begin, rows)
        grads = jnp.dot(g_ref[here, :], ow_ref[...], preferred_element_type=jnp.float32).astype(
            jnp.bfloat16
        )
        cosine, sine = cos_ref[here, :], sin_ref[here, :]
        pulled = []
        key_grad = jnp.zeros((k_ref.shape[0], HD), jnp.float32)
        value_grad = jnp.zeros((k_ref.shape[0], HD), jnp.float32)
        for h in range(heads):
            query = q_ref[here, h * HD : (h + 1) * HD]
            grad = grads[:, h * HD : (h + 1) * HD]
            scores = SCORE_SCALE * lax.dot_general(
                query, keys, COLS_DIMS, preferred_element_type=jnp.float32
            )
            scores = jnp.where(allowed, scores, NEGATIVE)
            weights = jnp.exp(scores - top_ref[here, h : h + 1])
            chances = weights / total_ref[here, h : h + 1]
            prob_grad = lax.dot_general(grad, vals, COLS_DIMS, preferred_element_type=jnp.float32)
            delta = jnp.sum(chances * prob_grad, axis=-1, keepdims=True)
            score_grad = (chances * (prob_grad - delta)).astype(jnp.bfloat16)
            query_grad = SCORE_SCALE * jnp.dot(
                score_grad, keys, preferred_element_type=jnp.float32
            )
            pulled.append(turn_back(query_grad, cosine, sine))
            key_grad += lax.dot_general(
                score_grad, query, ROWS_DIMS, preferred_element_type=jnp.float32
            )
            value_grad += lax.dot_general(
                chances.astype(jnp.bfloat16), grad, ROWS_DIMS, preferred_element_type=jnp.float32
            )
        qkvg_ref[here, 0:q_cols] = jnp.concatenate(pulled, axis=1).astype(jnp.bfloat16)
        dk_ref[...] += SCORE_SCALE * key_grad
        dv_ref[...] += value_grad
        return carry

    lax.fori_loop(0, steps, step, 0)

    def finish(i, carry):
        here = pl.ds(pl.multiple_of(i * rows, rows), rows)
        key_low = turn_back(dk_ref[here, :], cos_ref[here, :], sin_ref[here, :])
        qkvg_ref[here, q_cols:] = jnp.concatenate([key_low, dv_ref[here, :]], axis=1).astype(
            jnp.bfloat16
        )
        part = lax.dot_general(
            qkvg_ref[here, :], w_ref[...], COLS_DIMS, preferred_element_type=jnp.float32
        )
        part_ref[here, :] = part.astype(jnp.bfloat16)
        inputs = x_ref[here, :].astype(jnp.float32)
        scale = lax.rsqrt(jnp.mean(inputs * inputs, axis=-1, keepdims=True) + EPSILON)
        gain_ref[...] += jnp.sum(part * inputs * scale, axis=0, keepdims=True)
        return carry

    lax.fori_loop(0, steps, finish, 0)


def rear(grads_in, o_w, queries, keys, vals, top, total, row_ids, col_ids, cosine, sine, qkv_w, x):
    rows, model = x.shape
    heads = H // KVH
    return pl.pallas_call(
        functools.partial(rear_kernel, heads=heads, rows=min(256, rows)),
        out_shape=[
            jax.ShapeDtypeStruct((rows, qkv_w.shape[1]), jnp.bfloat16),
            jax.ShapeDtypeStruct((rows, model), jnp.bfloat16),
            jax.ShapeDtypeStruct((1, model), jnp.float32),
        ],
        scratch_shapes=[
            pltpu.VMEM((rows, HD), jnp.float32),
            pltpu.VMEM((rows, HD), jnp.float32),
        ],
        name="rear",
    )(grads_in, o_w, queries, keys, vals, top, total, row_ids, col_ids, cosine, sine, qkv_w, x)


def after(value, *earlier):
    return lax.optimization_barrier((value, *earlier))[0]


def rounded(values):
    return lax.reduce_precision(values, 8, 7)


def rope_parts(seq_lengths, places):
    seq_ends = jnp.cumsum(seq_lengths)
    seq_starts = seq_ends - seq_lengths
    member = (places[:, None] >= seq_starts[None, :]) & (places[:, None] < seq_ends[None, :])
    offsets = jnp.sum(jnp.where(member, places[:, None] - seq_starts[None, :], 0), axis=-1)
    frequency = THETA ** (-jnp.arange(HD // 2, dtype=jnp.float32) * 2.0 / HD)
    angles = offsets.astype(jnp.float32)[:, None] * frequency[None, :]
    angles = jnp.concatenate([angles, angles], axis=-1)[:, None, :]
    seq_ids = locate(places, seq_ends)
    return seq_ids, jnp.cos(angles), jnp.sin(angles)


def per_device(
    tokens,
    cotangent,
    lengths,
    deal,
    routes,
    gates,
    q_weight,
    k_weight,
    v_weight,
    o_weight,
    gain_attn,
    gain_moe,
    in_weight,
    down_weight,
):
    n_dp = lax.axis_size("dp")
    n_ex = lax.axis_size("expert")
    tok_rows = tokens.shape[1]
    model = tokens.shape[2]
    kv_here = KVH // n_dp
    heads_per = H // KVH
    q_cols = kv_here * heads_per * HD
    kv_cols = kv_here * HD
    own_experts = in_weight.shape[1]
    ff_here = FF // n_dp
    ff_cols = own_experts * ff_here
    w_rows = q_weight.shape[0]
    ex_index = lax.axis_index("expert")
    group_ids = jnp.arange(deal.shape[0], dtype=jnp.int32)
    dealt_of = jnp.argmax((deal[None, :] == group_ids[:, None]).astype(jnp.int32), axis=1)
    own_dealt = jnp.sum(jnp.where(deal == ex_index, group_ids, 0))

    def by_owner(weight):
        return weight.astype(jnp.bfloat16).reshape(w_rows, n_dp, weight.shape[1] // n_dp)

    length_parts = jnp.stack([lengths[0] // 128, lengths[0] % 128]).reshape(-1).astype(jnp.bfloat16)
    n_len = length_parts.shape[0]
    extra = jnp.concatenate(
        [
            gain_attn.astype(jnp.bfloat16)[:, None],
            gain_moe.astype(jnp.bfloat16)[:, None],
            jnp.broadcast_to(length_parts[None, :], (w_rows, n_len)),
            jnp.zeros((w_rows, 126 - n_len), jnp.bfloat16),
        ],
        axis=1,
    )
    d_rows = in_weight.shape[0]

    def pack_in(tie):
        return (
            tie(in_weight)
            .astype(jnp.bfloat16)
            .reshape(in_weight.shape[0], own_experts, 2, n_dp, ff_here)
            .transpose(3, 0, 2, 1, 4)
            .reshape(n_dp, in_weight.shape[0], 2 * ff_cols)
        )

    attn_out = jnp.concatenate(
        [
            by_owner(q_weight),
            by_owner(k_weight),
            by_owner(v_weight),
            by_owner(o_weight),
            jnp.broadcast_to(extra[:, None, :], (w_rows, n_dp, 128)),
        ],
        axis=2,
    ).transpose(1, 0, 2)
    attn_in = lax.all_to_all(attn_out, "dp", split_axis=0, concat_axis=0, tiled=True)

    group_tokens, (_, in_out, _, _) = dp_gather(
        tokens[0], (None, lambda tie, works: pack_in(tie), None, None)
    )
    attn_two = jnp.stack([attn_in, swap_core(attn_in)])
    attn_four = joined(attn_two, swap_x(attn_two))
    in_w = lax.all_to_all(
        after(in_out, group_tokens, attn_in), "dp", split_axis=0, concat_axis=0, tiled=True
    ).reshape(model, 2 * ff_cols)
    z_own, y_own = lax.axis_index("dp") // 2, lax.axis_index("dp") % 2
    slot_dp = 2 * jnp.asarray(SLOT_Z, jnp.int32)[:, z_own]
    block_dp = jnp.stack([slot_dp + y_own, slot_dp + 1 - y_own], axis=1).reshape(-1)
    places = (block_dp[:, None] * tok_rows + jnp.arange(tok_rows, dtype=jnp.int32)).reshape(-1)


    def of_expert(index):
        return lax.dynamic_index_in_dim(attn_four, index ^ ex_index, 0, keepdims=False)

    attn_all = jnp.stack([of_expert(e) for e in range(n_ex)])
    attn_w = attn_all.transpose(1, 0, 2, 3).reshape(model, -1)
    qkv_cols = q_cols + 2 * kv_cols
    qkv_w = attn_w[:, :qkv_cols]
    o_w = attn_w[:, qkv_cols : qkv_cols + q_cols]
    side = attn_w[:, qkv_cols + q_cols :]
    gain_one = side[:, 0].astype(jnp.float32)
    gain_two = side[:, 1].astype(jnp.float32)
    own_parts = of_expert(own_dealt)[
        0, 0, qkv_cols + q_cols + 2 : qkv_cols + q_cols + 2 + n_len
    ].astype(jnp.int32)
    seq_lengths = own_parts[: n_len // 2] * 128 + own_parts[n_len // 2 :]

    down_w = down_weight.astype(jnp.bfloat16).transpose(1, 0, 2).reshape(ff_cols, model)

    every = jnp.arange(E, dtype=jnp.int32)[None, :]
    dense = sum(
        jnp.where(routes[0][:, k : k + 1] == every, gates[0][:, k : k + 1], 0.0)
        for k in range(TOPK)
    )
    dense_top = rounded(dense)
    dense_mid = rounded(dense - dense_top)
    meta = jnp.concatenate(
        [
            dense_top,
            dense_mid,
            dense - dense_top - dense_mid,
            jnp.zeros((tok_rows, 128 - 3 * E), jnp.float32),
        ],
        axis=1,
    ).astype(jnp.bfloat16)

    seq_ids, cosine, sine_table = rope_parts(seq_lengths, places)
    cosine, sine_table = cosine[:, 0], sine_table[:, 0]
    row_ids = jnp.stack([seq_ids, places], axis=1)
    col_ids = jnp.stack([seq_ids, places], axis=0)

    def attention(tie):
        return front(
            tie(group_tokens), gain_one[None], qkv_w, o_w, cosine, sine_table, row_ids, col_ids
        )

    cot_out = after(jnp.concatenate([cotangent[0], meta], axis=1), group_tokens)
    cot_all, branch, attended = gather_beside_sum(cot_out, attention)
    normed, queries, keys, vals, mixed_low, run_top, run_total, _ = attended
    rows_from, meta_from = far_order(ex_index, dealt_of)
    cot_rows, meta_all = take_blocks(
        jnp.stack([rows_from, meta_from]),
        cot_all,
        [(0, 0, model), (1, model // 128, 128)],
        tok_rows // 2,
    )
    inputs = tokens[0].astype(jnp.float32)
    middle = inputs + RESIDUAL * branch
    second_scale = lax.rsqrt(jnp.mean(middle * middle, axis=-1, keepdims=True) + EPSILON)
    sent_rows = (middle * second_scale * gain_two).astype(jnp.bfloat16)
    sent_rows = after(sent_rows, in_w, cot_rows)
    part_rows = 16 * tok_rows

    def spread_gates(tie, works):
        column = jnp.arange(128, dtype=jnp.int32)[:, None]
        owner = ex_index * own_experts + jnp.arange(ff_cols, dtype=jnp.int32)[None, :] // ff_here
        spread = ((column % E == owner) & (column < 3 * E)).astype(jnp.bfloat16)
        return jnp.dot(tie(meta_all), spread, preferred_element_type=jnp.float32)

    def pull(tie, works):
        return lax.dot_general(
            tie(cot_rows), down_w, COLS_DIMS, preferred_element_type=jnp.float32
        )

    def up(sent):
        return jnp.dot(sent, in_w, preferred_element_type=jnp.float32)

    def down(gate_up, gates_here, pulled_here):
        gate_part = gate_up[:, :ff_cols]
        up_part = gate_up[:, ff_cols:]
        sigma = jax.nn.sigmoid(gate_part)
        silu = gate_part * sigma
        hidden = (silu * up_part).astype(jnp.bfloat16).astype(jnp.float32)
        weighted_here = (gates_here * hidden).astype(jnp.bfloat16)
        hidden_grad = RESIDUAL * gates_here * pulled_here
        gate_grad = hidden_grad * up_part * (sigma * (1.0 + gate_part * (1.0 - sigma)))
        up_grad = hidden_grad * silu
        grads_here = jnp.concatenate([gate_grad, up_grad], axis=1).astype(jnp.bfloat16)
        return weighted_here, grads_here

    def back(grads_here):
        return lax.dot_general(
            grads_here, in_w, COLS_DIMS, preferred_element_type=jnp.float32
        ).astype(jnp.bfloat16)

    def of_part(number, works, gate_up):
        rows_here = slice(number * part_rows, (number + 1) * part_rows)
        return down(gate_up, works[2][rows_here], works[3][rows_here])

    def first_up(tie, works, sent):
        return up(tie(sent))

    def first_down(tie, works):
        weighted_here, grads_here = of_part(0, works, tie(works[4]))
        return weighted_here, grads_here, back(grads_here)

    sent_parts, works = gather_pairs(
        sent_rows, (None, spread_gates, pull, first_up, first_down)
    )
    weighted_first, grads_first, back_first = works[5]
    weighted_second, grads_second = of_part(1, works, up(sent_parts[1]))

    def out_first(tie, works):
        return jnp.dot(tie(weighted_first), down_w, preferred_element_type=jnp.float32).astype(
            jnp.bfloat16
        )

    def out_second(tie, works):
        return jnp.dot(tie(weighted_second), down_w, preferred_element_type=jnp.float32).astype(
            jnp.bfloat16
        )

    def in_first(tie, works):
        return lax.dot_general(
            tie(sent_parts[0]), grads_first, ROWS_DIMS, preferred_element_type=jnp.float32
        )

    out_sum = []

    def in_second(tie, works):
        out_sum.append(PairScatter(works[:2]))
        term = works[2] + lax.dot_general(
            tie(sent_parts[1]), grads_second, ROWS_DIMS, preferred_element_type=jnp.float32
        )
        return term, out_sum[0].step(tie)

    def down_first(tie, works):
        out_sum[0].keep(works[3][1])
        term = lax.dot_general(
            tie(weighted_first), cot_rows[:part_rows], ROWS_DIMS, preferred_element_type=jnp.float32
        )
        return term, out_sum[0].step(tie)

    def down_second(tie, works):
        out_sum[0].keep(works[4][1])
        term = works[4][0] + lax.dot_general(
            tie(weighted_second),
            cot_rows[part_rows:],
            ROWS_DIMS,
            preferred_element_type=jnp.float32,
        )
        return term, out_sum[0].step(tie)

    sent_grad, works = scatter_pairs(
        (back_first, back(grads_second)),
        (out_first, out_second, in_first, in_second, down_first, down_second),
    )
    out_sum = out_sum[0]
    out_sum.keep(works[5][1])
    in_term = works[3][0].astype(jnp.bfloat16)
    down_grad = (RESIDUAL * works[5][0]).reshape(own_experts, ff_here, model).transpose(1, 0, 2)
    upstream = cotangent[0].astype(jnp.float32)
    scaled_grad = sent_grad * gain_two
    middle_grad = (
        upstream
        + second_scale * scaled_grad
        - middle
        * second_scale**3
        * jnp.mean(scaled_grad * middle, axis=-1, keepdims=True)
    )
    gain_two_part = jnp.sum(sent_grad * middle * second_scale, axis=0)
    branch_grad = (RESIDUAL * middle_grad).astype(jnp.bfloat16)

    def out_step(tie, works):
        if works:
            out_sum.keep(works[-1])
        return out_sum.step(tie)

    branch_grad_all, works = dp_gather(branch_grad, (out_step, out_step, out_step, None))
    out_sum.keep(works[2])
    output = middle + RESIDUAL * out_sum.total()
    in_back = lax.all_to_all(
        after(in_term, branch_grad_all).reshape(n_dp, in_weight.shape[0], 2 * ff_cols),
        "dp",
        split_axis=0,
        concat_axis=0,
        tiled=True,
    )


    qkv_grad, normed_grad_part, gain_one_part = rear(
        branch_grad_all,
        o_w,
        queries,
        keys,
        vals,
        run_top,
        run_total,
        row_ids,
        col_ids,
        cosine,
        sine_table,
        qkv_w,
        group_tokens,
    )
    total = DpScatter(normed_grad_part)

    def weight_grads(tie):
        qkv_term = lax.dot_general(
            normed, tie(qkv_grad), ROWS_DIMS, preferred_element_type=jnp.float32
        )
        o_term = lax.dot_general(
            branch_grad_all, mixed_low, ROWS_DIMS, preferred_element_type=jnp.float32
        )
        grads = jnp.concatenate(
            [
                qkv_term,
                o_term,
                gain_one_part[0][:, None],
                gain_two_part[:, None],
                jnp.zeros((model, 126), jnp.float32),
            ],
            axis=1,
        ).astype(jnp.bfloat16)
        grads = grads.reshape(n_dp, n_ex, w_rows, -1)
        return [
            lax.dynamic_index_in_dim(grads, ex_index ^ k, 1, keepdims=False) for k in range(n_ex)
        ]

    def unpack_first(tie):
        return (
            tie(in_back)
            .reshape(n_dp, d_rows, 2, own_experts, ff_here)
            .transpose(3, 1, 2, 0, 4)
            .reshape(own_experts, d_rows, 2 * FF)
        )

    sums, (own_g, core_g, x_g, xc_g) = one_round(total.step(), (normed_grad_part,), weight_grads)
    total.keep(sums)
    core_pair = jnp.stack([core_g, xc_g])
    (sums, from_core), _ = one_round((total.step(), swap_core(core_pair)), (core_pair,))
    total.keep(sums)
    x_g = added(x_g, from_core[1])
    (sums, from_x), unpacked = one_round((total.step(), swap_x(x_g)), (x_g,), unpack_first)
    total.keep(sums)
    grads = lax.all_to_all(
        added(own_g, from_core[0], from_x), "dp", split_axis=0, concat_axis=0, tiled=True
    )
    (sums, grads), in_grad = one_round(
        (total.step(), grads),
        (from_x,),
        lambda tie: tie(unpacked).transpose(1, 0, 2).astype(jnp.float32),
    )
    total.keep(sums)
    grads = grads.astype(jnp.float32)
    normed_grad = total.total()

    def own_rows(begin, width):
        return grads[:, :, begin : begin + width].transpose(1, 0, 2).reshape(w_rows, n_dp * width)

    q_grad = own_rows(0, q_cols)
    k_grad = own_rows(q_cols, kv_cols)
    v_grad = own_rows(q_cols + kv_cols, kv_cols)
    o_grad = own_rows(qkv_cols, q_cols)
    gain_attn_grad = jnp.sum(grads[:, :, qkv_cols + q_cols], axis=0)
    gain_moe_grad = jnp.sum(grads[:, :, qkv_cols + q_cols + 1], axis=0)

    own_scale = lax.rsqrt(jnp.mean(inputs * inputs, axis=-1, keepdims=True) + EPSILON)
    scaled_one = normed_grad * gain_one
    input_grad = (
        middle_grad
        + own_scale * scaled_one
        - inputs * own_scale**3 * jnp.mean(scaled_one * inputs, axis=-1, keepdims=True)
    )
    return (
        output[None],
        input_grad[None],
        q_grad,
        k_grad,
        v_grad,
        o_grad,
        gain_attn_grad,
        gain_moe_grad,
        in_grad,
        down_grad,
    )


def per_layer(*args):
    return per_device(*args)


def solution(mesh):
    placed = (
        P("expert", "dp", None),
        P("expert", "dp", None),
        P("expert", None),
        P(),
        P("expert", "dp", None),
        P("expert", "dp", None),
        P(("dp", "expert"), None),
        P(("dp", "expert"), None),
        P(("dp", "expert"), None),
        P(("dp", "expert"), None),
        P(("dp", "expert")),
        P(("dp", "expert")),
        P("dp", "expert", None),
        P("dp", "expert", None),
    )
    n_dp = mesh.shape["dp"]
    split_heads = n_dp == 8 and mesh.shape["expert"] == 4
    return jax.shard_map(
        per_layer if split_heads else per_device_wide,
        mesh=mesh,
        in_specs=placed,
        out_specs=(
            P("expert", "dp", None),
            P("expert", "dp", None),
            P(("dp", "expert"), None),
            P(("dp", "expert"), None),
            P(("dp", "expert"), None),
            P(("dp", "expert"), None),
            P(("dp", "expert")),
            P(("dp", "expert")),
            P("dp", "expert", None),
            P("dp", "expert", None),
        ),
        check_vma=False,
    )
```

```python
import functools

import jax
import jax.numpy as jnp
from jax import lax
from jax.experimental import pallas as pl
from jax.experimental.pallas import tpu as pltpu
from jax.sharding import PartitionSpec as P


H = 24
KVH = 8
HD = 64
E = 40
FF = 512
TOPK = 8
CAP = 40


EPSILON = 1e-06
RESIDUAL = 0.22
SCORE_SCALE = 0.015625
THETA = 10000.0
NEGATIVE = -1e30
ROWS_DIMS = (((0,), (0,)), ((), ()))
COLS_DIMS = (((1,), (1,)), ((), ()))


def rms_scale(values, gain):
    return values * lax.rsqrt(jnp.mean(values * values, axis=-1, keepdims=True) + EPSILON) * gain


def rotate(values, cosine, sine_table):
    half_width = values.shape[-1] // 2
    turned = jnp.concatenate([-values[..., half_width:], values[..., :half_width]], axis=-1)
    return values * cosine + turned * sine_table


def turn_back(grads_in, cosine, sine_table):
    half_width = grads_in.shape[-1] // 2
    scaled = grads_in * sine_table
    return grads_in * cosine + jnp.concatenate(
        [scaled[..., half_width:], -scaled[..., :half_width]], axis=-1
    )


def silu_product(gate_in, up_in):
    return jax.nn.silu(gate_in) * up_in


def locate(where_at, seq_ends):
    return jnp.sum((where_at[:, None] >= seq_ends[None, :]).astype(jnp.int32), axis=-1)


def cut_block(source, begin_at, block_rows, heads):
    piece = lax.dynamic_slice_in_dim(source, begin_at, block_rows, 0)
    return piece.reshape(block_rows, heads, source.shape[1] // heads)


def group_chooser(wanted, carried, pieces, start):
    piece_rows = pieces[0].shape[0]
    inside = (wanted >= start) & (wanted < start + piece_rows)
    offset_at = jnp.clip(wanted, 0, piece_rows - 1)
    return tuple(
        (
            jnp.where(inside, lax.dynamic_slice_in_dim(member_piece, offset_at, 1, 0), member_carry)
            for member_piece, member_carry in zip(pieces, carried)
        )
    )


def per_device_wide(
    tokens,
    cotangent,
    lengths,
    deal,
    routes,
    gates,
    q_weight,
    k_weight,
    v_weight,
    o_weight,
    gain_attn,
    gain_moe,
    in_weight,
    down_weight,
):
    tok_rows = tokens.shape[1]
    model_width = tokens.shape[2]
    group_rows = tok_rows * lax.axis_size("dp")
    block_rows = min(512, group_rows)
    heads_per = H // KVH
    owner_index = lax.axis_index("expert")
    group_ids = jnp.arange(deal.shape[0], dtype=jnp.int32)
    wanted_in = jnp.sum(jnp.where(group_ids == owner_index, deal, 0))
    wanted_out = jnp.sum(jnp.where(deal == owner_index, group_ids, 0))
    dealt_tokens, dealt_cotangent = group_chooser(
        wanted_in,
        (jnp.zeros_like(tokens), jnp.zeros_like(cotangent)),
        (
            lax.all_gather(tokens, "expert", axis=0, tiled=True),
            lax.all_gather(cotangent, "expert", axis=0, tiled=True),
        ),
        jnp.int32(0),
    )
    inputs = dealt_tokens[0].astype(jnp.float32)
    q_full, k_full, v_full, o_full, gain_one, gain_two = (
        lax.all_gather(q_weight.astype(jnp.bfloat16), ("dp", "expert"), axis=0, tiled=True),
        lax.all_gather(k_weight.astype(jnp.bfloat16), ("dp", "expert"), axis=0, tiled=True),
        lax.all_gather(v_weight.astype(jnp.bfloat16), ("dp", "expert"), axis=0, tiled=True),
        lax.all_gather(o_weight.astype(jnp.bfloat16), ("dp", "expert"), axis=0, tiled=True),
        lax.all_gather(gain_attn.astype(jnp.bfloat16), ("dp", "expert"), axis=0, tiled=True),
        lax.all_gather(gain_moe.astype(jnp.bfloat16), ("dp", "expert"), axis=0, tiled=True),
    )
    gain_one = gain_one.astype(jnp.float32)
    gain_two = gain_two.astype(jnp.float32)
    seq_lengths = lengths[0]
    seq_ends = jnp.cumsum(seq_lengths)
    seq_starts = seq_ends - seq_lengths
    first_place = lax.axis_index("dp") * tok_rows
    places = first_place + jnp.arange(tok_rows, dtype=jnp.int32)
    member = (places[:, None] >= seq_starts[None, :]) & (places[:, None] < seq_ends[None, :])
    offsets = jnp.sum(jnp.where(member, places[:, None] - seq_starts[None, :], 0), axis=-1)
    frequency = THETA ** (-jnp.arange(HD // 2, dtype=jnp.float32) * 2.0 / HD)
    angles = offsets.astype(jnp.float32)[:, None] * frequency[None, :]
    angles = jnp.concatenate([angles, angles], axis=-1)[:, None, :]
    cosine = jnp.cos(angles)
    sine_table = jnp.sin(angles)
    query_seq = locate(places, seq_ends)
    seq_floor = jnp.sum(jnp.where(member[0], seq_starts, 0))
    low_block = seq_floor // block_rows
    high_block = (first_place + tok_rows - 1) // block_rows + 1
    normed = rms_scale(inputs, gain_one).astype(jnp.bfloat16)
    query_pre = jnp.dot(normed, q_full, preferred_element_type=jnp.float32).reshape(tok_rows, H, HD)
    key_pre = jnp.dot(normed, k_full, preferred_element_type=jnp.float32).reshape(tok_rows, KVH, HD)
    value_rows = jnp.dot(normed, v_full, preferred_element_type=jnp.float32).astype(jnp.bfloat16)
    queries = (
        rotate(query_pre, cosine, sine_table)
        .astype(jnp.bfloat16)
        .reshape(tok_rows, KVH, heads_per, HD)
    )
    key_rows = rotate(key_pre, cosine, sine_table).astype(jnp.bfloat16).reshape(tok_rows, KVH * HD)
    all_keys, all_values = (
        lax.all_gather(key_rows, "dp", axis=0, tiled=True),
        lax.all_gather(value_rows, "dp", axis=0, tiled=True),
    )

    def scores_for(block_id, key_block):
        begin_at = block_id * block_rows
        key_places = begin_at + jnp.arange(block_rows, dtype=jnp.int32)
        allowed = (query_seq[:, None] == locate(key_places, seq_ends)[None, :]) & (
            key_places[None, :] <= places[:, None]
        )
        raw_scores = SCORE_SCALE * jnp.einsum(
            "tkgd,skd->kgts", queries, key_block, preferred_element_type=jnp.float32
        )
        return (raw_scores, allowed)

    def stats_step(block_id, carried):
        run_top, run_total = carried
        key_block = cut_block(all_keys, block_id * block_rows, block_rows, KVH)
        raw_scores, allowed = scores_for(block_id, key_block)
        new_top = jnp.maximum(run_top, jnp.max(jnp.where(allowed, raw_scores, NEGATIVE), axis=-1))
        weights_now = jnp.where(allowed, jnp.exp(raw_scores - new_top[..., None]), 0.0)
        run_total = run_total * jnp.exp(run_top - new_top) + jnp.sum(weights_now, axis=-1)
        return (new_top, run_total)

    top_init = jnp.full((KVH, heads_per, tok_rows), NEGATIVE, jnp.float32)
    total_init = jnp.zeros((KVH, heads_per, tok_rows), jnp.float32)
    run_top, run_total = lax.fori_loop(low_block, high_block, stats_step, (top_init, total_init))
    log_total = run_top + jnp.log(run_total)

    def attn_probs(block_id, key_block):
        raw_scores, allowed = scores_for(block_id, key_block)
        return jnp.where(allowed, jnp.exp(raw_scores - log_total[..., None]), 0.0)

    def value_step(block_id, running):
        key_block = cut_block(all_keys, block_id * block_rows, block_rows, KVH)
        value_block = cut_block(all_values, block_id * block_rows, block_rows, KVH)
        chances = attn_probs(block_id, key_block).astype(jnp.bfloat16)
        return running + jnp.einsum(
            "kgts,skd->tkgd", chances, value_block, preferred_element_type=jnp.float32
        )

    mixed_init = jnp.zeros((tok_rows, KVH, heads_per, HD), jnp.float32)
    mixed_rows = lax.fori_loop(low_block, high_block, value_step, mixed_init).reshape(
        tok_rows, H * HD
    )
    mixed_low = mixed_rows.astype(jnp.bfloat16)
    branch = lax.dot_general(mixed_low, o_full, COLS_DIMS, preferred_element_type=jnp.float32)
    middle = inputs + RESIDUAL * branch
    sent_rows = rms_scale(middle, gain_two).astype(jnp.bfloat16)
    route_ids = routes[0].reshape(tok_rows * TOPK)
    matches = (route_ids[:, None] == jnp.arange(E, dtype=jnp.int32)[None, :]).astype(jnp.int32)
    slot_rank = jnp.sum(matches * jnp.cumsum(matches, axis=0), axis=-1) - 1
    slot_index = route_ids * CAP + slot_rank
    copies = jnp.repeat(sent_rows, TOPK, axis=0)
    outgoing = (
        jnp.zeros((E * CAP, model_width), jnp.bfloat16)
        .at[slot_index]
        .set(copies)
        .reshape(E, CAP, model_width)
    )
    arrived = lax.all_to_all(outgoing, "expert", split_axis=0, concat_axis=1, tiled=True)
    w_in, w_down = (
        lax.all_gather(in_weight.astype(jnp.bfloat16), "dp", axis=0, tiled=True),
        lax.all_gather(down_weight.astype(jnp.bfloat16), "dp", axis=0, tiled=True),
    )
    gate_up = jnp.einsum("erd,def->erf", arrived, w_in, preferred_element_type=jnp.float32)
    gate_part = gate_up[..., :FF]
    up_part = gate_up[..., FF:]
    hidden = silu_product(gate_part, up_part).astype(jnp.bfloat16)
    produced = jnp.einsum(
        "erf,fed->erd", hidden, w_down, preferred_element_type=jnp.float32
    ).astype(jnp.bfloat16)
    returned = lax.all_to_all(produced, "expert", split_axis=1, concat_axis=0, tiled=True).reshape(
        E * CAP, model_width
    )
    route_gates = gates[0].reshape(tok_rows * TOPK)
    picked = returned[slot_index].astype(jnp.float32) * route_gates[:, None]
    expert_sum = jnp.sum(picked.reshape(tok_rows, TOPK, model_width), axis=1)
    output = middle + RESIDUAL * expert_sum
    upstream = dealt_cotangent[0].astype(jnp.float32)
    spread = (RESIDUAL * route_gates[:, None] * jnp.repeat(upstream, TOPK, axis=0)).astype(
        jnp.bfloat16
    )
    back_out = (
        jnp.zeros((E * CAP, model_width), jnp.bfloat16)
        .at[slot_index]
        .set(spread)
        .reshape(E, CAP, model_width)
    )
    back_in = lax.all_to_all(back_out, "expert", split_axis=0, concat_axis=1, tiled=True)
    hidden_grad = jnp.einsum("erd,fed->erf", back_in, w_down, preferred_element_type=jnp.float32)
    down_term = jnp.einsum("erf,erd->fed", hidden, back_in, preferred_element_type=jnp.float32)
    ignored, silu_pull = jax.vjp(silu_product, gate_part, up_part)
    gate_grad, up_grad = silu_pull(hidden_grad)
    gate_up_grad = jnp.concatenate([gate_grad, up_grad], axis=-1).astype(jnp.bfloat16)
    in_term = jnp.einsum("erd,erf->def", arrived, gate_up_grad, preferred_element_type=jnp.float32)
    arrived_grad = jnp.einsum(
        "erf,def->erd", gate_up_grad, w_in, preferred_element_type=jnp.float32
    ).astype(jnp.bfloat16)
    sent_back = lax.all_to_all(
        arrived_grad, "expert", split_axis=1, concat_axis=0, tiled=True
    ).reshape(E * CAP, model_width)
    sent_grad = jnp.sum(
        sent_back[slot_index].astype(jnp.float32).reshape(tok_rows, TOPK, model_width), axis=1
    )
    in_grad, down_grad = (
        lax.psum_scatter(
            in_term.astype(jnp.bfloat16), "dp", scatter_dimension=0, tiled=True
        ).astype(jnp.float32),
        lax.psum_scatter(
            down_term.astype(jnp.bfloat16), "dp", scatter_dimension=0, tiled=True
        ).astype(jnp.float32),
    )
    ignored, second_pull = jax.vjp(rms_scale, middle, gain_two)
    middle_part, gain_two_term = second_pull(sent_grad)
    middle_grad = upstream + middle_part
    branch_grad = (RESIDUAL * middle_grad).astype(jnp.bfloat16)
    o_term = lax.dot_general(branch_grad, mixed_low, ROWS_DIMS, preferred_element_type=jnp.float32)
    grad_heads = jnp.dot(branch_grad, o_full, preferred_element_type=jnp.float32).astype(
        jnp.bfloat16
    )
    grad_heads = grad_heads.reshape(tok_rows, KVH, heads_per, HD)

    def delta_step(block_id, running):
        key_block = cut_block(all_keys, block_id * block_rows, block_rows, KVH)
        value_block = cut_block(all_values, block_id * block_rows, block_rows, KVH)
        chances = attn_probs(block_id, key_block)
        prob_grad = jnp.einsum(
            "tkgd,skd->kgts", grad_heads, value_block, preferred_element_type=jnp.float32
        )
        return running + jnp.sum(chances * prob_grad, axis=-1)

    row_delta = lax.fori_loop(
        low_block, high_block, delta_step, jnp.zeros((KVH, heads_per, tok_rows), jnp.float32)
    )

    def grad_step(block_id, carried):
        query_grad, key_buffer, value_buffer = carried
        begin_at = block_id * block_rows
        key_block = cut_block(all_keys, begin_at, block_rows, KVH)
        value_block = cut_block(all_values, begin_at, block_rows, KVH)
        chances = attn_probs(block_id, key_block)
        prob_grad = jnp.einsum(
            "tkgd,skd->kgts", grad_heads, value_block, preferred_element_type=jnp.float32
        )
        score_grad = (chances * (prob_grad - row_delta[..., None])).astype(jnp.bfloat16)
        query_grad = query_grad + SCORE_SCALE * jnp.einsum(
            "kgts,skd->tkgd", score_grad, key_block, preferred_element_type=jnp.float32
        )
        key_part = SCORE_SCALE * jnp.einsum(
            "kgts,tkgd->skd", score_grad, queries, preferred_element_type=jnp.float32
        )
        value_part = jnp.einsum(
            "kgts,tkgd->skd",
            chances.astype(jnp.bfloat16),
            grad_heads,
            preferred_element_type=jnp.float32,
        )
        key_buffer = lax.dynamic_update_slice_in_dim(
            key_buffer, key_part.reshape(block_rows, KVH * HD), begin_at, 0
        )
        value_buffer = lax.dynamic_update_slice_in_dim(
            value_buffer, value_part.reshape(block_rows, KVH * HD), begin_at, 0
        )
        return (query_grad, key_buffer, value_buffer)

    grad_init = (
        jnp.zeros((tok_rows, KVH, heads_per, HD), jnp.float32),
        jnp.zeros((group_rows, KVH * HD), jnp.float32),
        jnp.zeros((group_rows, KVH * HD), jnp.float32),
    )
    query_grad, key_buffer, value_buffer = lax.fori_loop(
        low_block, high_block, grad_step, grad_init
    )
    key_grad, value_grad = (
        lax.psum_scatter(
            key_buffer.astype(jnp.bfloat16), "dp", scatter_dimension=0, tiled=True
        ).astype(jnp.float32),
        lax.psum_scatter(
            value_buffer.astype(jnp.bfloat16), "dp", scatter_dimension=0, tiled=True
        ).astype(jnp.float32),
    )
    query_low = (
        turn_back(query_grad.reshape(tok_rows, H, HD), cosine, sine_table)
        .reshape(tok_rows, H * HD)
        .astype(jnp.bfloat16)
    )
    key_low = (
        turn_back(key_grad.reshape(tok_rows, KVH, HD), cosine, sine_table)
        .reshape(tok_rows, KVH * HD)
        .astype(jnp.bfloat16)
    )
    value_low = value_grad.astype(jnp.bfloat16)
    q_term = lax.dot_general(normed, query_low, ROWS_DIMS, preferred_element_type=jnp.float32)
    k_term = lax.dot_general(normed, key_low, ROWS_DIMS, preferred_element_type=jnp.float32)
    v_term = lax.dot_general(normed, value_low, ROWS_DIMS, preferred_element_type=jnp.float32)
    normed_grad = lax.dot_general(query_low, q_full, COLS_DIMS, preferred_element_type=jnp.float32)
    normed_grad = normed_grad + lax.dot_general(
        key_low, k_full, COLS_DIMS, preferred_element_type=jnp.float32
    )
    normed_grad = normed_grad + lax.dot_general(
        value_low, v_full, COLS_DIMS, preferred_element_type=jnp.float32
    )
    ignored, first_pull = jax.vjp(rms_scale, inputs, gain_one)
    input_part, gain_one_term = first_pull(normed_grad)
    input_grad = middle_grad + input_part
    q_grad, k_grad, v_grad, o_grad, gain_attn_grad, gain_moe_grad = (
        lax.psum_scatter(q_term, ("dp", "expert"), scatter_dimension=0, tiled=True),
        lax.psum_scatter(k_term, ("dp", "expert"), scatter_dimension=0, tiled=True),
        lax.psum_scatter(v_term, ("dp", "expert"), scatter_dimension=0, tiled=True),
        lax.psum_scatter(o_term, ("dp", "expert"), scatter_dimension=0, tiled=True),
        lax.psum_scatter(gain_one_term, ("dp", "expert"), scatter_dimension=0, tiled=True),
        lax.psum_scatter(gain_two_term, ("dp", "expert"), scatter_dimension=0, tiled=True),
    )
    given_output, given_input_grad = group_chooser(
        wanted_out,
        (
            jnp.zeros((1, tok_rows, model_width), jnp.float32),
            jnp.zeros((1, tok_rows, model_width), jnp.float32),
        ),
        (
            lax.all_gather(output[None].astype(jnp.bfloat16), "expert", axis=0, tiled=True).astype(
                jnp.float32
            ),
            lax.all_gather(
                input_grad[None].astype(jnp.bfloat16), "expert", axis=0, tiled=True
            ).astype(jnp.float32),
        ),
        jnp.int32(0),
    )
    return (
        given_output,
        given_input_grad,
        q_grad,
        k_grad,
        v_grad,
        o_grad,
        gain_attn_grad,
        gain_moe_grad,
        in_grad,
        down_grad,
    )


SWAP_Y = [(i, i ^ 1) for i in range(8)]
SWAP_CORE = [(j, j ^ 1) for j in range(4)]
SWAP_X = [(j, j ^ 2) for j in range(4)]


def along_z(moves):
    return [(2 * s + y, 2 * d + y) for s, d in moves for y in range(2)]


Z_NEAR = along_z([(0, 1), (1, 0), (2, 3), (3, 2)])
Z_MIDDLE = along_z([(1, 2), (2, 1)])
Z_OUT = along_z([(1, 0), (2, 3)])
Z_IN = along_z([(0, 1), (3, 2)])
SLOT_Z = ((0, 1, 2, 3), (1, 0, 3, 2), (2, 2, 1, 1), (3, 3, 0, 0))


def over_dp(piece, moves):
    return lax.ppermute(piece, "dp", moves)


def over_expert(piece, moves):
    return lax.ppermute(piece, "expert", moves)


def added(first, *others):
    total = first.astype(jnp.float32)
    for other in others:
        total = total + other.astype(jnp.float32)
    return total.astype(jnp.bfloat16)


def halves(array):
    half = array.shape[0] // 2
    return array[:half], array[half:]


def joined(*arrays):
    return jnp.concatenate(arrays, axis=0)


def one_round(outs, ins, cover=None):
    if cover is None:
        return lax.optimization_barrier(outs), None
    return lax.optimization_barrier((outs, cover(lambda x: after(x, *ins))))


def swap_y(value):
    return over_dp(value, SWAP_Y)


def swap_x(value):
    return over_expert(value, SWAP_X)


def swap_core(value):
    return over_expert(value, SWAP_CORE)


def dp_gather(piece, covers=(None, None, None, None)):
    works = []

    def run(outs, ins, cover):
        outs, work = one_round(outs, ins, cover and (lambda tie: cover(tie, works)))
        works.append(work)
        return outs

    near, middle, y0 = run(
        (over_dp(piece, Z_NEAR), over_dp(piece, Z_MIDDLE), swap_y(piece)), (piece,), covers[0]
    )
    far, out1, y1 = run(
        (over_dp(near, Z_MIDDLE), over_dp(middle, Z_OUT), swap_y(near)), (near, middle), covers[1]
    )
    third = middle + out1
    out2, y2 = run((over_dp(far, Z_OUT), swap_y(third)), (far, third), covers[2])
    fourth = far + out2
    y3 = run(swap_y(fourth), (fourth,), covers[3])
    return joined(piece, y0, near, y1, third, y2, fourth, y3), works


class DpScatter:
    def __init__(self, total):
        blocks = jnp.split(total, 8, axis=0)
        self.own, self.sent = blocks[0::2], blocks[1::2]
        self.round = 0

    def step(self, tie=lambda v: v):
        self.round += 1
        if self.round == 1:
            self.z = swap_y(tie(self.sent[3]))
        elif self.round == 2:
            self.fourth = added(self.own[3], self.z)
            self.z = over_dp(tie(self.fourth), Z_IN), swap_y(self.sent[2])
        elif self.round == 3:
            fourth = added(self.fourth, self.z[0])
            self.third = added(self.own[2], self.z[1])
            self.z = (
                over_dp(tie(fourth), Z_MIDDLE),
                over_dp(self.third, Z_IN),
                swap_y(self.sent[1]),
            )
        else:
            third = added(self.third, self.z[1])
            near = added(self.own[1], self.z[2], self.z[0])
            self.z = (
                over_dp(tie(near), Z_NEAR),
                over_dp(third, Z_MIDDLE),
                swap_y(self.sent[0]),
            )
        return self.z

    def keep(self, values):
        self.z = values

    def total(self):
        total = self.own[0].astype(jnp.float32)
        for value in self.z:
            total = total + value.astype(jnp.float32)
        return total


def gather_beside_sum(piece, attention):
    (near, middle, y0), attended = one_round(
        (over_dp(piece, Z_NEAR), over_dp(piece, Z_MIDDLE), swap_y(piece)), (piece,), attention
    )
    part = attended[-1]
    pair0 = joined(piece, y0)
    total = DpScatter(part)
    (far, out1, y1, x0, sums), _ = one_round(
        (
            over_dp(near, Z_MIDDLE),
            over_dp(middle, Z_OUT),
            swap_y(near),
            swap_x(pair0),
            total.step(),
        ),
        (near, middle, pair0),
    )
    total.keep(sums)
    third = middle + out1
    pair1 = joined(near, y1)
    (out2, y2, x1, sums), _ = one_round(
        (over_dp(far, Z_OUT), swap_y(third), swap_x(pair1), total.step()), (far, third, pair1)
    )
    total.keep(sums)
    fourth = far + out2
    pair2 = joined(third, y2)
    (y3, x2, sums), _ = one_round((swap_y(fourth), swap_x(pair2), total.step()), (fourth, pair2))
    total.keep(sums)
    pair3 = joined(fourth, y3)
    (x3, sums), _ = one_round((swap_x(pair3), total.step()), (pair3,))
    total.keep(sums)
    here = joined(pair0, x0, pair1, x1, pair2, x2, pair3, x3)
    return joined(here, swap_core(here)), total.total(), attended


def gather_pairs(piece, covers):
    works = []

    def run(outs, ins, cover=None):
        outs, work = one_round(outs, ins, cover and (lambda tie: cover(tie, works)))
        works.append(work)
        return outs

    near, middle = run(
        (over_dp(piece, Z_NEAR), over_dp(piece, Z_MIDDLE)), (piece,), covers[0]
    )

    def split(first, second):
        (ft, fl), (st, sl) = halves(first), halves(second)
        return joined(ft, st), joined(fl, sl)

    top, low = split(piece, near)
    far, out1, y_top, x_low = run(
        (over_dp(near, Z_MIDDLE), over_dp(middle, Z_OUT), swap_y(top), swap_x(low)),
        (top, low),
        covers[1],
    )
    third = middle + out1
    top, low = joined(top, y_top), joined(low, x_low)
    out2, x_top, y_low = run(
        (over_dp(far, Z_OUT), swap_x(top), swap_y(low)), (top, low), covers[2]
    )
    here = joined(top, x_top, low, y_low)
    top, low = split(third, far + out2)
    y_top, x_low, there = run(
        (swap_y(top), swap_x(low), swap_core(here)), (top, low, here), covers[3]
    )
    first = joined(here, there)
    top, low = joined(top, y_top), joined(low, x_low)
    x_top, y_low = run(
        (swap_x(top), swap_y(low)), (top, low), lambda tie, works: covers[4](tie, works, first)
    )
    here = joined(top, x_top, low, y_low)
    there = run(swap_core(here), (here,), covers[5])
    return (first, joined(here, there)), works


class PairScatter:
    def __init__(self, totals):
        (self.m0, self.o0), (self.m1, self.o1) = [halves(t) for t in totals]
        self.round = 0

    def across(self, parts, first, second, tie):
        (ta, tb), (la, lb) = [halves(p) for p in parts]
        return (ta, la), (first(tie(tb)), second(tie(lb)))

    def both(self, kept, moved):
        return [added(k, m) for k, m in zip(kept, moved)]

    def step(self, tie=lambda v: v):
        self.round += 1
        if self.round == 1:
            self.moved = swap_core(tie(self.o1))
        elif self.round == 2:
            parts = halves(added(self.m1, self.moved))
            self.kept1, moved1 = self.across(parts, swap_x, swap_y, tie)
            self.moved = moved1, swap_core(tie(self.o0))
        elif self.round == 3:
            parts1 = self.both(self.kept1, self.moved[0])
            parts0 = halves(added(self.m0, self.moved[1]))
            self.kept1, moved1 = self.across(parts1, swap_y, swap_x, tie)
            self.kept0, moved0 = self.across(parts0, swap_x, swap_y, tie)
            self.moved = moved1, moved0
        elif self.round == 4:
            (third_top, fourth_top), (third_low, fourth_low) = [
                halves(p) for p in self.both(self.kept1, self.moved[0])
            ]
            self.third, self.fourth = joined(third_top, third_low), joined(fourth_top, fourth_low)
            parts0 = self.both(self.kept0, self.moved[1])
            self.kept0, moved0 = self.across(parts0, swap_y, swap_x, tie)
            self.moved = moved0, over_dp(tie(self.fourth), Z_IN)
        elif self.round == 5:
            (own_top, near_top), (own_low, near_low) = [
                halves(p) for p in self.both(self.kept0, self.moved[0])
            ]
            self.own, self.near = joined(own_top, own_low), joined(near_top, near_low)
            fourth = added(self.fourth, self.moved[1])
            self.moved = over_dp(tie(fourth), Z_MIDDLE), over_dp(tie(self.third), Z_IN)
        else:
            near, third = added(self.near, self.moved[0]), added(self.third, self.moved[1])
            self.moved = over_dp(tie(near), Z_NEAR), over_dp(tie(third), Z_MIDDLE)
        return self.moved

    def keep(self, values):
        self.moved = values

    def total(self):
        total = self.own.astype(jnp.float32)
        for value in self.moved:
            total = total + value.astype(jnp.float32)
        return total


def scatter_pairs(totals, covers):
    works = []
    scatter = PairScatter(totals)
    for cover in covers:
        outs = scatter.step()
        outs, work = one_round(outs, (), cover and (lambda tie: cover(tie, works)))
        scatter.keep(outs)
        works.append(work)
    return scatter.total(), works


def far_order(ex_index, dealt_of):
    r = jnp.arange(64, dtype=jnp.int32)
    pair, core, half, outer, inner = r // 32, r // 16 % 2, r // 8 % 2, r // 4 % 2, r // 2 % 2
    slot = 2 * pair + r % 2
    flip_y = jnp.where(half == 0, inner, outer)
    flip_x = jnp.where(half == 0, outer, inner)

    def place(flip):
        return ((flip % 2 * 4 + slot) * 4 + flip // 2 * 2 + flip_y) * 2 + half

    flip = 2 * flip_x + core
    return place(flip), place(jnp.take(dealt_of, ex_index ^ flip) ^ ex_index)


def take_kernel(index_ref, *refs, at_once):
    count = len(refs) // (at_once + 1)
    for p in range(count):
        target = refs[count * at_once + p]
        rows = target.shape[0] // at_once
        for k in range(at_once):
            target[k * rows : (k + 1) * rows, :] = refs[p * at_once + k][...]


def take_blocks(index, array, parts, block):
    at_once = 8
    steps = index.shape[1] // at_once

    def source(row, column, k):
        return lambda i, idx: (idx[row, at_once * i + k], column)

    return pl.pallas_call(
        functools.partial(take_kernel, at_once=at_once),
        out_shape=[
            jax.ShapeDtypeStruct((index.shape[1] * block, width), array.dtype)
            for row, column, width in parts
        ],
        grid_spec=pltpu.PrefetchScalarGridSpec(
            num_scalar_prefetch=1,
            grid=(steps,),
            in_specs=[
                pl.BlockSpec((block, width), source(row, column, k))
                for row, column, width in parts
                for k in range(at_once)
            ],
            out_specs=[
                pl.BlockSpec((at_once * block, width), lambda i, idx: (i, 0))
                for row, column, width in parts
            ],
        ),
        name="take_blocks",
    )(index, *([array] * (at_once * len(parts))))


def attend_masks(row_ids, col_ids, begin, rows):
    seq_rows = row_ids[pl.ds(begin, rows), 0:1]
    place_rows = row_ids[pl.ds(begin, rows), 1:2]
    return (seq_rows == col_ids[0:1, :]) & (col_ids[1:2, :] <= place_rows)


def front_kernel(
    x_ref, gain_ref, w_ref, ow_ref, cos_ref, sin_ref, row_ids, col_ids,
    normed_ref, q_ref, k_ref, v_ref, o_ref, top_ref, total_ref, part_ref, *, heads, rows
):
    q_cols = heads * HD
    steps = x_ref.shape[0] // rows

    def project(i, carry):
        here = pl.ds(pl.multiple_of(i * rows, rows), rows)
        inputs = x_ref[here, :].astype(jnp.float32)
        scale = lax.rsqrt(jnp.mean(inputs * inputs, axis=-1, keepdims=True) + EPSILON)
        normed = (inputs * scale * gain_ref[...]).astype(jnp.bfloat16)
        normed_ref[here, :] = normed
        qkv = jnp.dot(normed, w_ref[...], preferred_element_type=jnp.float32)
        cosine, sine = cos_ref[here, :], sin_ref[here, :]
        turned = []
        for h in range(heads + 1):
            turned.append(rotate(qkv[:, h * HD : (h + 1) * HD], cosine, sine))
        q_ref[here, :] = jnp.concatenate(turned[:heads], axis=1).astype(jnp.bfloat16)
        k_ref[here, :] = turned[heads].astype(jnp.bfloat16)
        v_ref[here, :] = qkv[:, q_cols + HD :].astype(jnp.bfloat16)
        return carry

    lax.fori_loop(0, steps, project, 0)
    keys, vals = k_ref[...], v_ref[...]

    def step(i, carry):
        begin = pl.multiple_of(i * rows, rows)
        here = pl.ds(begin, rows)
        allowed = attend_masks(row_ids, col_ids, begin, rows)
        outs, tops, totals = [], [], []
        for h in range(heads):
            scores = SCORE_SCALE * lax.dot_general(
                q_ref[here, h * HD : (h + 1) * HD],
                keys,
                COLS_DIMS,
                preferred_element_type=jnp.float32,
            )
            scores = jnp.where(allowed, scores, NEGATIVE)
            top = jnp.max(scores, axis=-1, keepdims=True)
            weights = jnp.exp(scores - top)
            total = jnp.sum(weights, axis=-1, keepdims=True)
            chances = (weights / total).astype(jnp.bfloat16)
            outs.append(jnp.dot(chances, vals, preferred_element_type=jnp.float32))
            tops.append(top)
            totals.append(total)
        mixed = jnp.concatenate(outs, axis=1).astype(jnp.bfloat16)
        o_ref[here, :] = mixed
        top_ref[here, :] = jnp.concatenate(tops, axis=1)
        total_ref[here, :] = jnp.concatenate(totals, axis=1)
        part_ref[here, :] = lax.dot_general(
            mixed, ow_ref[...], COLS_DIMS, preferred_element_type=jnp.float32
        ).astype(jnp.bfloat16)
        return carry

    lax.fori_loop(0, steps, step, 0)


def front(inputs, gain, qkv_w, o_w, cosine, sine, row_ids, col_ids):
    rows, model = inputs.shape
    heads = H // KVH
    low = jnp.bfloat16
    return pl.pallas_call(
        functools.partial(front_kernel, heads=heads, rows=min(256, rows)),
        out_shape=[
            jax.ShapeDtypeStruct((rows, model), low),
            jax.ShapeDtypeStruct((rows, heads * HD), low),
            jax.ShapeDtypeStruct((rows, HD), low),
            jax.ShapeDtypeStruct((rows, HD), low),
            jax.ShapeDtypeStruct((rows, heads * HD), low),
            jax.ShapeDtypeStruct((rows, heads), jnp.float32),
            jax.ShapeDtypeStruct((rows, heads), jnp.float32),
            jax.ShapeDtypeStruct((rows, model), low),
        ],
        name="front",
    )(inputs, gain, qkv_w, o_w, cosine, sine, row_ids, col_ids)


def rear_kernel(
    g_ref, ow_ref, q_ref, k_ref, v_ref, top_ref, total_ref, row_ids, col_ids, cos_ref, sin_ref,
    w_ref, x_ref, qkvg_ref, part_ref, gain_ref, dk_ref, dv_ref, *, heads, rows
):
    q_cols = heads * HD
    steps = x_ref.shape[0] // rows
    dk_ref[...] = jnp.zeros_like(dk_ref)
    dv_ref[...] = jnp.zeros_like(dv_ref)
    gain_ref[...] = jnp.zeros_like(gain_ref)
    keys, vals = k_ref[...], v_ref[...]

    def step(i, carry):
        begin = pl.multiple_of(i * rows, rows)
        here = pl.ds(begin, rows)
        allowed = attend_masks(row_ids, col_ids, begin, rows)
        grads = jnp.dot(g_ref[here, :], ow_ref[...], preferred_element_type=jnp.float32).astype(
            jnp.bfloat16
        )
        cosine, sine = cos_ref[here, :], sin_ref[here, :]
        pulled = []
        key_grad = jnp.zeros((k_ref.shape[0], HD), jnp.float32)
        value_grad = jnp.zeros((k_ref.shape[0], HD), jnp.float32)
        for h in range(heads):
            query = q_ref[here, h * HD : (h + 1) * HD]
            grad = grads[:, h * HD : (h + 1) * HD]
            scores = SCORE_SCALE * lax.dot_general(
                query, keys, COLS_DIMS, preferred_element_type=jnp.float32
            )
            scores = jnp.where(allowed, scores, NEGATIVE)
            weights = jnp.exp(scores - top_ref[here, h : h + 1])
            chances = weights / total_ref[here, h : h + 1]
            prob_grad = lax.dot_general(grad, vals, COLS_DIMS, preferred_element_type=jnp.float32)
            delta = jnp.sum(chances * prob_grad, axis=-1, keepdims=True)
            score_grad = (chances * (prob_grad - delta)).astype(jnp.bfloat16)
            query_grad = SCORE_SCALE * jnp.dot(
                score_grad, keys, preferred_element_type=jnp.float32
            )
            pulled.append(turn_back(query_grad, cosine, sine))
            key_grad += lax.dot_general(
                score_grad, query, ROWS_DIMS, preferred_element_type=jnp.float32
            )
            value_grad += lax.dot_general(
                chances.astype(jnp.bfloat16), grad, ROWS_DIMS, preferred_element_type=jnp.float32
            )
        qkvg_ref[here, 0:q_cols] = jnp.concatenate(pulled, axis=1).astype(jnp.bfloat16)
        dk_ref[...] += SCORE_SCALE * key_grad
        dv_ref[...] += value_grad
        return carry

    lax.fori_loop(0, steps, step, 0)

    def finish(i, carry):
        here = pl.ds(pl.multiple_of(i * rows, rows), rows)
        key_low = turn_back(dk_ref[here, :], cos_ref[here, :], sin_ref[here, :])
        qkvg_ref[here, q_cols:] = jnp.concatenate([key_low, dv_ref[here, :]], axis=1).astype(
            jnp.bfloat16
        )
        part = lax.dot_general(
            qkvg_ref[here, :], w_ref[...], COLS_DIMS, preferred_element_type=jnp.float32
        )
        part_ref[here, :] = part.astype(jnp.bfloat16)
        inputs = x_ref[here, :].astype(jnp.float32)
        scale = lax.rsqrt(jnp.mean(inputs * inputs, axis=-1, keepdims=True) + EPSILON)
        gain_ref[...] += jnp.sum(part * inputs * scale, axis=0, keepdims=True)
        return carry

    lax.fori_loop(0, steps, finish, 0)


def rear(grads_in, o_w, queries, keys, vals, top, total, row_ids, col_ids, cosine, sine, qkv_w, x):
    rows, model = x.shape
    heads = H // KVH
    return pl.pallas_call(
        functools.partial(rear_kernel, heads=heads, rows=min(256, rows)),
        out_shape=[
            jax.ShapeDtypeStruct((rows, qkv_w.shape[1]), jnp.bfloat16),
            jax.ShapeDtypeStruct((rows, model), jnp.bfloat16),
            jax.ShapeDtypeStruct((1, model), jnp.float32),
        ],
        scratch_shapes=[
            pltpu.VMEM((rows, HD), jnp.float32),
            pltpu.VMEM((rows, HD), jnp.float32),
        ],
        name="rear",
    )(grads_in, o_w, queries, keys, vals, top, total, row_ids, col_ids, cosine, sine, qkv_w, x)


def pack_kernel(x_ref, o_ref, *, width):
    experts = x_ref.shape[0]
    half = x_ref.shape[2] // 2
    for i in range(o_ref.shape[0]):
        for g in range(2):
            at = g * half + i * width
            row = jnp.concatenate([x_ref[e, :, at : at + width] for e in range(experts)], axis=1)
            o_ref[i, :, g * experts * width : (g + 1) * experts * width] = row.astype(jnp.bfloat16)


def pack_weights(weight, devices, rows=48):
    experts, d_rows, columns = weight.shape
    width = columns // 2 // devices
    return pl.pallas_call(
        functools.partial(pack_kernel, width=width),
        out_shape=jax.ShapeDtypeStruct((devices, d_rows, 2 * experts * width), jnp.bfloat16),
        grid=(d_rows // rows,),
        in_specs=[pl.BlockSpec((experts, rows, columns), lambda r: (0, r, 0))],
        out_specs=pl.BlockSpec((devices, rows, 2 * experts * width), lambda r: (0, r, 0)),
        name="pack_weights",
    )(weight)


def unpack_kernel(x_ref, o_ref, *, width):
    experts = o_ref.shape[0]
    half = o_ref.shape[2] // 2
    for e in range(experts):
        for g in range(2):
            at = (g * experts + e) * width
            row = jnp.concatenate(
                [x_ref[i, :, at : at + width] for i in range(x_ref.shape[0])], axis=1
            )
            o_ref[e, :, g * half : (g + 1) * half] = row.astype(jnp.float32)


def unpack_grads(moved, experts, rows=48):
    devices, d_rows, columns = moved.shape
    width = columns // 2 // experts
    return pl.pallas_call(
        functools.partial(unpack_kernel, width=width),
        out_shape=jax.ShapeDtypeStruct((experts, d_rows, 2 * devices * width), jnp.float32),
        grid=(d_rows // rows,),
        in_specs=[pl.BlockSpec((devices, rows, columns), lambda r: (0, r, 0))],
        out_specs=pl.BlockSpec((experts, rows, 2 * devices * width), lambda r: (0, r, 0)),
        name="unpack_grads",
    )(moved)


def after(value, *earlier):
    return lax.optimization_barrier((value, *earlier))[0]


def rounded(values):
    return lax.reduce_precision(values, 8, 7)


def rope_parts(seq_lengths, places):
    seq_ends = jnp.cumsum(seq_lengths)
    seq_starts = seq_ends - seq_lengths
    member = (places[:, None] >= seq_starts[None, :]) & (places[:, None] < seq_ends[None, :])
    offsets = jnp.sum(jnp.where(member, places[:, None] - seq_starts[None, :], 0), axis=-1)
    frequency = THETA ** (-jnp.arange(HD // 2, dtype=jnp.float32) * 2.0 / HD)
    angles = offsets.astype(jnp.float32)[:, None] * frequency[None, :]
    angles = jnp.concatenate([angles, angles], axis=-1)[:, None, :]
    seq_ids = locate(places, seq_ends)
    return seq_ids, jnp.cos(angles), jnp.sin(angles)


def per_device(
    tokens,
    cotangent,
    lengths,
    deal,
    routes,
    gates,
    q_weight,
    k_weight,
    v_weight,
    o_weight,
    gain_attn,
    gain_moe,
    in_weight,
    down_weight,
):
    n_dp = lax.axis_size("dp")
    n_ex = lax.axis_size("expert")
    tok_rows = tokens.shape[1]
    model = tokens.shape[2]
    kv_here = KVH // n_dp
    heads_per = H // KVH
    q_cols = kv_here * heads_per * HD
    kv_cols = kv_here * HD
    own_experts = in_weight.shape[1]
    ff_here = FF // n_dp
    ff_cols = own_experts * ff_here
    w_rows = q_weight.shape[0]
    ex_index = lax.axis_index("expert")
    group_ids = jnp.arange(deal.shape[0], dtype=jnp.int32)
    dealt_of = jnp.argmax((deal[None, :] == group_ids[:, None]).astype(jnp.int32), axis=1)
    own_dealt = jnp.sum(jnp.where(deal == ex_index, group_ids, 0))

    def by_owner(weight):
        return weight.astype(jnp.bfloat16).reshape(w_rows, n_dp, weight.shape[1] // n_dp)

    length_parts = jnp.stack([lengths[0] // 128, lengths[0] % 128]).reshape(-1).astype(jnp.bfloat16)
    n_len = length_parts.shape[0]
    extra = jnp.concatenate(
        [
            gain_attn.astype(jnp.bfloat16)[:, None],
            gain_moe.astype(jnp.bfloat16)[:, None],
            jnp.broadcast_to(length_parts[None, :], (w_rows, n_len)),
            jnp.zeros((w_rows, 126 - n_len), jnp.bfloat16),
        ],
        axis=1,
    )

    def pack_in(tie):
        return pack_weights(tie(in_weight).transpose(1, 0, 2), n_dp)

    attn_out = jnp.concatenate(
        [
            by_owner(q_weight),
            by_owner(k_weight),
            by_owner(v_weight),
            by_owner(o_weight),
            jnp.broadcast_to(extra[:, None, :], (w_rows, n_dp, 128)),
        ],
        axis=2,
    ).transpose(1, 0, 2)
    attn_in = lax.all_to_all(attn_out, "dp", split_axis=0, concat_axis=0, tiled=True)

    group_tokens, (_, in_out, _, _) = dp_gather(
        tokens[0], (None, lambda tie, works: pack_in(tie), None, None)
    )
    attn_two = jnp.stack([attn_in, swap_core(attn_in)])
    attn_four = joined(attn_two, swap_x(attn_two))
    in_w = lax.all_to_all(
        after(in_out, group_tokens, attn_in), "dp", split_axis=0, concat_axis=0, tiled=True
    ).reshape(model, 2 * ff_cols)
    z_own, y_own = lax.axis_index("dp") // 2, lax.axis_index("dp") % 2
    slot_dp = 2 * jnp.asarray(SLOT_Z, jnp.int32)[:, z_own]
    block_dp = jnp.stack([slot_dp + y_own, slot_dp + 1 - y_own], axis=1).reshape(-1)
    places = (block_dp[:, None] * tok_rows + jnp.arange(tok_rows, dtype=jnp.int32)).reshape(-1)


    def of_expert(index):
        return lax.dynamic_index_in_dim(attn_four, index ^ ex_index, 0, keepdims=False)

    attn_all = jnp.stack([of_expert(e) for e in range(n_ex)])
    attn_w = attn_all.transpose(1, 0, 2, 3).reshape(model, -1)
    qkv_cols = q_cols + 2 * kv_cols
    qkv_w = attn_w[:, :qkv_cols]
    o_w = attn_w[:, qkv_cols : qkv_cols + q_cols]
    side = attn_w[:, qkv_cols + q_cols :]
    gain_one = side[:, 0].astype(jnp.float32)
    gain_two = side[:, 1].astype(jnp.float32)
    own_parts = of_expert(own_dealt)[
        0, 0, qkv_cols + q_cols + 2 : qkv_cols + q_cols + 2 + n_len
    ].astype(jnp.int32)
    seq_lengths = own_parts[: n_len // 2] * 128 + own_parts[n_len // 2 :]

    down_w = down_weight.astype(jnp.bfloat16).transpose(1, 0, 2).reshape(ff_cols, model)

    every = jnp.arange(E, dtype=jnp.int32)[None, :]
    dense = sum(
        jnp.where(routes[0][:, k : k + 1] == every, gates[0][:, k : k + 1], 0.0)
        for k in range(TOPK)
    )
    dense_top = rounded(dense)
    dense_mid = rounded(dense - dense_top)
    meta = jnp.concatenate(
        [
            dense_top,
            dense_mid,
            dense - dense_top - dense_mid,
            jnp.zeros((tok_rows, 128 - 3 * E), jnp.float32),
        ],
        axis=1,
    ).astype(jnp.bfloat16)

    seq_ids, cosine, sine_table = rope_parts(seq_lengths, places)
    cosine, sine_table = cosine[:, 0], sine_table[:, 0]
    row_ids = jnp.stack([seq_ids, places], axis=1)
    col_ids = jnp.stack([seq_ids, places], axis=0)

    def attention(tie):
        return front(
            tie(group_tokens), gain_one[None], qkv_w, o_w, cosine, sine_table, row_ids, col_ids
        )

    cot_out = after(jnp.concatenate([cotangent[0], meta], axis=1), group_tokens)
    cot_all, branch, attended = gather_beside_sum(cot_out, attention)
    normed, queries, keys, vals, mixed_low, run_top, run_total, _ = attended
    rows_from, meta_from = far_order(ex_index, dealt_of)
    inputs = tokens[0].astype(jnp.float32)
    middle = inputs + RESIDUAL * branch
    second_scale = lax.rsqrt(jnp.mean(middle * middle, axis=-1, keepdims=True) + EPSILON)
    sent_rows = (middle * second_scale * gain_two).astype(jnp.bfloat16)
    sent_rows = after(sent_rows, in_w, cot_all)
    part_rows = 16 * tok_rows

    def order_rows(tie, works):
        return take_blocks(
            jnp.stack([rows_from, meta_from]),
            tie(cot_all),
            [(0, 0, model), (1, model // 128, 128)],
            tok_rows // 2,
        )

    def pull(tie, works):
        return lax.dot_general(
            tie(works[0][0]), down_w, COLS_DIMS, preferred_element_type=jnp.float32
        )

    def spread_gates(tie, works):
        column = jnp.arange(128, dtype=jnp.int32)[:, None]
        owner = ex_index * own_experts + jnp.arange(ff_cols, dtype=jnp.int32)[None, :] // ff_here
        spread = ((column % E == owner) & (column < 3 * E)).astype(jnp.bfloat16)
        return jnp.dot(tie(works[0][1]), spread, preferred_element_type=jnp.float32)

    def up(sent):
        return jnp.dot(sent, in_w, preferred_element_type=jnp.float32)

    def down(gate_up, gates_here, pulled_here):
        gate_part = gate_up[:, :ff_cols]
        up_part = gate_up[:, ff_cols:]
        sigma = jax.nn.sigmoid(gate_part)
        silu = gate_part * sigma
        hidden = (silu * up_part).astype(jnp.bfloat16).astype(jnp.float32)
        weighted_here = (gates_here * hidden).astype(jnp.bfloat16)
        hidden_grad = RESIDUAL * gates_here * pulled_here
        gate_grad = hidden_grad * up_part * (sigma * (1.0 + gate_part * (1.0 - sigma)))
        up_grad = hidden_grad * silu
        grads_here = jnp.concatenate([gate_grad, up_grad], axis=1).astype(jnp.bfloat16)
        return weighted_here, grads_here

    def back(grads_here):
        return lax.dot_general(
            grads_here, in_w, COLS_DIMS, preferred_element_type=jnp.float32
        ).astype(jnp.bfloat16)

    def of_part(number, works, gate_up):
        rows_here = slice(number * part_rows, (number + 1) * part_rows)
        return down(gate_up, works[2][rows_here], works[1][rows_here])

    def first_up(tie, works, sent):
        return up(tie(sent))

    def first_down(tie, works):
        weighted_here, grads_here = of_part(0, works, tie(works[4]))
        return weighted_here, grads_here, back(grads_here)

    sent_parts, works = gather_pairs(
        sent_rows, (order_rows, pull, spread_gates, None, first_up, first_down)
    )
    cot_rows = works[0][0]
    weighted_first, grads_first, back_first = works[5]
    weighted_second, grads_second = of_part(1, works, up(sent_parts[1]))

    def out_first(tie, works):
        return jnp.dot(tie(weighted_first), down_w, preferred_element_type=jnp.float32).astype(
            jnp.bfloat16
        )

    def out_second(tie, works):
        return jnp.dot(tie(weighted_second), down_w, preferred_element_type=jnp.float32).astype(
            jnp.bfloat16
        )

    def in_first(tie, works):
        return lax.dot_general(
            tie(sent_parts[0]), grads_first, ROWS_DIMS, preferred_element_type=jnp.float32
        )

    out_sum = []

    def in_second(tie, works):
        out_sum.append(PairScatter(works[:2]))
        term = works[2] + lax.dot_general(
            tie(sent_parts[1]), grads_second, ROWS_DIMS, preferred_element_type=jnp.float32
        )
        return term, out_sum[0].step(tie)

    def down_first(tie, works):
        out_sum[0].keep(works[3][1])
        term = lax.dot_general(
            tie(weighted_first), cot_rows[:part_rows], ROWS_DIMS, preferred_element_type=jnp.float32
        )
        return term, out_sum[0].step(tie)

    def down_second(tie, works):
        out_sum[0].keep(works[4][1])
        term = works[4][0] + lax.dot_general(
            tie(weighted_second),
            cot_rows[part_rows:],
            ROWS_DIMS,
            preferred_element_type=jnp.float32,
        )
        return term, out_sum[0].step(tie)

    sent_grad, works = scatter_pairs(
        (back_first, back(grads_second)),
        (out_first, out_second, in_first, in_second, down_first, down_second),
    )
    out_sum = out_sum[0]
    out_sum.keep(works[5][1])
    in_term = works[3][0].astype(jnp.bfloat16)
    down_grad = (RESIDUAL * works[5][0]).reshape(own_experts, ff_here, model).transpose(1, 0, 2)
    upstream = cotangent[0].astype(jnp.float32)
    scaled_grad = sent_grad * gain_two
    middle_grad = (
        upstream
        + second_scale * scaled_grad
        - middle
        * second_scale**3
        * jnp.mean(scaled_grad * middle, axis=-1, keepdims=True)
    )
    gain_two_part = jnp.sum(sent_grad * middle * second_scale, axis=0)
    branch_grad = (RESIDUAL * middle_grad).astype(jnp.bfloat16)

    def out_step(tie, works):
        if works:
            out_sum.keep(works[-1])
        return out_sum.step(tie)

    branch_grad_all, works = dp_gather(branch_grad, (out_step, out_step, out_step, None))
    out_sum.keep(works[2])
    output = middle + RESIDUAL * out_sum.total()
    in_back = lax.all_to_all(
        after(in_term, branch_grad_all).reshape(n_dp, in_weight.shape[0], 2 * ff_cols),
        "dp",
        split_axis=0,
        concat_axis=0,
        tiled=True,
    )


    qkv_grad, normed_grad_part, gain_one_part = rear(
        branch_grad_all,
        o_w,
        queries,
        keys,
        vals,
        run_top,
        run_total,
        row_ids,
        col_ids,
        cosine,
        sine_table,
        qkv_w,
        group_tokens,
    )
    total = DpScatter(normed_grad_part)

    def weight_grads(tie):
        qkv_term = lax.dot_general(
            normed, tie(qkv_grad), ROWS_DIMS, preferred_element_type=jnp.float32
        )
        o_term = lax.dot_general(
            branch_grad_all, mixed_low, ROWS_DIMS, preferred_element_type=jnp.float32
        )
        grads = jnp.concatenate(
            [
                qkv_term,
                o_term,
                gain_one_part[0][:, None],
                gain_two_part[:, None],
                jnp.zeros((model, 126), jnp.float32),
            ],
            axis=1,
        ).astype(jnp.bfloat16)
        grads = grads.reshape(n_dp, n_ex, w_rows, -1)
        return [
            lax.dynamic_index_in_dim(grads, ex_index ^ k, 1, keepdims=False) for k in range(n_ex)
        ]

    sums, (own_g, core_g, x_g, xc_g) = one_round(total.step(), (normed_grad_part,), weight_grads)
    total.keep(sums)
    core_pair = jnp.stack([core_g, xc_g])
    (sums, from_core), _ = one_round((total.step(), swap_core(core_pair)), (core_pair,))
    total.keep(sums)
    x_g = added(x_g, from_core[1])
    (sums, from_x), _ = one_round((total.step(), swap_x(x_g)), (x_g,))
    total.keep(sums)
    grads = lax.all_to_all(
        added(own_g, from_core[0], from_x), "dp", split_axis=0, concat_axis=0, tiled=True
    )
    (sums, grads), in_grad = one_round(
        (total.step(), grads),
        (from_x,),
        lambda tie: unpack_grads(tie(in_back), own_experts).transpose(1, 0, 2),
    )
    total.keep(sums)
    grads = grads.astype(jnp.float32)
    normed_grad = total.total()

    def own_rows(begin, width):
        return grads[:, :, begin : begin + width].transpose(1, 0, 2).reshape(w_rows, n_dp * width)

    q_grad = own_rows(0, q_cols)
    k_grad = own_rows(q_cols, kv_cols)
    v_grad = own_rows(q_cols + kv_cols, kv_cols)
    o_grad = own_rows(qkv_cols, q_cols)
    gain_attn_grad = jnp.sum(grads[:, :, qkv_cols + q_cols], axis=0)
    gain_moe_grad = jnp.sum(grads[:, :, qkv_cols + q_cols + 1], axis=0)

    own_scale = lax.rsqrt(jnp.mean(inputs * inputs, axis=-1, keepdims=True) + EPSILON)
    scaled_one = normed_grad * gain_one
    input_grad = (
        middle_grad
        + own_scale * scaled_one
        - inputs * own_scale**3 * jnp.mean(scaled_one * inputs, axis=-1, keepdims=True)
    )
    return (
        output[None],
        input_grad[None],
        q_grad,
        k_grad,
        v_grad,
        o_grad,
        gain_attn_grad,
        gain_moe_grad,
        in_grad,
        down_grad,
    )


def per_layer(*args):
    return per_device(*args)


def solution(mesh):
    placed = (
        P("expert", "dp", None),
        P("expert", "dp", None),
        P("expert", None),
        P(),
        P("expert", "dp", None),
        P("expert", "dp", None),
        P(("dp", "expert"), None),
        P(("dp", "expert"), None),
        P(("dp", "expert"), None),
        P(("dp", "expert"), None),
        P(("dp", "expert")),
        P(("dp", "expert")),
        P("dp", "expert", None),
        P("dp", "expert", None),
    )
    n_dp = mesh.shape["dp"]
    split_heads = n_dp == 8 and mesh.shape["expert"] == 4
    return jax.shard_map(
        per_layer if split_heads else per_device_wide,
        mesh=mesh,
        in_specs=placed,
        out_specs=(
            P("expert", "dp", None),
            P("expert", "dp", None),
            P(("dp", "expert"), None),
            P(("dp", "expert"), None),
            P(("dp", "expert"), None),
            P(("dp", "expert"), None),
            P(("dp", "expert")),
            P(("dp", "expert")),
            P("dp", "expert", None),
            P("dp", "expert", None),
        ),
        check_vma=False,
    )
```

```python
import functools

import jax
import jax.numpy as jnp
from jax import lax
from jax.experimental import pallas as pl
from jax.experimental.pallas import tpu as pltpu
from jax.sharding import PartitionSpec as P


H = 24
KVH = 8
HD = 64
E = 40
FF = 512
TOPK = 8
CAP = 40


EPSILON = 1e-06
RESIDUAL = 0.22
SCORE_SCALE = 0.015625
THETA = 10000.0
NEGATIVE = -1e30
ROWS_DIMS = (((0,), (0,)), ((), ()))
COLS_DIMS = (((1,), (1,)), ((), ()))


def rms_scale(values, gain):
    return values * lax.rsqrt(jnp.mean(values * values, axis=-1, keepdims=True) + EPSILON) * gain


def rotate(values, cosine, sine_table):
    half_width = values.shape[-1] // 2
    turned = jnp.concatenate([-values[..., half_width:], values[..., :half_width]], axis=-1)
    return values * cosine + turned * sine_table


def turn_back(grads_in, cosine, sine_table):
    half_width = grads_in.shape[-1] // 2
    scaled = grads_in * sine_table
    return grads_in * cosine + jnp.concatenate(
        [scaled[..., half_width:], -scaled[..., :half_width]], axis=-1
    )


def silu_product(gate_in, up_in):
    return jax.nn.silu(gate_in) * up_in


def locate(where_at, seq_ends):
    return jnp.sum((where_at[:, None] >= seq_ends[None, :]).astype(jnp.int32), axis=-1)


def cut_block(source, begin_at, block_rows, heads):
    piece = lax.dynamic_slice_in_dim(source, begin_at, block_rows, 0)
    return piece.reshape(block_rows, heads, source.shape[1] // heads)


def group_chooser(wanted, carried, pieces, start):
    piece_rows = pieces[0].shape[0]
    inside = (wanted >= start) & (wanted < start + piece_rows)
    offset_at = jnp.clip(wanted, 0, piece_rows - 1)
    return tuple(
        (
            jnp.where(inside, lax.dynamic_slice_in_dim(member_piece, offset_at, 1, 0), member_carry)
            for member_piece, member_carry in zip(pieces, carried)
        )
    )


def per_device_wide(
    tokens,
    cotangent,
    lengths,
    deal,
    routes,
    gates,
    q_weight,
    k_weight,
    v_weight,
    o_weight,
    gain_attn,
    gain_moe,
    in_weight,
    down_weight,
):
    tok_rows = tokens.shape[1]
    model_width = tokens.shape[2]
    group_rows = tok_rows * lax.axis_size("dp")
    block_rows = min(512, group_rows)
    heads_per = H // KVH
    owner_index = lax.axis_index("expert")
    group_ids = jnp.arange(deal.shape[0], dtype=jnp.int32)
    wanted_in = jnp.sum(jnp.where(group_ids == owner_index, deal, 0))
    wanted_out = jnp.sum(jnp.where(deal == owner_index, group_ids, 0))
    dealt_tokens, dealt_cotangent = group_chooser(
        wanted_in,
        (jnp.zeros_like(tokens), jnp.zeros_like(cotangent)),
        (
            lax.all_gather(tokens, "expert", axis=0, tiled=True),
            lax.all_gather(cotangent, "expert", axis=0, tiled=True),
        ),
        jnp.int32(0),
    )
    inputs = dealt_tokens[0].astype(jnp.float32)
    q_full, k_full, v_full, o_full, gain_one, gain_two = (
        lax.all_gather(q_weight.astype(jnp.bfloat16), ("dp", "expert"), axis=0, tiled=True),
        lax.all_gather(k_weight.astype(jnp.bfloat16), ("dp", "expert"), axis=0, tiled=True),
        lax.all_gather(v_weight.astype(jnp.bfloat16), ("dp", "expert"), axis=0, tiled=True),
        lax.all_gather(o_weight.astype(jnp.bfloat16), ("dp", "expert"), axis=0, tiled=True),
        lax.all_gather(gain_attn.astype(jnp.bfloat16), ("dp", "expert"), axis=0, tiled=True),
        lax.all_gather(gain_moe.astype(jnp.bfloat16), ("dp", "expert"), axis=0, tiled=True),
    )
    gain_one = gain_one.astype(jnp.float32)
    gain_two = gain_two.astype(jnp.float32)
    seq_lengths = lengths[0]
    seq_ends = jnp.cumsum(seq_lengths)
    seq_starts = seq_ends - seq_lengths
    first_place = lax.axis_index("dp") * tok_rows
    places = first_place + jnp.arange(tok_rows, dtype=jnp.int32)
    member = (places[:, None] >= seq_starts[None, :]) & (places[:, None] < seq_ends[None, :])
    offsets = jnp.sum(jnp.where(member, places[:, None] - seq_starts[None, :], 0), axis=-1)
    frequency = THETA ** (-jnp.arange(HD // 2, dtype=jnp.float32) * 2.0 / HD)
    angles = offsets.astype(jnp.float32)[:, None] * frequency[None, :]
    angles = jnp.concatenate([angles, angles], axis=-1)[:, None, :]
    cosine = jnp.cos(angles)
    sine_table = jnp.sin(angles)
    query_seq = locate(places, seq_ends)
    seq_floor = jnp.sum(jnp.where(member[0], seq_starts, 0))
    low_block = seq_floor // block_rows
    high_block = (first_place + tok_rows - 1) // block_rows + 1
    normed = rms_scale(inputs, gain_one).astype(jnp.bfloat16)
    query_pre = jnp.dot(normed, q_full, preferred_element_type=jnp.float32).reshape(tok_rows, H, HD)
    key_pre = jnp.dot(normed, k_full, preferred_element_type=jnp.float32).reshape(tok_rows, KVH, HD)
    value_rows = jnp.dot(normed, v_full, preferred_element_type=jnp.float32).astype(jnp.bfloat16)
    queries = (
        rotate(query_pre, cosine, sine_table)
        .astype(jnp.bfloat16)
        .reshape(tok_rows, KVH, heads_per, HD)
    )
    key_rows = rotate(key_pre, cosine, sine_table).astype(jnp.bfloat16).reshape(tok_rows, KVH * HD)
    all_keys, all_values = (
        lax.all_gather(key_rows, "dp", axis=0, tiled=True),
        lax.all_gather(value_rows, "dp", axis=0, tiled=True),
    )

    def scores_for(block_id, key_block):
        begin_at = block_id * block_rows
        key_places = begin_at + jnp.arange(block_rows, dtype=jnp.int32)
        allowed = (query_seq[:, None] == locate(key_places, seq_ends)[None, :]) & (
            key_places[None, :] <= places[:, None]
        )
        raw_scores = SCORE_SCALE * jnp.einsum(
            "tkgd,skd->kgts", queries, key_block, preferred_element_type=jnp.float32
        )
        return (raw_scores, allowed)

    def stats_step(block_id, carried):
        run_top, run_total = carried
        key_block = cut_block(all_keys, block_id * block_rows, block_rows, KVH)
        raw_scores, allowed = scores_for(block_id, key_block)
        new_top = jnp.maximum(run_top, jnp.max(jnp.where(allowed, raw_scores, NEGATIVE), axis=-1))
        weights_now = jnp.where(allowed, jnp.exp(raw_scores - new_top[..., None]), 0.0)
        run_total = run_total * jnp.exp(run_top - new_top) + jnp.sum(weights_now, axis=-1)
        return (new_top, run_total)

    top_init = jnp.full((KVH, heads_per, tok_rows), NEGATIVE, jnp.float32)
    total_init = jnp.zeros((KVH, heads_per, tok_rows), jnp.float32)
    run_top, run_total = lax.fori_loop(low_block, high_block, stats_step, (top_init, total_init))
    log_total = run_top + jnp.log(run_total)

    def attn_probs(block_id, key_block):
        raw_scores, allowed = scores_for(block_id, key_block)
        return jnp.where(allowed, jnp.exp(raw_scores - log_total[..., None]), 0.0)

    def value_step(block_id, running):
        key_block = cut_block(all_keys, block_id * block_rows, block_rows, KVH)
        value_block = cut_block(all_values, block_id * block_rows, block_rows, KVH)
        chances = attn_probs(block_id, key_block).astype(jnp.bfloat16)
        return running + jnp.einsum(
            "kgts,skd->tkgd", chances, value_block, preferred_element_type=jnp.float32
        )

    mixed_init = jnp.zeros((tok_rows, KVH, heads_per, HD), jnp.float32)
    mixed_rows = lax.fori_loop(low_block, high_block, value_step, mixed_init).reshape(
        tok_rows, H * HD
    )
    mixed_low = mixed_rows.astype(jnp.bfloat16)
    branch = lax.dot_general(mixed_low, o_full, COLS_DIMS, preferred_element_type=jnp.float32)
    middle = inputs + RESIDUAL * branch
    sent_rows = rms_scale(middle, gain_two).astype(jnp.bfloat16)
    route_ids = routes[0].reshape(tok_rows * TOPK)
    matches = (route_ids[:, None] == jnp.arange(E, dtype=jnp.int32)[None, :]).astype(jnp.int32)
    slot_rank = jnp.sum(matches * jnp.cumsum(matches, axis=0), axis=-1) - 1
    slot_index = route_ids * CAP + slot_rank
    copies = jnp.repeat(sent_rows, TOPK, axis=0)
    outgoing = (
        jnp.zeros((E * CAP, model_width), jnp.bfloat16)
        .at[slot_index]
        .set(copies)
        .reshape(E, CAP, model_width)
    )
    arrived = lax.all_to_all(outgoing, "expert", split_axis=0, concat_axis=1, tiled=True)
    w_in, w_down = (
        lax.all_gather(in_weight.astype(jnp.bfloat16), "dp", axis=0, tiled=True),
        lax.all_gather(down_weight.astype(jnp.bfloat16), "dp", axis=0, tiled=True),
    )
    gate_up = jnp.einsum("erd,def->erf", arrived, w_in, preferred_element_type=jnp.float32)
    gate_part = gate_up[..., :FF]
    up_part = gate_up[..., FF:]
    hidden = silu_product(gate_part, up_part).astype(jnp.bfloat16)
    produced = jnp.einsum(
        "erf,fed->erd", hidden, w_down, preferred_element_type=jnp.float32
    ).astype(jnp.bfloat16)
    returned = lax.all_to_all(produced, "expert", split_axis=1, concat_axis=0, tiled=True).reshape(
        E * CAP, model_width
    )
    route_gates = gates[0].reshape(tok_rows * TOPK)
    picked = returned[slot_index].astype(jnp.float32) * route_gates[:, None]
    expert_sum = jnp.sum(picked.reshape(tok_rows, TOPK, model_width), axis=1)
    output = middle + RESIDUAL * expert_sum
    upstream = dealt_cotangent[0].astype(jnp.float32)
    spread = (RESIDUAL * route_gates[:, None] * jnp.repeat(upstream, TOPK, axis=0)).astype(
        jnp.bfloat16
    )
    back_out = (
        jnp.zeros((E * CAP, model_width), jnp.bfloat16)
        .at[slot_index]
        .set(spread)
        .reshape(E, CAP, model_width)
    )
    back_in = lax.all_to_all(back_out, "expert", split_axis=0, concat_axis=1, tiled=True)
    hidden_grad = jnp.einsum("erd,fed->erf", back_in, w_down, preferred_element_type=jnp.float32)
    down_term = jnp.einsum("erf,erd->fed", hidden, back_in, preferred_element_type=jnp.float32)
    ignored, silu_pull = jax.vjp(silu_product, gate_part, up_part)
    gate_grad, up_grad = silu_pull(hidden_grad)
    gate_up_grad = jnp.concatenate([gate_grad, up_grad], axis=-1).astype(jnp.bfloat16)
    in_term = jnp.einsum("erd,erf->def", arrived, gate_up_grad, preferred_element_type=jnp.float32)
    arrived_grad = jnp.einsum(
        "erf,def->erd", gate_up_grad, w_in, preferred_element_type=jnp.float32
    ).astype(jnp.bfloat16)
    sent_back = lax.all_to_all(
        arrived_grad, "expert", split_axis=1, concat_axis=0, tiled=True
    ).reshape(E * CAP, model_width)
    sent_grad = jnp.sum(
        sent_back[slot_index].astype(jnp.float32).reshape(tok_rows, TOPK, model_width), axis=1
    )
    in_grad, down_grad = (
        lax.psum_scatter(
            in_term.astype(jnp.bfloat16), "dp", scatter_dimension=0, tiled=True
        ).astype(jnp.float32),
        lax.psum_scatter(
            down_term.astype(jnp.bfloat16), "dp", scatter_dimension=0, tiled=True
        ).astype(jnp.float32),
    )
    ignored, second_pull = jax.vjp(rms_scale, middle, gain_two)
    middle_part, gain_two_term = second_pull(sent_grad)
    middle_grad = upstream + middle_part
    branch_grad = (RESIDUAL * middle_grad).astype(jnp.bfloat16)
    o_term = lax.dot_general(branch_grad, mixed_low, ROWS_DIMS, preferred_element_type=jnp.float32)
    grad_heads = jnp.dot(branch_grad, o_full, preferred_element_type=jnp.float32).astype(
        jnp.bfloat16
    )
    grad_heads = grad_heads.reshape(tok_rows, KVH, heads_per, HD)

    def delta_step(block_id, running):
        key_block = cut_block(all_keys, block_id * block_rows, block_rows, KVH)
        value_block = cut_block(all_values, block_id * block_rows, block_rows, KVH)
        chances = attn_probs(block_id, key_block)
        prob_grad = jnp.einsum(
            "tkgd,skd->kgts", grad_heads, value_block, preferred_element_type=jnp.float32
        )
        return running + jnp.sum(chances * prob_grad, axis=-1)

    row_delta = lax.fori_loop(
        low_block, high_block, delta_step, jnp.zeros((KVH, heads_per, tok_rows), jnp.float32)
    )

    def grad_step(block_id, carried):
        query_grad, key_buffer, value_buffer = carried
        begin_at = block_id * block_rows
        key_block = cut_block(all_keys, begin_at, block_rows, KVH)
        value_block = cut_block(all_values, begin_at, block_rows, KVH)
        chances = attn_probs(block_id, key_block)
        prob_grad = jnp.einsum(
            "tkgd,skd->kgts", grad_heads, value_block, preferred_element_type=jnp.float32
        )
        score_grad = (chances * (prob_grad - row_delta[..., None])).astype(jnp.bfloat16)
        query_grad = query_grad + SCORE_SCALE * jnp.einsum(
            "kgts,skd->tkgd", score_grad, key_block, preferred_element_type=jnp.float32
        )
        key_part = SCORE_SCALE * jnp.einsum(
            "kgts,tkgd->skd", score_grad, queries, preferred_element_type=jnp.float32
        )
        value_part = jnp.einsum(
            "kgts,tkgd->skd",
            chances.astype(jnp.bfloat16),
            grad_heads,
            preferred_element_type=jnp.float32,
        )
        key_buffer = lax.dynamic_update_slice_in_dim(
            key_buffer, key_part.reshape(block_rows, KVH * HD), begin_at, 0
        )
        value_buffer = lax.dynamic_update_slice_in_dim(
            value_buffer, value_part.reshape(block_rows, KVH * HD), begin_at, 0
        )
        return (query_grad, key_buffer, value_buffer)

    grad_init = (
        jnp.zeros((tok_rows, KVH, heads_per, HD), jnp.float32),
        jnp.zeros((group_rows, KVH * HD), jnp.float32),
        jnp.zeros((group_rows, KVH * HD), jnp.float32),
    )
    query_grad, key_buffer, value_buffer = lax.fori_loop(
        low_block, high_block, grad_step, grad_init
    )
    key_grad, value_grad = (
        lax.psum_scatter(
            key_buffer.astype(jnp.bfloat16), "dp", scatter_dimension=0, tiled=True
        ).astype(jnp.float32),
        lax.psum_scatter(
            value_buffer.astype(jnp.bfloat16), "dp", scatter_dimension=0, tiled=True
        ).astype(jnp.float32),
    )
    query_low = (
        turn_back(query_grad.reshape(tok_rows, H, HD), cosine, sine_table)
        .reshape(tok_rows, H * HD)
        .astype(jnp.bfloat16)
    )
    key_low = (
        turn_back(key_grad.reshape(tok_rows, KVH, HD), cosine, sine_table)
        .reshape(tok_rows, KVH * HD)
        .astype(jnp.bfloat16)
    )
    value_low = value_grad.astype(jnp.bfloat16)
    q_term = lax.dot_general(normed, query_low, ROWS_DIMS, preferred_element_type=jnp.float32)
    k_term = lax.dot_general(normed, key_low, ROWS_DIMS, preferred_element_type=jnp.float32)
    v_term = lax.dot_general(normed, value_low, ROWS_DIMS, preferred_element_type=jnp.float32)
    normed_grad = lax.dot_general(query_low, q_full, COLS_DIMS, preferred_element_type=jnp.float32)
    normed_grad = normed_grad + lax.dot_general(
        key_low, k_full, COLS_DIMS, preferred_element_type=jnp.float32
    )
    normed_grad = normed_grad + lax.dot_general(
        value_low, v_full, COLS_DIMS, preferred_element_type=jnp.float32
    )
    ignored, first_pull = jax.vjp(rms_scale, inputs, gain_one)
    input_part, gain_one_term = first_pull(normed_grad)
    input_grad = middle_grad + input_part
    q_grad, k_grad, v_grad, o_grad, gain_attn_grad, gain_moe_grad = (
        lax.psum_scatter(q_term, ("dp", "expert"), scatter_dimension=0, tiled=True),
        lax.psum_scatter(k_term, ("dp", "expert"), scatter_dimension=0, tiled=True),
        lax.psum_scatter(v_term, ("dp", "expert"), scatter_dimension=0, tiled=True),
        lax.psum_scatter(o_term, ("dp", "expert"), scatter_dimension=0, tiled=True),
        lax.psum_scatter(gain_one_term, ("dp", "expert"), scatter_dimension=0, tiled=True),
        lax.psum_scatter(gain_two_term, ("dp", "expert"), scatter_dimension=0, tiled=True),
    )
    given_output, given_input_grad = group_chooser(
        wanted_out,
        (
            jnp.zeros((1, tok_rows, model_width), jnp.float32),
            jnp.zeros((1, tok_rows, model_width), jnp.float32),
        ),
        (
            lax.all_gather(output[None].astype(jnp.bfloat16), "expert", axis=0, tiled=True).astype(
                jnp.float32
            ),
            lax.all_gather(
                input_grad[None].astype(jnp.bfloat16), "expert", axis=0, tiled=True
            ).astype(jnp.float32),
        ),
        jnp.int32(0),
    )
    return (
        given_output,
        given_input_grad,
        q_grad,
        k_grad,
        v_grad,
        o_grad,
        gain_attn_grad,
        gain_moe_grad,
        in_grad,
        down_grad,
    )


SWAP_Y = [(i, i ^ 1) for i in range(8)]
SWAP_CORE = [(j, j ^ 1) for j in range(4)]
SWAP_X = [(j, j ^ 2) for j in range(4)]


def along_z(moves):
    return [(2 * s + y, 2 * d + y) for s, d in moves for y in range(2)]


Z_NEAR = along_z([(0, 1), (1, 0), (2, 3), (3, 2)])
Z_MIDDLE = along_z([(1, 2), (2, 1)])
Z_OUT = along_z([(1, 0), (2, 3)])
Z_IN = along_z([(0, 1), (3, 2)])
SLOT_Z = ((0, 1, 2, 3), (1, 0, 3, 2), (2, 2, 1, 1), (3, 3, 0, 0))


def over_dp(piece, moves):
    return lax.ppermute(piece, "dp", moves)


def over_expert(piece, moves):
    return lax.ppermute(piece, "expert", moves)


def added(first, *others):
    total = first.astype(jnp.float32)
    for other in others:
        total = total + other.astype(jnp.float32)
    return total.astype(jnp.bfloat16)


def halves(array):
    half = array.shape[0] // 2
    return array[:half], array[half:]


def joined(*arrays):
    return jnp.concatenate(arrays, axis=0)


def one_round(outs, ins, cover=None):
    if cover is None:
        return lax.optimization_barrier(outs), None
    return lax.optimization_barrier((outs, cover(lambda x: after(x, *ins))))


def swap_y(value):
    return over_dp(value, SWAP_Y)


def swap_x(value):
    return over_expert(value, SWAP_X)


def swap_core(value):
    return over_expert(value, SWAP_CORE)


def dp_gather(piece, covers=(None, None, None, None)):
    works = []

    def run(outs, ins, cover):
        outs, work = one_round(outs, ins, cover and (lambda tie: cover(tie, works)))
        works.append(work)
        return outs

    near, middle, y0 = run(
        (over_dp(piece, Z_NEAR), over_dp(piece, Z_MIDDLE), swap_y(piece)), (piece,), covers[0]
    )
    far, out1, y1 = run(
        (over_dp(near, Z_MIDDLE), over_dp(middle, Z_OUT), swap_y(near)), (near, middle), covers[1]
    )
    third = middle + out1
    out2, y2 = run((over_dp(far, Z_OUT), swap_y(third)), (far, third), covers[2])
    fourth = far + out2
    y3 = run(swap_y(fourth), (fourth,), covers[3])
    return joined(piece, y0, near, y1, third, y2, fourth, y3), works


class DpScatter:
    def __init__(self, total):
        blocks = jnp.split(total, 8, axis=0)
        self.own, self.sent = blocks[0::2], blocks[1::2]
        self.round = 0

    def step(self, tie=lambda v: v):
        self.round += 1
        if self.round == 1:
            self.z = swap_y(tie(self.sent[3]))
        elif self.round == 2:
            self.fourth = added(self.own[3], self.z)
            self.z = over_dp(tie(self.fourth), Z_IN), swap_y(self.sent[2])
        elif self.round == 3:
            fourth = added(self.fourth, self.z[0])
            self.third = added(self.own[2], self.z[1])
            self.z = (
                over_dp(tie(fourth), Z_MIDDLE),
                over_dp(self.third, Z_IN),
                swap_y(self.sent[1]),
            )
        else:
            third = added(self.third, self.z[1])
            near = added(self.own[1], self.z[2], self.z[0])
            self.z = (
                over_dp(tie(near), Z_NEAR),
                over_dp(third, Z_MIDDLE),
                swap_y(self.sent[0]),
            )
        return self.z

    def keep(self, values):
        self.z = values

    def total(self):
        total = self.own[0].astype(jnp.float32)
        for value in self.z:
            total = total + value.astype(jnp.float32)
        return total


def gather_pairs(piece, covers):
    works = []

    def run(outs, ins, cover=None):
        outs, work = one_round(outs, ins, cover and (lambda tie: cover(tie, works)))
        works.append(work)
        return outs

    near, middle = run(
        (over_dp(piece, Z_NEAR), over_dp(piece, Z_MIDDLE)), (piece,), covers[0]
    )

    def split(first, second):
        (ft, fl), (st, sl) = halves(first), halves(second)
        return joined(ft, st), joined(fl, sl)

    top, low = split(piece, near)
    far, out1, y_top, x_low = run(
        (over_dp(near, Z_MIDDLE), over_dp(middle, Z_OUT), swap_y(top), swap_x(low)),
        (top, low),
        covers[1],
    )
    third = middle + out1
    top, low = joined(top, y_top), joined(low, x_low)
    out2, x_top, y_low = run(
        (over_dp(far, Z_OUT), swap_x(top), swap_y(low)), (top, low), covers[2]
    )
    here = joined(top, x_top, low, y_low)
    top, low = split(third, far + out2)
    y_top, x_low, there = run(
        (swap_y(top), swap_x(low), swap_core(here)), (top, low, here), covers[3]
    )
    first = joined(here, there)
    top, low = joined(top, y_top), joined(low, x_low)
    x_top, y_low = run(
        (swap_x(top), swap_y(low)), (top, low), lambda tie, works: covers[4](tie, works, first)
    )
    here = joined(top, x_top, low, y_low)
    there = run(swap_core(here), (here,), covers[5])
    return (first, joined(here, there)), works


class PairScatter:
    def __init__(self, totals):
        (self.m0, self.o0), (self.m1, self.o1) = [halves(t) for t in totals]
        self.round = 0

    def across(self, parts, first, second, tie):
        (ta, tb), (la, lb) = [halves(p) for p in parts]
        return (ta, la), (first(tie(tb)), second(tie(lb)))

    def both(self, kept, moved):
        return [added(k, m) for k, m in zip(kept, moved)]

    def step(self, tie=lambda v: v):
        self.round += 1
        if self.round == 1:
            self.moved = swap_core(tie(self.o1))
        elif self.round == 2:
            parts = halves(added(self.m1, self.moved))
            self.kept1, moved1 = self.across(parts, swap_x, swap_y, tie)
            self.moved = moved1, swap_core(tie(self.o0))
        elif self.round == 3:
            parts1 = self.both(self.kept1, self.moved[0])
            parts0 = halves(added(self.m0, self.moved[1]))
            self.kept1, moved1 = self.across(parts1, swap_y, swap_x, tie)
            self.kept0, moved0 = self.across(parts0, swap_x, swap_y, tie)
            self.moved = moved1, moved0
        elif self.round == 4:
            (third_top, fourth_top), (third_low, fourth_low) = [
                halves(p) for p in self.both(self.kept1, self.moved[0])
            ]
            self.third, self.fourth = joined(third_top, third_low), joined(fourth_top, fourth_low)
            parts0 = self.both(self.kept0, self.moved[1])
            self.kept0, moved0 = self.across(parts0, swap_y, swap_x, tie)
            self.moved = moved0, over_dp(tie(self.fourth), Z_IN)
        elif self.round == 5:
            (own_top, near_top), (own_low, near_low) = [
                halves(p) for p in self.both(self.kept0, self.moved[0])
            ]
            self.own, self.near = joined(own_top, own_low), joined(near_top, near_low)
            fourth = added(self.fourth, self.moved[1])
            self.moved = over_dp(tie(fourth), Z_MIDDLE), over_dp(tie(self.third), Z_IN)
        else:
            near, third = added(self.near, self.moved[0]), added(self.third, self.moved[1])
            self.moved = over_dp(tie(near), Z_NEAR), over_dp(tie(third), Z_MIDDLE)
        return self.moved

    def keep(self, values):
        self.moved = values

    def total(self):
        total = self.own.astype(jnp.float32)
        for value in self.moved:
            total = total + value.astype(jnp.float32)
        return total


def scatter_pairs(totals, covers):
    works = []
    scatter = PairScatter(totals)
    for cover in covers:
        outs = scatter.step()
        outs, work = one_round(outs, (), cover and (lambda tie: cover(tie, works)))
        scatter.keep(outs)
        works.append(work)
    return scatter.total(), works


def far_order(ex_index, dealt_of):
    r = jnp.arange(64, dtype=jnp.int32)
    pair, core, half, outer, inner = r // 32, r // 16 % 2, r // 8 % 2, r // 4 % 2, r // 2 % 2
    slot = 2 * pair + r % 2
    flip_y = jnp.where(half == 0, inner, outer)
    flip_x = jnp.where(half == 0, outer, inner)

    def place(flip):
        return ((flip % 2 * 4 + slot) * 4 + flip // 2 * 2 + flip_y) * 2 + half

    flip = 2 * flip_x + core
    return place(flip), place(jnp.take(dealt_of, ex_index ^ flip) ^ ex_index)


def take_kernel(index_ref, *refs, at_once):
    count = len(refs) // (at_once + 1)
    for p in range(count):
        target = refs[count * at_once + p]
        rows = target.shape[0] // at_once
        for k in range(at_once):
            target[k * rows : (k + 1) * rows, :] = refs[p * at_once + k][...]


def take_blocks(index, array, parts, block):
    at_once = 8
    steps = index.shape[1] // at_once

    def source(row, column, k):
        return lambda i, idx: (idx[row, at_once * i + k], column)

    return pl.pallas_call(
        functools.partial(take_kernel, at_once=at_once),
        out_shape=[
            jax.ShapeDtypeStruct((index.shape[1] * block, width), array.dtype)
            for row, column, width in parts
        ],
        grid_spec=pltpu.PrefetchScalarGridSpec(
            num_scalar_prefetch=1,
            grid=(steps,),
            in_specs=[
                pl.BlockSpec((block, width), source(row, column, k))
                for row, column, width in parts
                for k in range(at_once)
            ],
            out_specs=[
                pl.BlockSpec((at_once * block, width), lambda i, idx: (i, 0))
                for row, column, width in parts
            ],
        ),
        name="take_blocks",
    )(index, *([array] * (at_once * len(parts))))


def attend_masks(row_ids, col_ids, begin, rows):
    seq_rows = row_ids[pl.ds(begin, rows), 0:1]
    place_rows = row_ids[pl.ds(begin, rows), 1:2]
    return (seq_rows == col_ids[0:1, :]) & (col_ids[1:2, :] <= place_rows)


def front_kernel(
    x_ref, gain_ref, w_ref, ow_ref, cos_ref, sin_ref, row_ids, col_ids,
    normed_ref, q_ref, k_ref, v_ref, o_ref, top_ref, total_ref, part_ref, *, heads, rows
):
    q_cols = heads * HD
    steps = x_ref.shape[0] // rows

    def project(i, carry):
        here = pl.ds(pl.multiple_of(i * rows, rows), rows)
        inputs = x_ref[here, :].astype(jnp.float32)
        scale = lax.rsqrt(jnp.mean(inputs * inputs, axis=-1, keepdims=True) + EPSILON)
        normed = (inputs * scale * gain_ref[...]).astype(jnp.bfloat16)
        normed_ref[here, :] = normed
        qkv = jnp.dot(normed, w_ref[...], preferred_element_type=jnp.float32)
        cosine, sine = cos_ref[here, :], sin_ref[here, :]
        turned = []
        for h in range(heads + 1):
            turned.append(rotate(qkv[:, h * HD : (h + 1) * HD], cosine, sine))
        q_ref[here, :] = jnp.concatenate(turned[:heads], axis=1).astype(jnp.bfloat16)
        k_ref[here, :] = turned[heads].astype(jnp.bfloat16)
        v_ref[here, :] = qkv[:, q_cols + HD :].astype(jnp.bfloat16)
        return carry

    lax.fori_loop(0, steps, project, 0)
    keys, vals = k_ref[...], v_ref[...]

    def step(i, carry):
        begin = pl.multiple_of(i * rows, rows)
        here = pl.ds(begin, rows)
        allowed = attend_masks(row_ids, col_ids, begin, rows)
        outs, tops, totals = [], [], []
        for h in range(heads):
            scores = SCORE_SCALE * lax.dot_general(
                q_ref[here, h * HD : (h + 1) * HD],
                keys,
                COLS_DIMS,
                preferred_element_type=jnp.float32,
            )
            scores = jnp.where(allowed, scores, NEGATIVE)
            top = jnp.max(scores, axis=-1, keepdims=True)
            weights = jnp.exp(scores - top)
            total = jnp.sum(weights, axis=-1, keepdims=True)
            chances = (weights / total).astype(jnp.bfloat16)
            outs.append(jnp.dot(chances, vals, preferred_element_type=jnp.float32))
            tops.append(top)
            totals.append(total)
        mixed = jnp.concatenate(outs, axis=1).astype(jnp.bfloat16)
        o_ref[here, :] = mixed
        top_ref[here, :] = jnp.concatenate(tops, axis=1)
        total_ref[here, :] = jnp.concatenate(totals, axis=1)
        part_ref[here, :] = lax.dot_general(
            mixed, ow_ref[...], COLS_DIMS, preferred_element_type=jnp.float32
        ).astype(jnp.bfloat16)
        return carry

    lax.fori_loop(0, steps, step, 0)


def front(inputs, gain, qkv_w, o_w, cosine, sine, row_ids, col_ids):
    rows, model = inputs.shape
    heads = H // KVH
    low = jnp.bfloat16
    return pl.pallas_call(
        functools.partial(front_kernel, heads=heads, rows=min(256, rows)),
        out_shape=[
            jax.ShapeDtypeStruct((rows, model), low),
            jax.ShapeDtypeStruct((rows, heads * HD), low),
            jax.ShapeDtypeStruct((rows, HD), low),
            jax.ShapeDtypeStruct((rows, HD), low),
            jax.ShapeDtypeStruct((rows, heads * HD), low),
            jax.ShapeDtypeStruct((rows, heads), jnp.float32),
            jax.ShapeDtypeStruct((rows, heads), jnp.float32),
            jax.ShapeDtypeStruct((rows, model), low),
        ],
        name="front",
    )(inputs, gain, qkv_w, o_w, cosine, sine, row_ids, col_ids)


def rear_kernel(
    g_ref, ow_ref, q_ref, k_ref, v_ref, top_ref, total_ref, row_ids, col_ids, cos_ref, sin_ref,
    w_ref, x_ref, qkvg_ref, part_ref, gain_ref, dk_ref, dv_ref, *, heads, rows
):
    q_cols = heads * HD
    steps = x_ref.shape[0] // rows
    dk_ref[...] = jnp.zeros_like(dk_ref)
    dv_ref[...] = jnp.zeros_like(dv_ref)
    gain_ref[...] = jnp.zeros_like(gain_ref)
    keys, vals = k_ref[...], v_ref[...]

    def step(i, carry):
        begin = pl.multiple_of(i * rows, rows)
        here = pl.ds(begin, rows)
        allowed = attend_masks(row_ids, col_ids, begin, rows)
        grads = jnp.dot(g_ref[here, :], ow_ref[...], preferred_element_type=jnp.float32).astype(
            jnp.bfloat16
        )
        cosine, sine = cos_ref[here, :], sin_ref[here, :]
        pulled = []
        key_grad = jnp.zeros((k_ref.shape[0], HD), jnp.float32)
        value_grad = jnp.zeros((k_ref.shape[0], HD), jnp.float32)
        for h in range(heads):
            query = q_ref[here, h * HD : (h + 1) * HD]
            grad = grads[:, h * HD : (h + 1) * HD]
            scores = SCORE_SCALE * lax.dot_general(
                query, keys, COLS_DIMS, preferred_element_type=jnp.float32
            )
            scores = jnp.where(allowed, scores, NEGATIVE)
            weights = jnp.exp(scores - top_ref[here, h : h + 1])
            chances = weights / total_ref[here, h : h + 1]
            prob_grad = lax.dot_general(grad, vals, COLS_DIMS, preferred_element_type=jnp.float32)
            delta = jnp.sum(chances * prob_grad, axis=-1, keepdims=True)
            score_grad = (chances * (prob_grad - delta)).astype(jnp.bfloat16)
            query_grad = SCORE_SCALE * jnp.dot(
                score_grad, keys, preferred_element_type=jnp.float32
            )
            pulled.append(turn_back(query_grad, cosine, sine))
            key_grad += lax.dot_general(
                score_grad, query, ROWS_DIMS, preferred_element_type=jnp.float32
            )
            value_grad += lax.dot_general(
                chances.astype(jnp.bfloat16), grad, ROWS_DIMS, preferred_element_type=jnp.float32
            )
        qkvg_ref[here, 0:q_cols] = jnp.concatenate(pulled, axis=1).astype(jnp.bfloat16)
        dk_ref[...] += SCORE_SCALE * key_grad
        dv_ref[...] += value_grad
        return carry

    lax.fori_loop(0, steps, step, 0)

    def finish(i, carry):
        here = pl.ds(pl.multiple_of(i * rows, rows), rows)
        key_low = turn_back(dk_ref[here, :], cos_ref[here, :], sin_ref[here, :])
        qkvg_ref[here, q_cols:] = jnp.concatenate([key_low, dv_ref[here, :]], axis=1).astype(
            jnp.bfloat16
        )
        part = lax.dot_general(
            qkvg_ref[here, :], w_ref[...], COLS_DIMS, preferred_element_type=jnp.float32
        )
        part_ref[here, :] = part.astype(jnp.bfloat16)
        inputs = x_ref[here, :].astype(jnp.float32)
        scale = lax.rsqrt(jnp.mean(inputs * inputs, axis=-1, keepdims=True) + EPSILON)
        gain_ref[...] += jnp.sum(part * inputs * scale, axis=0, keepdims=True)
        return carry

    lax.fori_loop(0, steps, finish, 0)


def rear(grads_in, o_w, queries, keys, vals, top, total, row_ids, col_ids, cosine, sine, qkv_w, x):
    rows, model = x.shape
    heads = H // KVH
    return pl.pallas_call(
        functools.partial(rear_kernel, heads=heads, rows=min(256, rows)),
        out_shape=[
            jax.ShapeDtypeStruct((rows, qkv_w.shape[1]), jnp.bfloat16),
            jax.ShapeDtypeStruct((rows, model), jnp.bfloat16),
            jax.ShapeDtypeStruct((1, model), jnp.float32),
        ],
        scratch_shapes=[
            pltpu.VMEM((rows, HD), jnp.float32),
            pltpu.VMEM((rows, HD), jnp.float32),
        ],
        name="rear",
    )(grads_in, o_w, queries, keys, vals, top, total, row_ids, col_ids, cosine, sine, qkv_w, x)


def pack_kernel(x_ref, o_ref, *, width):
    experts = x_ref.shape[0]
    half = x_ref.shape[2] // 2
    for i in range(o_ref.shape[0]):
        for g in range(2):
            at = g * half + i * width
            row = jnp.concatenate([x_ref[e, :, at : at + width] for e in range(experts)], axis=1)
            o_ref[i, :, g * experts * width : (g + 1) * experts * width] = row.astype(jnp.bfloat16)


def pack_weights(weight, devices, rows=48):
    experts, d_rows, columns = weight.shape
    width = columns // 2 // devices
    return pl.pallas_call(
        functools.partial(pack_kernel, width=width),
        out_shape=jax.ShapeDtypeStruct((devices, d_rows, 2 * experts * width), jnp.bfloat16),
        grid=(d_rows // rows,),
        in_specs=[pl.BlockSpec((experts, rows, columns), lambda r: (0, r, 0))],
        out_specs=pl.BlockSpec((devices, rows, 2 * experts * width), lambda r: (0, r, 0)),
        name="pack_weights",
    )(weight)


def unpack_kernel(x_ref, o_ref, *, width):
    experts = o_ref.shape[0]
    half = o_ref.shape[2] // 2
    for e in range(experts):
        for g in range(2):
            at = (g * experts + e) * width
            row = jnp.concatenate(
                [x_ref[i, :, at : at + width] for i in range(x_ref.shape[0])], axis=1
            )
            o_ref[e, :, g * half : (g + 1) * half] = row.astype(jnp.float32)


def unpack_grads(moved, experts, rows=48):
    devices, d_rows, columns = moved.shape
    width = columns // 2 // experts
    return pl.pallas_call(
        functools.partial(unpack_kernel, width=width),
        out_shape=jax.ShapeDtypeStruct((experts, d_rows, 2 * devices * width), jnp.float32),
        grid=(d_rows // rows,),
        in_specs=[pl.BlockSpec((devices, rows, columns), lambda r: (0, r, 0))],
        out_specs=pl.BlockSpec((experts, rows, 2 * devices * width), lambda r: (0, r, 0)),
        name="unpack_grads",
    )(moved)


def after(value, *earlier):
    return lax.optimization_barrier((value, *earlier))[0]


def rounded(values):
    return lax.reduce_precision(values, 8, 7)


def rope_parts(seq_lengths, places):
    seq_ends = jnp.cumsum(seq_lengths)
    seq_starts = seq_ends - seq_lengths
    member = (places[:, None] >= seq_starts[None, :]) & (places[:, None] < seq_ends[None, :])
    offsets = jnp.sum(jnp.where(member, places[:, None] - seq_starts[None, :], 0), axis=-1)
    frequency = THETA ** (-jnp.arange(HD // 2, dtype=jnp.float32) * 2.0 / HD)
    angles = offsets.astype(jnp.float32)[:, None] * frequency[None, :]
    angles = jnp.concatenate([angles, angles], axis=-1)[:, None, :]
    seq_ids = locate(places, seq_ends)
    return seq_ids, jnp.cos(angles), jnp.sin(angles)


def per_device(
    tokens,
    cotangent,
    lengths,
    deal,
    routes,
    gates,
    q_weight,
    k_weight,
    v_weight,
    o_weight,
    gain_attn,
    gain_moe,
    in_weight,
    down_weight,
):
    n_dp = lax.axis_size("dp")
    n_ex = lax.axis_size("expert")
    tok_rows = tokens.shape[1]
    model = tokens.shape[2]
    kv_here = KVH // n_dp
    heads_per = H // KVH
    q_cols = kv_here * heads_per * HD
    kv_cols = kv_here * HD
    own_experts = in_weight.shape[1]
    ff_here = FF // n_dp
    ff_cols = own_experts * ff_here
    w_rows = q_weight.shape[0]
    ex_index = lax.axis_index("expert")
    group_ids = jnp.arange(deal.shape[0], dtype=jnp.int32)
    dealt_of = jnp.argmax((deal[None, :] == group_ids[:, None]).astype(jnp.int32), axis=1)
    own_dealt = jnp.sum(jnp.where(deal == ex_index, group_ids, 0))

    def by_owner(weight):
        return weight.astype(jnp.bfloat16).reshape(w_rows, n_dp, weight.shape[1] // n_dp)

    length_parts = jnp.stack([lengths[0] // 128, lengths[0] % 128]).reshape(-1).astype(jnp.bfloat16)
    n_len = length_parts.shape[0]
    extra = jnp.concatenate(
        [
            gain_attn.astype(jnp.bfloat16)[:, None],
            gain_moe.astype(jnp.bfloat16)[:, None],
            jnp.broadcast_to(length_parts[None, :], (w_rows, n_len)),
            jnp.zeros((w_rows, 126 - n_len), jnp.bfloat16),
        ],
        axis=1,
    )

    def pack_in(tie):
        return pack_weights(tie(in_weight).transpose(1, 0, 2), n_dp)

    attn_out = jnp.concatenate(
        [
            by_owner(q_weight),
            by_owner(k_weight),
            by_owner(v_weight),
            by_owner(o_weight),
            jnp.broadcast_to(extra[:, None, :], (w_rows, n_dp, 128)),
        ],
        axis=2,
    ).transpose(1, 0, 2)
    attn_in = lax.all_to_all(attn_out, "dp", split_axis=0, concat_axis=0, tiled=True)

    every = jnp.arange(E, dtype=jnp.int32)[None, :]
    dense = sum(
        jnp.where(routes[0][:, k : k + 1] == every, gates[0][:, k : k + 1], 0.0)
        for k in range(TOPK)
    )
    dense_top = rounded(dense)
    dense_mid = rounded(dense - dense_top)
    meta = jnp.concatenate(
        [
            dense_top,
            dense_mid,
            dense - dense_top - dense_mid,
            jnp.zeros((tok_rows, 128 - 3 * E), jnp.float32),
        ],
        axis=1,
    ).astype(jnp.bfloat16)

    piece = tokens[0]
    (near, middle, y0), _ = one_round(
        (over_dp(piece, Z_NEAR), over_dp(piece, Z_MIDDLE), swap_y(piece)), (piece,)
    )
    (far, out1, y1), in_out = one_round(
        (over_dp(near, Z_MIDDLE), over_dp(middle, Z_OUT), swap_y(near)), (near, middle), pack_in
    )
    third = middle + out1
    (out2, y2), _ = one_round((over_dp(far, Z_OUT), swap_y(third)), (far, third))
    fourth = far + out2
    cot_piece = after(jnp.concatenate([cotangent[0], meta], axis=1), third)
    (y3, cot_near, cot_middle), _ = one_round(
        (swap_y(fourth), over_dp(cot_piece, Z_NEAR), over_dp(cot_piece, Z_MIDDLE)),
        (fourth, cot_piece),
    )
    group_tokens = joined(piece, y0, near, y1, third, y2, fourth, y3)
    attn_two = jnp.stack([attn_in, swap_core(attn_in)])
    attn_four = joined(attn_two, swap_x(attn_two))
    in_w = lax.all_to_all(
        after(in_out, cot_near, attn_in), "dp", split_axis=0, concat_axis=0, tiled=True
    ).reshape(model, 2 * ff_cols)
    z_own, y_own = lax.axis_index("dp") // 2, lax.axis_index("dp") % 2
    slot_dp = 2 * jnp.asarray(SLOT_Z, jnp.int32)[:, z_own]
    block_dp = jnp.stack([slot_dp + y_own, slot_dp + 1 - y_own], axis=1).reshape(-1)
    places = (block_dp[:, None] * tok_rows + jnp.arange(tok_rows, dtype=jnp.int32)).reshape(-1)


    def of_expert(index):
        return lax.dynamic_index_in_dim(attn_four, index ^ ex_index, 0, keepdims=False)

    attn_all = jnp.stack([of_expert(e) for e in range(n_ex)])
    attn_w = attn_all.transpose(1, 0, 2, 3).reshape(model, -1)
    qkv_cols = q_cols + 2 * kv_cols
    qkv_w = attn_w[:, :qkv_cols]
    o_w = attn_w[:, qkv_cols : qkv_cols + q_cols]
    side = attn_w[:, qkv_cols + q_cols :]
    gain_one = side[:, 0].astype(jnp.float32)
    gain_two = side[:, 1].astype(jnp.float32)
    own_parts = of_expert(own_dealt)[
        0, 0, qkv_cols + q_cols + 2 : qkv_cols + q_cols + 2 + n_len
    ].astype(jnp.int32)
    seq_lengths = own_parts[: n_len // 2] * 128 + own_parts[n_len // 2 :]

    down_w = down_weight.astype(jnp.bfloat16).transpose(1, 0, 2).reshape(ff_cols, model)

    seq_ids, cosine, sine_table = rope_parts(seq_lengths, places)
    cosine, sine_table = cosine[:, 0], sine_table[:, 0]
    row_ids = jnp.stack([seq_ids, places], axis=1)
    col_ids = jnp.stack([seq_ids, places], axis=0)

    def attention(tie):
        return front(
            tie(group_tokens), gain_one[None], qkv_w, o_w, cosine, sine_table, row_ids, col_ids
        )

    (cot_far, out1, y0), _ = one_round(
        (over_dp(cot_near, Z_MIDDLE), over_dp(cot_middle, Z_OUT), swap_y(cot_piece)),
        (cot_near, cot_middle),
    )
    third = cot_middle + out1
    pair0 = joined(cot_piece, y0)
    outs = over_dp(cot_far, Z_OUT), swap_y(cot_near), swap_x(pair0)
    (out2, y1, x0), attended = one_round(outs, (cot_far, pair0), attention)
    fourth = cot_far + out2
    pair1 = joined(cot_near, y1)
    total = DpScatter(attended[-1])
    (y2, x1, sums), _ = one_round((swap_y(third), swap_x(pair1), total.step()), (third, pair1))
    total.keep(sums)
    pair2 = joined(third, y2)
    (y3, x2, sums), _ = one_round((swap_y(fourth), swap_x(pair2), total.step()), (fourth, pair2))
    total.keep(sums)
    pair3 = joined(fourth, y3)
    (x3, sums), _ = one_round((swap_x(pair3), total.step()), (pair3,))
    total.keep(sums)
    cot_here = joined(pair0, x0, pair1, x1, pair2, x2, pair3, x3)
    (sums, cot_there), _ = one_round((total.step(), swap_core(cot_here)), (cot_here,))
    total.keep(sums)
    cot_all, branch = joined(cot_here, cot_there), total.total()
    normed, queries, keys, vals, mixed_low, run_top, run_total, _ = attended
    rows_from, meta_from = far_order(ex_index, dealt_of)
    inputs = tokens[0].astype(jnp.float32)
    middle = inputs + RESIDUAL * branch
    second_scale = lax.rsqrt(jnp.mean(middle * middle, axis=-1, keepdims=True) + EPSILON)
    sent_rows = (middle * second_scale * gain_two).astype(jnp.bfloat16)
    sent_rows = after(sent_rows, in_w, cot_all)
    part_rows = 16 * tok_rows

    def order_rows(tie, works):
        return take_blocks(
            jnp.stack([rows_from, meta_from]),
            tie(cot_all),
            [(0, 0, model), (1, model // 128, 128)],
            tok_rows // 2,
        )

    def pull(tie, works):
        return lax.dot_general(
            tie(works[0][0]), down_w, COLS_DIMS, preferred_element_type=jnp.float32
        )

    def spread_gates(tie, works):
        column = jnp.arange(128, dtype=jnp.int32)[:, None]
        owner = ex_index * own_experts + jnp.arange(ff_cols, dtype=jnp.int32)[None, :] // ff_here
        spread = ((column % E == owner) & (column < 3 * E)).astype(jnp.bfloat16)
        return jnp.dot(tie(works[0][1]), spread, preferred_element_type=jnp.float32)

    def up(sent):
        return jnp.dot(sent, in_w, preferred_element_type=jnp.float32)

    def down(gate_up, gates_here, pulled_here):
        gate_part = gate_up[:, :ff_cols]
        up_part = gate_up[:, ff_cols:]
        sigma = jax.nn.sigmoid(gate_part)
        silu = gate_part * sigma
        hidden = (silu * up_part).astype(jnp.bfloat16).astype(jnp.float32)
        weighted_here = (gates_here * hidden).astype(jnp.bfloat16)
        hidden_grad = RESIDUAL * gates_here * pulled_here
        gate_grad = hidden_grad * up_part * (sigma * (1.0 + gate_part * (1.0 - sigma)))
        up_grad = hidden_grad * silu
        grads_here = jnp.concatenate([gate_grad, up_grad], axis=1).astype(jnp.bfloat16)
        return weighted_here, grads_here

    def back(grads_here):
        return lax.dot_general(
            grads_here, in_w, COLS_DIMS, preferred_element_type=jnp.float32
        ).astype(jnp.bfloat16)

    def of_part(number, works, gate_up):
        rows_here = slice(number * part_rows, (number + 1) * part_rows)
        return down(gate_up, works[2][rows_here], works[1][rows_here])

    def first_up(tie, works, sent):
        return up(tie(sent))

    def first_down(tie, works):
        weighted_here, grads_here = of_part(0, works, tie(works[4]))
        return weighted_here, grads_here, back(grads_here)

    sent_parts, works = gather_pairs(
        sent_rows, (order_rows, pull, spread_gates, None, first_up, first_down)
    )
    cot_rows = works[0][0]
    weighted_first, grads_first, back_first = works[5]
    weighted_second, grads_second = of_part(1, works, up(sent_parts[1]))

    def out_first(tie, works):
        return jnp.dot(tie(weighted_first), down_w, preferred_element_type=jnp.float32).astype(
            jnp.bfloat16
        )

    def out_second(tie, works):
        return jnp.dot(tie(weighted_second), down_w, preferred_element_type=jnp.float32).astype(
            jnp.bfloat16
        )

    def in_first(tie, works):
        return lax.dot_general(
            tie(sent_parts[0]), grads_first, ROWS_DIMS, preferred_element_type=jnp.float32
        )

    out_sum = []

    def in_second(tie, works):
        out_sum.append(PairScatter(works[:2]))
        term = works[2] + lax.dot_general(
            tie(sent_parts[1]), grads_second, ROWS_DIMS, preferred_element_type=jnp.float32
        )
        return term, out_sum[0].step(tie)

    def down_first(tie, works):
        out_sum[0].keep(works[3][1])
        term = lax.dot_general(
            tie(weighted_first), cot_rows[:part_rows], ROWS_DIMS, preferred_element_type=jnp.float32
        )
        return term, out_sum[0].step(tie)

    def down_second(tie, works):
        out_sum[0].keep(works[4][1])
        term = works[4][0] + lax.dot_general(
            tie(weighted_second),
            cot_rows[part_rows:],
            ROWS_DIMS,
            preferred_element_type=jnp.float32,
        )
        return term, out_sum[0].step(tie)

    sent_grad, works = scatter_pairs(
        (back_first, back(grads_second)),
        (out_first, out_second, in_first, in_second, down_first, down_second),
    )
    out_sum = out_sum[0]
    out_sum.keep(works[5][1])
    in_term = works[3][0].astype(jnp.bfloat16)
    down_grad = (RESIDUAL * works[5][0]).reshape(own_experts, ff_here, model).transpose(1, 0, 2)
    upstream = cotangent[0].astype(jnp.float32)
    scaled_grad = sent_grad * gain_two
    middle_grad = (
        upstream
        + second_scale * scaled_grad
        - middle
        * second_scale**3
        * jnp.mean(scaled_grad * middle, axis=-1, keepdims=True)
    )
    gain_two_part = jnp.sum(sent_grad * middle * second_scale, axis=0)
    branch_grad = (RESIDUAL * middle_grad).astype(jnp.bfloat16)

    def out_step(tie, works):
        if works:
            out_sum.keep(works[-1])
        return out_sum.step(tie)

    branch_grad_all, works = dp_gather(branch_grad, (out_step, out_step, out_step, None))
    out_sum.keep(works[2])
    output = middle + RESIDUAL * out_sum.total()
    in_back = lax.all_to_all(
        after(in_term, branch_grad_all).reshape(n_dp, in_weight.shape[0], 2 * ff_cols),
        "dp",
        split_axis=0,
        concat_axis=0,
        tiled=True,
    )


    qkv_grad, normed_grad_part, gain_one_part = rear(
        branch_grad_all,
        o_w,
        queries,
        keys,
        vals,
        run_top,
        run_total,
        row_ids,
        col_ids,
        cosine,
        sine_table,
        qkv_w,
        group_tokens,
    )
    total = DpScatter(normed_grad_part)

    def weight_grads(tie):
        qkv_term = lax.dot_general(
            normed, tie(qkv_grad), ROWS_DIMS, preferred_element_type=jnp.float32
        )
        o_term = lax.dot_general(
            branch_grad_all, mixed_low, ROWS_DIMS, preferred_element_type=jnp.float32
        )
        grads = jnp.concatenate(
            [
                qkv_term,
                o_term,
                gain_one_part[0][:, None],
                gain_two_part[:, None],
                jnp.zeros((model, 126), jnp.float32),
            ],
            axis=1,
        ).astype(jnp.bfloat16)
        grads = grads.reshape(n_dp, n_ex, w_rows, -1)
        return [
            lax.dynamic_index_in_dim(grads, ex_index ^ k, 1, keepdims=False) for k in range(n_ex)
        ]

    sums, (own_g, core_g, x_g, xc_g) = one_round(total.step(), (normed_grad_part,), weight_grads)
    total.keep(sums)
    core_pair = jnp.stack([core_g, xc_g])
    (sums, from_core), _ = one_round((total.step(), swap_core(core_pair)), (core_pair,))
    total.keep(sums)
    x_g = added(x_g, from_core[1])
    (sums, from_x), _ = one_round((total.step(), swap_x(x_g)), (x_g,))
    total.keep(sums)
    grads = lax.all_to_all(
        added(own_g, from_core[0], from_x), "dp", split_axis=0, concat_axis=0, tiled=True
    )
    (sums, grads), in_grad = one_round(
        (total.step(), grads),
        (from_x,),
        lambda tie: unpack_grads(tie(in_back), own_experts).transpose(1, 0, 2),
    )
    total.keep(sums)
    grads = grads.astype(jnp.float32)
    normed_grad = total.total()

    def own_rows(begin, width):
        return grads[:, :, begin : begin + width].transpose(1, 0, 2).reshape(w_rows, n_dp * width)

    q_grad = own_rows(0, q_cols)
    k_grad = own_rows(q_cols, kv_cols)
    v_grad = own_rows(q_cols + kv_cols, kv_cols)
    o_grad = own_rows(qkv_cols, q_cols)
    gain_attn_grad = jnp.sum(grads[:, :, qkv_cols + q_cols], axis=0)
    gain_moe_grad = jnp.sum(grads[:, :, qkv_cols + q_cols + 1], axis=0)

    own_scale = lax.rsqrt(jnp.mean(inputs * inputs, axis=-1, keepdims=True) + EPSILON)
    scaled_one = normed_grad * gain_one
    input_grad = (
        middle_grad
        + own_scale * scaled_one
        - inputs * own_scale**3 * jnp.mean(scaled_one * inputs, axis=-1, keepdims=True)
    )
    return (
        output[None],
        input_grad[None],
        q_grad,
        k_grad,
        v_grad,
        o_grad,
        gain_attn_grad,
        gain_moe_grad,
        in_grad,
        down_grad,
    )


def per_layer(*args):
    return per_device(*args)


def solution(mesh):
    placed = (
        P("expert", "dp", None),
        P("expert", "dp", None),
        P("expert", None),
        P(),
        P("expert", "dp", None),
        P("expert", "dp", None),
        P(("dp", "expert"), None),
        P(("dp", "expert"), None),
        P(("dp", "expert"), None),
        P(("dp", "expert"), None),
        P(("dp", "expert")),
        P(("dp", "expert")),
        P("dp", "expert", None),
        P("dp", "expert", None),
    )
    n_dp = mesh.shape["dp"]
    split_heads = n_dp == 8 and mesh.shape["expert"] == 4
    return jax.shard_map(
        per_layer if split_heads else per_device_wide,
        mesh=mesh,
        in_specs=placed,
        out_specs=(
            P("expert", "dp", None),
            P("expert", "dp", None),
            P(("dp", "expert"), None),
            P(("dp", "expert"), None),
            P(("dp", "expert"), None),
            P(("dp", "expert"), None),
            P(("dp", "expert")),
            P(("dp", "expert")),
            P("dp", "expert", None),
            P("dp", "expert", None),
        ),
        check_vma=False,
    )
```
